256 devices in a mesh: comp: 2 (over core), gx: 32 (over z, y), gy: 4 (over x).
Axes of the slice: x: 4, y: 4, z: 8, core: 2. Of those that a mesh axis runs over, the one named last changes fastest.
Arguments:
- atm_state: float32 [2, 72, 128, 4096], P('comp', None, 'gy', 'gx'), may hold values from -6 to 6
- atm_mass: float32 [128, 4096], P('gy', 'gx'), may hold values from 0.5 to 2
- coupler: float32 [16, 72], replicated, may hold values from -0.75 to 0.75
- flux_dest: int32 [4, 2048, 1], P('gy', 'gx'), may hold values from 0 to 31; in each aligned block of 64 rows (0 to 63, 64 to 127, ..., all dimensions but the last counted through in order) at most 6 rows name the same one
- flux_dst_blk: int32 [4, 2048], P('gy', 'gx'), may hold values from 0 to 15
- flux_src_blk: int32 [4, 2048], P('gy', 'gx'), may hold values from 0 to 31
- conservative_flux_weights: bfloat16 [4, 2048, 128, 128], P('gy', 'gx'), may hold values from -0.25 to 0.25
- ocn_tracers: float32 [2, 2, 80, 64, 4096], P('comp', None, None, 'gy', 'gx'), may hold values from -6 to 6
- ocean_neighbour_codes: int32 [6, 64, 4096], P(None, 'gy', 'gx'), may hold values from 0 to 7, as said below
- ocn_rates: float32 [6, 64, 4096], P(None, 'gy', 'gx'), may hold values from 0.03 to 0.15
- lev_speed: float32 [80], replicated, may hold values from 0.3 to 1
- profile: float32 [2, 80, 16], replicated, may hold values from -0.6 to 0.6
- back_owner: int32 [4, 2048], P('gy', 'gx'), may hold values from 0 to 31
- back_src_blk: int32 [4, 2048], P('gy', 'gx'), may hold values from 0 to 15
- back_dst_blk: int32 [4, 2048], P('gy', 'gx'), may hold values from 0 to 31
- return_remap_weights: bfloat16 [4, 2048, 128, 128], P('gy', 'gx'), may hold values from -0.375 to 0.375
Outputs:
- dss_out: float32 [2, 72, 128, 4096], P('comp', None, 'gy', 'gx')
- sfc_out: float32 [2, 2, 128, 4096], P('comp', None, 'gy', 'gx')
- ocn_out: float32 [2, 2, 80, 64, 4096], P('comp', None, None, 'gy', 'gx')
The draws below stay inside these ranges and needn't reach their ends.
Inputs may be any that keep to these rules, and one draw needn't show every extreme that they name: `flux_dest`: the 64 rows of one holder name one ocean owner at most 6 times, and 6 times in some holder. `ocean_neighbour_codes`: the 6 codes of a cell are distinct.
All inputs are finite; a program needn't handle non-finite values.
Results may differ from the reference program's by a relative error of at most 0.0037.
Values may be sent and summed in bfloat16 or wider, within the bound.
No kernel may reach another device: no remote copies, remote signals or barrier semaphores. Data moves between devices by JAX's collectives and lax.ppermute only.
A program may use at most 128 MiB of HBM per device.

```python
import math
import jax
import jax.numpy as jnp
import numpy as np
from jax import lax

LEV_A = 72
LEV_O = 80
NF = 16
NTR = 2
NB = 6
OY = 16
TILES_DEV = 64
ADV = 4
TILE = 128
PY = 32
NYA = 128
NXA = 4096
NYO = 64
NXO = 4096
TILES_TOT = 2048
CAP = 6
N_GX = 32
N_GY = 4


def draw_ocean_neighbour_codes(key, part):
    scores = jax.random.randint(key, (8, NYO, NXO), 0, 1 << 20) * 8 + jnp.arange(8, dtype=jnp.int32)[:, None, None]
    order = jnp.argsort(scores, axis=0, stable=True)
    return order[:NB].astype(jnp.int32)


def draw_ocn_rates(key, part):
    values = jax.random.uniform(key, (NB, NYO, NXO), jnp.float32, 0.2, 1.0)
    return (0.15 * values).astype(jnp.float32)


def plant(result, stream_key, smallest, largest):
    longest = result.shape.index(max(result.shape))
    spots = []
    for shift in (0, 1):
        where = [jax.random.randint(jax.random.fold_in(stream_key, axis), (), 0, length) for axis, length in enumerate(result.shape)]
        where[longest] = (where[longest] + shift) % result.shape[longest]
        spots.append(tuple(where))
    return result.at[spots[0]].set(smallest).at[spots[1]].set(largest)


def levels(rng, extent, shards, least, high):
    def one(dim, blocks):
        heights = jax.random.uniform(jax.random.fold_in(jax.random.fold_in(rng, 6), dim), (blocks,), jnp.float32, least / len(shards), high / len(shards))
        return jnp.repeat(jnp.exp(heights), extent[dim] // blocks).reshape((-1,) + (1,) * (len(extent) - dim - 1))

    level = one(*shards[0])
    for cut in shards[1:]:
        level = level * one(*cut)
    return level


def assign_block(rng, own, number, rows, amount, top, most, lean):
    order = jax.random.permutation(rng, amount)
    crowded, common = load_shares(amount, rows * top, most, lean, True), load_shares(amount, rows * top, most, lean, False)
    places = jnp.arange(amount)

    def named(tallies, offset_by):
        used = int((tallies > 0).sum())
        fixed = max(1, used // 4)
        passed = fixed + (places - fixed + offset_by * (used - fixed)) % max(1, amount - fixed)
        return jnp.zeros((amount,), jnp.int32).at[order[jnp.where(places < fixed, places, passed)]].set(jnp.asarray(tallies, jnp.int32))

    tallies = jnp.where(number % 4 == 0, named(crowded, number // 4), named(common, number - number // 4 - 1))
    mixed = jax.random.permutation(jax.random.fold_in(own, 3), amount)
    source_of, receiver = mixed[0:amount // 2 * 2:2], mixed[1:amount // 2 * 2:2]
    room = jnp.minimum(tallies[source_of] - 1, most - tallies[receiver]) // 2
    room = jnp.where((source_of == order[0]) | (receiver == order[0]) | (tallies[receiver] == 0), 0, jnp.maximum(room, 0))
    passed = jax.random.randint(jax.random.fold_in(own, 4), (amount // 2,), 0, 1 << 20) % (room + 1)
    tallies = tallies.at[source_of].add(-passed).at[receiver].add(passed)
    items = jnp.searchsorted(jnp.cumsum(tallies), jnp.arange(rows * top), side="right").astype(jnp.int32)
    table = items.reshape(top, rows).T
    table = table[jax.random.permutation(jax.random.fold_in(own, 1), rows)]
    offset_by = jax.random.randint(jax.random.fold_in(own, 2), (rows, 1), 0, top)
    return jnp.take_along_axis(table, (jnp.arange(top)[None, :] + offset_by) % top, axis=1)


def load_shares(count, total, most, skew, full):
    weights = [(1 << 20) // math.isqrt(grade ** skew) + 1 for grade in range(1, count + 1)]
    largest = most if full else min(most, max(-(-total // count), total * weights[0] // sum(weights)))
    least = 1 if total - largest >= count - 1 else 0
    given, spare = [largest] + [least] * (count - 1), total - largest - least * (count - 1)
    while spare > 0:
        free = [i for i in range(1, count) if given[i] < largest] or [i for i in range(1, count) if given[i] < most]
        mass, remaining = sum([weights[i] for i in free]), spare
        for i in free:
            extra = min(most - given[i], max(1, remaining * weights[i] // mass), spare)
            given[i] = given[i] + extra
            spare = spare - extra
    return np.array(given)


def bell_draw(own_key, extent, spread, bound, pieces=(), kind=jnp.bfloat16):
    gain = levels(own_key, extent, pieces, -0.22, 0.18) if pieces else 1.0
    drawn = jax.random.normal(own_key, extent, jnp.float32) * spread * gain
    return jnp.minimum(jnp.maximum(drawn, -bound), bound).astype(kind)


def setup_inputs(seed: int = 0) -> dict:
    streams_of = jax.random.split(jax.random.key(seed), 17)
    atm_state = bell_draw(streams_of[0], (2, LEV_A, NYA, NXA), 1.0, 6.0, ((0, 2), (2, 4), (3, 32)), jnp.float32)
    atm_mass = jnp.clip(0.5 + 1.5 * jax.random.uniform(streams_of[1], (NYA, NXA), jnp.float32) ** levels(streams_of[1], (NYA, NXA), ((0, 4), (1, 32)), -0.2, 0.2), 0.5, 2.0)
    coupler = bell_draw(streams_of[2], (NF, LEV_A), LEV_A ** -0.5, 0.75, (), jnp.float32)
    flux_dest_keys = jax.random.split(jax.random.fold_in(streams_of[3], 1), N_GY * TILES_TOT // TILES_DEV)
    flux_dest_turns = jax.random.permutation(jax.random.fold_in(streams_of[3], 3), N_GY * TILES_TOT // TILES_DEV)
    flux_dest = jax.vmap(lambda own, number: assign_block(jax.random.fold_in(streams_of[3], 2), own, number, TILES_DEV, N_GX, 1, CAP, 2))(flux_dest_keys, flux_dest_turns).reshape((N_GY, TILES_TOT, 1))
    flux_dst_blk = plant(jax.random.randint(streams_of[4], (N_GY, TILES_TOT), 0, OY), jax.random.fold_in(streams_of[4], 1), 0, OY - 1).astype(jnp.int32)
    flux_src_blk = plant(jax.random.randint(streams_of[5], (N_GY, TILES_TOT), 0, PY), jax.random.fold_in(streams_of[5], 1), 0, PY - 1).astype(jnp.int32)
    conservative_flux_weights = bell_draw(streams_of[6], (N_GY, TILES_TOT, TILE, TILE), (4 * TILE) ** -0.5, 0.25, ((0, 4), (1, 32)))
    ocn_tracers = bell_draw(streams_of[7], (2, NTR, LEV_O, NYO, NXO), 1.0, 6.0, ((0, 2), (3, 4), (4, 32)), jnp.float32)
    ocean_neighbour_codes = draw_ocean_neighbour_codes(jax.random.fold_in(streams_of[16], 71), 0)
    ocn_rates = draw_ocn_rates(jax.random.fold_in(streams_of[16], 71), 0)
    lev_speed = jnp.clip(jnp.exp(jax.random.uniform(streams_of[10], (LEV_O,), jnp.float32, math.log(0.3), math.log(1.0))), 0.3, 1.0)
    profile = bell_draw(streams_of[11], (NTR, LEV_O, NF), 0.1, 0.6, (), jnp.float32)
    back_owner = plant(jax.random.randint(streams_of[12], (N_GY, TILES_TOT), 0, N_GX), jax.random.fold_in(streams_of[12], 1), 0, N_GX - 1).astype(jnp.int32)
    back_src_blk = plant(jax.random.randint(streams_of[13], (N_GY, TILES_TOT), 0, OY), jax.random.fold_in(streams_of[13], 1), 0, OY - 1).astype(jnp.int32)
    back_dst_blk = plant(jax.random.randint(streams_of[14], (N_GY, TILES_TOT), 0, PY), jax.random.fold_in(streams_of[14], 1), 0, PY - 1).astype(jnp.int32)
    return_remap_weights = bell_draw(streams_of[15], (N_GY, TILES_TOT, TILE, TILE), (2 * TILE) ** -0.5, 0.375, ((0, 4), (1, 32)))
    return {"atm_state": atm_state, "atm_mass": atm_mass, "coupler": coupler, "flux_dest": flux_dest, "flux_dst_blk": flux_dst_blk, "flux_src_blk": flux_src_blk, "conservative_flux_weights": conservative_flux_weights, "ocn_tracers": ocn_tracers, "ocean_neighbour_codes": ocean_neighbour_codes, "ocn_rates": ocn_rates, "lev_speed": lev_speed, "profile": profile, "back_owner": back_owner, "back_src_blk": back_src_blk, "back_dst_blk": back_dst_blk, "return_remap_weights": return_remap_weights}


OFFSETS = ((-1, -1), (-1, 0), (-1, 1), (0, -1), (0, 1), (1, -1), (1, 0), (1, 1))


def edge_assembly(padded):
    height = padded.shape[1] - 2
    width = padded.shape[2] - 2
    column_pos = jnp.arange(width) % 4
    along_x = padded[:, :, 1:-1] + jnp.where(column_pos == 0, padded[:, :, :-2], 0.0) + jnp.where(column_pos == 3, padded[:, :, 2:], 0.0)
    row_pos = (jnp.arange(height) % 4)[:, None]
    return along_x[:, 1:-1] + jnp.where(row_pos == 0, along_x[:, :-2], 0.0) + jnp.where(row_pos == 3, along_x[:, 2:], 0.0)


def tile_products(sources, weights):
    def one_band(paired_entry):
        return jnp.einsum('avb,apb->avp', paired_entry[0].astype(jnp.float32), paired_entry[1].astype(jnp.float32))
    return lax.map(one_band, (sources, weights))


def reference(atm_state, atm_mass, coupler, flux_dest, flux_dst_blk, flux_src_blk, conservative_flux_weights, ocn_tracers, ocean_neighbour_codes, ocn_rates, lev_speed, profile, back_owner, back_src_blk, back_dst_blk, return_remap_weights):
    state = atm_state[0]
    stacked = jnp.concatenate([state * atm_mass[None], atm_mass[None]], axis=0)
    assembled = edge_assembly(jnp.pad(stacked, ((0, 0), (1, 1), (1, 1))))
    dss = assembled[:-1] / assembled[-1]
    flux = jnp.dot(coupler, dss.reshape(LEV_A, -1), precision=lax.Precision.HIGHEST, preferred_element_type=jnp.float32)
    flux = flux.astype(jnp.bfloat16).reshape(NF, N_GY, PY, N_GX, TILE).transpose(1, 3, 2, 0, 4)
    band_index = jnp.arange(N_GY, dtype=jnp.int32)[:, None]
    holder_index = (jnp.arange(TILES_TOT, dtype=jnp.int32) // TILES_DEV)[None, :]
    sources = flux[band_index, holder_index, flux_src_blk]
    flux_part = tile_products(sources, conservative_flux_weights)
    ocean_blocks = jnp.zeros((N_GY, N_GX, OY, NF, TILE), jnp.float32)
    ocean_blocks = ocean_blocks.at[band_index, flux_dest[..., 0], flux_dst_blk].add(flux_part)
    flux_ocn = ocean_blocks.transpose(3, 0, 2, 1, 4).reshape(NF, NYO * NXO)
    rate8 = jnp.stack([jnp.sum(jnp.where(ocean_neighbour_codes == code, ocn_rates, 0.0), axis=0) for code in range(8)])
    total = jnp.sum(ocn_rates, axis=0)
    tracer = ocn_tracers[1]
    for repeat in range(ADV):
        padded = jnp.pad(tracer, ((0, 0), (0, 0), (1, 1), (1, 1)))
        change = -total * tracer
        for code, (shift_y, shift_x) in enumerate(OFFSETS):
            change = change + rate8[code] * padded[:, :, 1 + shift_y:1 + shift_y + NYO, 1 + shift_x:1 + shift_x + NXO]
        tracer = tracer + lev_speed[None, :, None, None] * change
    forcing = jnp.dot(profile.reshape(NTR * LEV_O, NF), flux_ocn, precision=lax.Precision.HIGHEST, preferred_element_type=jnp.float32)
    tracer = tracer + forcing.reshape(NTR, LEV_O, NYO, NXO)
    surface = tracer[:, 0].astype(jnp.bfloat16).reshape(NTR, N_GY, OY, N_GX, TILE).transpose(1, 3, 2, 0, 4)
    back_sources = surface[band_index, back_owner, back_src_blk]
    back_part = tile_products(back_sources, return_remap_weights)
    atm_blocks = jnp.zeros((N_GY, N_GX, PY, NTR, TILE), jnp.float32)
    atm_blocks = atm_blocks.at[band_index, holder_index, back_dst_blk].add(back_part)
    sfc = atm_blocks.transpose(3, 0, 2, 1, 4).reshape(NTR, NYA, NXA)
    dss_out = jnp.stack([dss, jnp.zeros_like(dss)])
    sfc_out = jnp.stack([sfc, jnp.zeros_like(sfc)])
    ocn_out = jnp.stack([jnp.zeros_like(tracer), tracer])
    return (dss_out, sfc_out, ocn_out)
```

```python
import functools

import jax
import jax.numpy as jnp
from jax import lax
from jax.experimental import pallas as pl
from jax.experimental.pallas import tpu as pltpu
from jax.sharding import PartitionSpec as P

F32 = jnp.float32
BF16 = jnp.bfloat16
ADV = 4
W = 128
PR = 176
EXT = 24
SLOTS = 6
TILES_PER_PEER = 9


def lanes(rows):
    return lax.broadcasted_iota(jnp.int32, (rows, W), 1)


def fetch(src, dst, sem):
    copy = pltpu.make_async_copy(src, dst, sem)
    copy.start()
    copy.wait()


def split(value):
    hi = value.astype(BF16)
    return hi, (value - hi.astype(F32)).astype(BF16)


def params():
    return pltpu.CompilerParams(vmem_limit_bytes=60 * 1024 * 1024)


def call(body, out_shape, n_smem, n_any, n_vmem, scratch):
    specs = (
        [pl.BlockSpec(memory_space=pltpu.SMEM)] * n_smem
        + [pl.BlockSpec(memory_space=pl.ANY)] * n_any
        + [pl.BlockSpec(memory_space=pltpu.VMEM)] * n_vmem
    )
    return pl.pallas_call(
        body,
        out_shape=out_shape,
        in_specs=specs,
        out_specs=[pl.BlockSpec(memory_space=pltpu.VMEM)] * len(out_shape),
        scratch_shapes=scratch,
        compiler_params=params(),
        name=body.__name__,
    )


def pack_rows(comp, state, tracer, mass, codes, rates, up, down, rate8, buf, sem):
    @pl.when(comp[0] == 0)
    def _():
        fetch(state, buf.at[pl.ds(0, 2304)], sem)
        for dst, y in ((up, 0), (down, 31)):
            m = jnp.broadcast_to(mass[y : y + 1, :], (8, W))
            parts = [buf[pl.ds(g * 256 + y, 8, stride=32), :] * m for g in range(9)] + [m]
            for p in range(5):
                hi, lo = split(jnp.concatenate(parts[2 * p : 2 * p + 2], axis=0))
                dst[16 * p : 16 * p + 16, :] = hi
                dst[80 + 16 * p : 96 + 16 * p, :] = lo

    @pl.when(comp[0] == 1)
    def _():
        fetch(tracer, buf, sem)
        for o in range(8):
            acc = jnp.zeros((16, W), F32)
            for k in range(6):
                rows = slice(16 * k, 16 * k + 16)
                acc = acc + jnp.where(codes[rows, :] == o, rates[rows, :], 0.0)
            rate8[16 * o : 16 * o + 16, :] = acc
        for dst, first in ((up, 0), (down, 12)):
            for j in range(ADV):
                y = first + j
                for p in range(10):
                    both = jnp.concatenate(
                        [buf[pl.ds(g * 128 + y, 8, stride=16), :] for g in (2 * p, 2 * p + 1)],
                        axis=0,
                    )
                    dst[j * PR + 16 * p : j * PR + 16 * p + 16, :] = both.astype(BF16)
                r = rate8[pl.ds(y, 8, stride=16), :]
                dst[j * PR + 160 : j * PR + 176, :] = jnp.concatenate([r, r], axis=0).astype(BF16)


def pack_columns(comp, state, tracer, mass, rate8, left, right, turned, buf, sem):
    lane = lanes(8)

    @pl.when(comp[0] == 0)
    def _():
        fetch(state, buf.at[pl.ds(0, 2304)], sem)
        for g in range(10):
            to_left = jnp.zeros((8, W), F32)
            to_right = jnp.zeros((8, W), F32)
            for y in range(32):
                v = jnp.broadcast_to(mass[y : y + 1, :], (8, W))
                if g < 9:
                    v = v * buf[pl.ds(g * 256 + y, 8, stride=32), :]
                turned[80 * y + 8 * g : 80 * y + 8 * g + 8, :] = v
                v = pltpu.roll(v, y, 1)
                to_left = jnp.where(lane == y, v, to_left)
                to_right = jnp.where(lane == (y - 1) % W, v, to_right)
            left[8 * g : 8 * g + 8, :] = to_left
            right[8 * g : 8 * g + 8, :] = to_right

    @pl.when(comp[0] == 1)
    def _():
        fetch(tracer, buf, sem)
        for g in range(21):
            to_left = jnp.zeros((8, W), F32)
            to_right = jnp.zeros((8, W), F32)
            for y in range(16):
                i = y + ADV
                if g < 20:
                    v = buf[pl.ds(g * 128 + y, 8, stride=16), :]
                    turned[160 * y + 8 * g : 160 * y + 8 * g + 8, :] = v
                else:
                    v = rate8[pl.ds(y, 8, stride=16), :]
                v = pltpu.roll(v, 4 * i, 1)
                to_left = jnp.where(lane // 4 == i, v, to_left)
                to_right = jnp.where(lane // 4 == i - 1, v, to_right)
            left[8 * g : 8 * g + 8, :] = to_left
            right[8 * g : 8 * g + 8, :] = to_right
        left[168:176, :] = jnp.zeros((8, W), F32)
        right[168:176, :] = jnp.zeros((8, W), F32)


def finish_columns(comp, raw_left, raw_right, above, below, left, right):
    lane = lanes(16)

    @pl.when(comp[0] == 0)
    def _():
        for p in range(5):
            rows = slice(16 * p, 16 * p + 16)
            low = slice(80 + 16 * p, 96 + 16 * p)
            up = above[rows, :].astype(F32) + above[low, :].astype(F32)
            down = below[rows, :].astype(F32) + below[low, :].astype(F32)
            down = pltpu.roll(down, 31, 1)
            for src, dst, at in ((raw_left, left, 0), (raw_right, right, 1)):
                v = src[rows, :]
                pos = (lane + at) % 4
                before = jnp.where(lane == (W - at) % W, up, pltpu.roll(v, 1, 1))
                after = jnp.where(lane == 31 - at, down, pltpu.roll(v, W - 1, 1))
                v = v + jnp.where(pos == 0, before, 0.0) + jnp.where(pos == 3, after, 0.0)
                hi, lo = split(v)
                dst[rows, :] = hi
                dst[low, :] = lo

    @pl.when(comp[0] == 1)
    def _():
        for p in range(11):
            rows = slice(16 * p, 16 * p + 16)
            to_left = raw_left[rows, :]
            to_right = raw_right[rows, :]
            for src, first in ((above, 0), (below, 20)):
                for j in range(ADV):
                    i = first + j
                    v = src[j * PR + 16 * p : j * PR + 16 * p + 16, :].astype(F32)
                    v = pltpu.roll(v, 4 * i, 1)
                    to_left = jnp.where(lane // 4 == i, v, to_left)
                    to_right = jnp.where(lane // 4 == (i - 1) % 32, v, to_right)
            left[rows, :] = to_left.astype(BF16)
            right[rows, :] = to_right.astype(BF16)


def swap_left(a, b):
    lane = lanes(a.shape[0])
    ra, rb = pltpu.roll(a, W - 1, 1), pltpu.roll(b, W - 1, 1)
    return jnp.where(lane == W - 1, rb, ra), jnp.where(lane == W - 1, ra, rb)


def swap_right(a, b):
    lane = lanes(a.shape[0])
    ra, rb = pltpu.roll(a, 1, 1), pltpu.roll(b, 1, 1)
    return jnp.where(lane == 0, rb, ra), jnp.where(lane == 0, ra, rb)


def halo_tile(from_right, from_left, i):
    lane = lanes(8)
    v = jnp.where(lane // 4 == i, from_right, from_left)
    v = pltpu.roll(v, (W - 4 * i) % W, 1)
    return jnp.where((lane < 4) | (lane >= W - 4), v, 0.0)


def extended(g, i, main, above, below, halo_l, halo_r):
    rows = slice(8 * g, 8 * g + 8)
    half = slice(8 * (g % 2), 8 * (g % 2) + 8)
    pair = 16 * (g // 2)

    def wide(ref, at):
        return ref[at : at + 16, :].astype(F32)[half]

    if i < ADV:
        a = wide(above, i * PR + pair)
    elif i >= EXT - ADV:
        a = wide(below, (i - EXT + ADV) * PR + pair)
    else:
        a = main(g, i - ADV)
    b = halo_tile(wide(halo_r, pair), wide(halo_l, pair), i)
    return a, b


RIGHTWARD = (2, 4, 7)
LEFTWARD = (0, 3, 5)


def prepare_rates(coef_a, coef_b, rate8, above, below, halo_l, halo_r):
    sub = lax.broadcasted_iota(jnp.int32, (8, W), 0)
    right = (sub == 2) | (sub == 4) | (sub == 7)
    left = (sub == 0) | (sub == 3) | (sub == 5)

    def main(g, y):
        return rate8[pl.ds(y, 8, stride=16), :]

    for i in range(EXT):
        a, b = extended(20, i, main, above, below, halo_l, halo_r)
        la, lb = swap_left(a, b)
        ra, rb = swap_right(a, b)
        coef_a[i * 16 : i * 16 + 8, :] = jnp.where(right, ra, jnp.where(left, la, a))
        coef_b[i * 16 : i * 16 + 8, :] = jnp.where(right, rb, jnp.where(left, lb, b))
        coef_a[i * 16 + 8 : i * 16 + 16, :] = jnp.broadcast_to(
            jnp.sum(a, axis=0, keepdims=True), (8, W)
        )
        coef_b[i * 16 + 8 : i * 16 + 16, :] = jnp.broadcast_to(
            jnp.sum(b, axis=0, keepdims=True), (8, W)
        )


def level_speeds(lev_speed, groups):
    sub = lax.broadcasted_iota(jnp.int32, (8, W), 0)
    speeds = []
    for g in groups:
        v = jnp.zeros((8, W), F32)
        for k in range(8):
            v = jnp.where(sub == k, lev_speed[(8 * g + k) % 80], v)
        speeds.append(v)
    return speeds


def fill(groups, ta, tb, main, above, below, halo_l, halo_r):
    wide = 8 * len(groups)
    for n, g in enumerate(groups):
        for part in range(3):
            span = range(8 * part, 8 * part + 8)
            pairs = [extended(g, i, main, above, below, halo_l, halo_r) for i in span]
            for i, (a, b) in zip(span, pairs):
                ta[i * wide + 8 * n : i * wide + 8 * n + 8, :] = a
                tb[i * wide + 8 * n : i * wide + 8 * n + 8, :] = b


def advect_cell(cells, coefs, speed):
    outs = []
    for (t0, t1, t2), c in zip(cells, coefs):
        to_r = c[2] * t0 + c[4] * t1 + c[7] * t2
        to_l = c[0] * t0 + c[3] * t1 + c[5] * t2
        mid = c[1] * t0 + c[6] * t2 - c[8] * t1
        outs.append((t1, to_r, to_l, mid))
    (a1, ar, al, am), (b1, br, bl, bm) = outs
    ua, ub = swap_left(ar, br)
    va, vb = swap_right(al, bl)
    return a1 + speed * (am + ua + va), b1 + speed * (bm + ub + vb)


def advect(pairs, coef_a, coef_b, speed, count, chunk, result):
    wide = count * 8

    def at(i, n):
        return pl.ds(pl.multiple_of(i * wide + 8 * n, 8), 8)

    for step in range(ADV):
        now, later = pairs[step % 2], pairs[(step + 1) % 2]
        last = step == ADV - 1

        def row(i, carry, now=now, later=later, last=last):
            def coef(ref, o):
                return jnp.broadcast_to(ref[pl.ds(i * 16 + o, 1), :], (8, W))

            coefs = [[coef(ref, o) for o in range(9)] for ref in (coef_a, coef_b)]
            for base in range(0, count, chunk):
                span = range(base, base + chunk)
                news = []
                for n in span:
                    cells = [[t[at(k, n), :] for k in (i - 1, i, i + 1)] for t in now]
                    news.append(advect_cell(cells, coefs, speed[8 * n : 8 * n + 8, :]))
                for n, (new_a, new_b) in zip(span, news):
                    if last:
                        place = pl.multiple_of((i - ADV) * wide + 8 * n, 8)
                        result[pl.ds(place, 8), :] = new_a
                    else:
                        later[0][at(i, n), :] = new_a
                        later[1][at(i, n), :] = new_b
            return carry

        lax.fori_loop(step + 1, EXT - 1 - step, row, 0)


def assemble(
    comp, lev_speed, turned, rate8, above, below, halo_l, halo_r, lhs,
    dss, own, flux, top, coef_a, coef_b,
    buf, sem, edge, high, low, far_l, far_r, ta, tb, tc, td,
):
    lane = lanes(8)

    @pl.when(comp[0] == 0)
    def _():
        copy = pltpu.make_async_copy(turned, buf.at[pl.ds(80, 2560)], sem)
        copy.start()
        for p in range(5):
            rows = slice(16 * p, 16 * p + 16)
            rest = slice(80 + 16 * p, 96 + 16 * p)
            v = halo_l[rows, :].astype(F32) + halo_l[rest, :].astype(F32)
            far_l[rows, :] = pltpu.roll(v, 2, 1)
            far_r[rows, :] = halo_r[rows, :].astype(F32) + halo_r[rest, :].astype(F32)
            v = above[rows, :].astype(F32) + above[rest, :].astype(F32)
            buf[16 * p : 16 * p + 16, :] = v
            v = below[rows, :].astype(F32) + below[rest, :].astype(F32)
            buf[2640 + 16 * p : 2656 + 16 * p, :] = v
        for g in range(10):
            rows = slice(8 * g, 8 * g + 8)
            from_l, from_r = far_l[rows, :], far_r[rows, :]
            for y in range(32):
                v = jnp.where(lane == y, from_r, from_l)
                at = 80 * y + 8 * g
                edge[at : at + 8, :] = pltpu.roll(v, (W - 1 - y) % W, 1)
        copy.wait()

        def quad(q, carry):
            first = lane % 4 == 0
            final = lane % 4 == 3
            outer = (lane == 0) | (lane == W - 1)

            def at(row, g, wide=80):
                return pl.ds(pl.multiple_of(row * wide + 8 * g, 8), 8)

            for r in range(4):
                y = 4 * q + r
                values = []
                for g in (9, 0, 1, 2, 3, 4, 5, 6, 7, 8):
                    v = buf[at(y + 1, g), :]
                    if r == 0:
                        v = v + buf[at(y, g), :]
                    if r == 3:
                        v = v + buf[at(y + 2, g), :]
                    near = jnp.where(first, pltpu.roll(v, 1, 1), pltpu.roll(v, W - 1, 1))
                    near = jnp.where(outer, edge[at(y, g), :], near)
                    v = v + jnp.where(first | final, near, 0.0)
                    if g == 9:
                        inverse = 1.0 / v
                    else:
                        values.append(v * inverse)
                for g, v in enumerate(values):
                    dss[at(y, g, 72), :] = v
                hi, lo = split(jnp.concatenate(values + [jnp.zeros((8, W), F32)], axis=0))
                high[y] = hi
                low[y] = lo
            return carry

        lax.fori_loop(0, 8, quad, 0)
        for y in range(32):
            first = jnp.dot(lhs[...], high[y], preferred_element_type=F32)
            second = jnp.dot(lhs[0:32, :], low[y], preferred_element_type=F32)
            total = first[0:32] + first[32:64] + second
            flux[y] = total[0:16].astype(BF16)
            hi, lo = split(total[16:32])
            own[y, 0:16] = hi
            own[y, 16:32] = lo

    @pl.when(comp[0] == 1)
    def _():
        copy = pltpu.make_async_copy(turned, buf.at[pl.ds(80, 2560)], sem)
        copy.start()
        prepare_rates(coef_a, coef_b, rate8, above, below, halo_l, halo_r)
        copy.wait()

        def main(g, y):
            return buf[80 + 160 * y + 8 * g : 88 + 160 * y + 8 * g, :]

        sub = lax.broadcasted_iota(jnp.int32, (8, W), 0)
        for i in range(EXT):
            first = extended(0, i, main, above, below, halo_l, halo_r)
            second = extended(10, i, main, above, below, halo_l, halo_r)
            for ref, u, v in zip((ta, tb), first, second):
                ref[8 * i : 8 * i + 8, :] = jnp.where(sub == 0, u, pltpu.roll(v, 1, 0))
        pairs = ((ta, tb), (tc, td))
        speed = lev_speed[0]
        for step in range(ADV):
            now, later = pairs[step % 2], pairs[(step + 1) % 2]
            for i in range(step + 1, EXT - 1 - step):
                new_a, new_b = advect_cell(
                    [[t[8 * k : 8 * k + 8, :] for k in (i - 1, i, i + 1)] for t in now],
                    [
                        [
                            jnp.broadcast_to(ref[16 * i + o : 16 * i + o + 1, :], (8, W))
                            for o in range(9)
                        ]
                        for ref in (coef_a, coef_b)
                    ],
                    speed,
                )
                later[0][8 * i : 8 * i + 8, :] = new_a
                later[1][8 * i : 8 * i + 8, :] = new_b
        for v in range(2):
            rows = [ta[pl.ds((ADV + y) * 8 + v, 8, stride=8), :] for y in (0, 8)]
            top[v] = jnp.concatenate(rows, axis=0).astype(BF16)


def tile_products(
    comp, me, src, dest, dst, own, arrived, weights, top, send, count, meta, parts
):
    band = send.shape[0] // TILES_PER_PEER
    tiles = weights.shape[0]

    lane8 = lanes(8)
    sub8 = lax.broadcasted_iota(jnp.int32, (8, W), 0)

    def product(lhs, t):
        return lax.dot_general(
            lhs[src[0, t]], weights[t], (((1,), (1,)), ((), ())), preferred_element_type=F32
        )

    @pl.when(comp[0] == 0)
    def _():
        for t in range(tiles):
            both = product(own, t)
            parts[8 * t : 8 * t + 8, :] = both[0:8] + both[16:24]
        pieces = []
        for v in range(2):
            for p in range(4):
                rows = [parts[pl.ds(128 * p + 64 * q + v, 8, stride=8), :] for q in range(2)]
                pieces.append(jnp.concatenate(rows, axis=0).astype(BF16))
        ids = jnp.zeros((8, W), F32)
        for t in range(tiles):
            named = jnp.where(sub8 == 0, dest[0, t], dst[0, t]).astype(F32)
            ids = jnp.where(lane8 % tiles == t, named, ids)
        pieces.append(jnp.concatenate([ids, ids], axis=0).astype(BF16))

        def spread(h, carry):
            for j, piece in enumerate(pieces):
                send[h * TILES_PER_PEER + j] = piece
            return carry

        lax.fori_loop(0, band, spread, 0)

    @pl.when(comp[0] == 1)
    def _():
        ids = jnp.where(sub8 == 0, me[0], lane8 % 16).astype(F32)
        ids = jnp.where((sub8 == 2) | (lane8 % tiles >= 16), -1.0, ids)

        def clear(h, carry):
            for j in range(TILES_PER_PEER):
                if j in (0, 4):
                    send[h * TILES_PER_PEER + j] = top[j // 4]
                else:
                    send[h * TILES_PER_PEER + j] = jnp.zeros((16, W), BF16)
            count[h] = 0
            meta[h] = ids
            return carry

        lax.fori_loop(0, band, clear, 0)
        for t in range(tiles):
            owner = dest[0, t]
            slot = count[owner]
            count[owner] = slot + 1
            place = slot + 1 + jnp.where(slot >= SLOTS // 2, 1, 0)
            send[owner * TILES_PER_PEER + place] = product(arrived, t).astype(BF16)
            named = jnp.where(
                (lane8 // 16 == place) & (sub8 == 2), dst[0, t].astype(F32), meta[owner]
            )
            meta[owner] = named

        def finish(h, carry):
            m = meta[h]
            send[h * TILES_PER_PEER + 8] = jnp.concatenate([m, m], axis=0).astype(BF16)
            return carry

        lax.fori_loop(0, band, finish, 0)


def advect_all(
    comp, lev_speed, turned, fields, above, below, halo_l, halo_r, coef_a, coef_b,
    result, dss, buf, sem, ta, tb, tc, td, speed,
):
    @pl.when(comp[0] == 0)
    def _():
        fetch(fields, buf.at[pl.ds(0, 2304)], sem)
        for f in range(72):
            for p in range(4):
                dss[32 * f + 8 * p : 32 * f + 8 * p + 8, :] = buf[
                    pl.ds(72 * 8 * p + f, 8, stride=72), :
                ]

    @pl.when(comp[0] == 1)
    def _():
        fetch(turned, buf, sem)
        dss[...] = jnp.zeros(dss.shape, F32)

        def main(g, y):
            return buf[160 * y + 8 * g : 160 * y + 8 * g + 8, :]

        groups = tuple(range(20))
        fill(groups, ta, tb, main, above, below, halo_l, halo_r)
        for n, v in enumerate(level_speeds(lev_speed, groups[:10])):
            speed[8 * n : 8 * n + 8, :] = v
            speed[80 + 8 * n : 88 + 8 * n, :] = v
        advect(((ta, tb), (tc, td)), coef_a, coef_b, speed, 20, 4, result)


def surface_select(back_owner, back_src, received, out):
    band = received.shape[0] // TILES_PER_PEER
    lane = lanes(1)
    sub8 = lax.broadcasted_iota(jnp.int32, (8, W), 0)
    wants = []
    for p in range(8):
        v = jnp.zeros((8, W), jnp.int32)
        for k in range(8):
            v = jnp.where(sub8 == k, back_owner[0, 8 * p + k] * 16 + back_src[0, 8 * p + k], v)
        wants.append(v)
    want = jnp.concatenate(wants, axis=0).astype(F32)

    def pair(q, carry):
        h = 2 * q
        ids = [
            received[(h + d) * TILES_PER_PEER + 8].astype(F32) for d in range(2)
        ]
        named = [v[0:1, :] * 16.0 + v[1:2, :] for v in ids]
        row = jnp.where(lane < 64, named[0], named[1])
        hot = jnp.where(jnp.broadcast_to(row, (64, W)) == want, 1.0, 0.0).astype(BF16)
        totals = []
        for v in range(2):
            rhs = jnp.concatenate(
                [
                    received[(h + d) * TILES_PER_PEER + 4 * v + j]
                    for d in range(2)
                    for j in range(4)
                ],
                axis=0,
            )
            totals.append(carry[v] + jnp.dot(hot, rhs, preferred_element_type=F32))
        return tuple(totals)

    zero = jnp.zeros((64, W), F32)
    sums = lax.fori_loop(0, band // 2, pair, (zero, zero), unroll=4)
    for v in range(2):
        out[64 * v : 64 * v + 64, :] = sums[v]


def surface_product(comp, back_dst, weights, mine, other, out, store, sem, table, parts, acc):
    tiles = weights.shape[0]

    @pl.when(comp[0] == 1)
    def _():
        out[...] = jnp.zeros(out.shape, F32)

    @pl.when(comp[0] == 0)
    def _():
        copy = pltpu.make_async_copy(weights, store, sem)
        copy.start()
        for v in range(2):
            rows = slice(64 * v, 64 * v + 64)
            hi, lo = split(mine[rows, :] + other[rows, :])
            for at, part in ((v, hi.astype(F32)), (2 + v, lo.astype(F32))):
                for p in range(8):
                    table[pl.ds(64 * p + at, 8, stride=8), :] = part[8 * p : 8 * p + 8]
        acc[...] = jnp.zeros(acc.shape, F32)
        copy.wait()
        for t in range(tiles):
            parts[8 * t : 8 * t + 8, :] = lax.dot_general(
                table[8 * t : 8 * t + 8, :].astype(BF16),
                store[t],
                (((1,), (1,)), ((), ())),
                preferred_element_type=F32,
            )
        for t in range(tiles):
            at = pl.ds(pl.multiple_of(back_dst[0, t] * 8, 8), 8)
            acc[at, :] = acc[at, :] + parts[8 * t : 8 * t + 8, :]
        for v in range(2):
            for p in range(4):
                out[32 * v + 8 * p : 32 * v + 8 * p + 8, :] = (
                    acc[pl.ds(64 * p + v, 8, stride=8), :]
                    + acc[pl.ds(64 * p + 2 + v, 8, stride=8), :]
                )


def force(comp, advected_ref, received_ref, profile, out, advected, received, sem, sem2):
    band = received.shape[0] // TILES_PER_PEER

    @pl.when(comp[0] == 0)
    def _():
        out[...] = jnp.zeros(out.shape, F32)

    @pl.when(comp[0] == 1)
    def _():
        late = pltpu.make_async_copy(advected_ref, advected, sem2)
        late.start()
        fetch(received_ref, received, sem)
        row = lax.broadcasted_iota(jnp.int32, (256, W), 0)
        point = jnp.where(row % 16 == lanes(256) % 16, row // 16, -2).astype(F32)

        def add(h, total):
            named = received[h * TILES_PER_PEER + 8].astype(F32)[2:3, :]
            hot = jnp.where(jnp.broadcast_to(named, (256, W)) == point, 1.0, 0.0)
            rhs = jnp.concatenate(
                [received[h * TILES_PER_PEER + j] for j in range(8)], axis=0
            )
            return total + jnp.dot(hot.astype(BF16), rhs, preferred_element_type=F32)

        total = lax.fori_loop(0, band, add, jnp.zeros((256, W), F32), unroll=4)
        level_hi, level_lo = split(profile[...])
        late.wait()
        for y in range(16):
            hi, lo = split(total[16 * y : 16 * y + 16, :])
            more = (
                jnp.dot(level_hi, hi, preferred_element_type=F32)
                + jnp.dot(level_hi, lo, preferred_element_type=F32)
                + jnp.dot(level_lo, hi, preferred_element_type=F32)
            )
            new = advected[160 * y : 160 * y + 160, :] + more
            for g in range(20):
                out[pl.ds(g * 128 + y, 8, stride=16), :] = new[8 * g : 8 * g + 8]


def shifted(array, axis, by):
    peers = lax.axis_size(axis)
    pairs = [(i, i + by) for i in range(peers) if 0 <= i + by < peers]
    return lax.ppermute(array, axis, pairs)


def shape(*dims, dtype=F32):
    return jax.ShapeDtypeStruct(dims, dtype)


def shards(
    atm_state,
    atm_mass,
    coupler,
    flux_dest,
    flux_dst_blk,
    flux_src_blk,
    conservative_flux_weights,
    ocn_tracers,
    ocean_neighbour_codes,
    ocn_rates,
    lev_speed,
    profile,
    back_owner,
    back_src_blk,
    back_dst_blk,
    return_remap_weights,
):
    comp = lax.axis_index("comp").astype(jnp.int32).reshape(1)
    band = lax.axis_size("gx")
    state = atm_state.reshape(72 * 32, W)
    tracer = ocn_tracers.reshape(2 * 80 * 16, W)
    codes = ocean_neighbour_codes.reshape(96, W)
    rates = ocn_rates.reshape(96, W)
    dma = pltpu.SemaphoreType.DMA
    buf = pltpu.VMEM((2560, W), F32)

    up, down, rate8 = call(
        pack_rows,
        [shape(4 * PR, W, dtype=BF16), shape(4 * PR, W, dtype=BF16), shape(128, W)],
        1, 2, 3,
        [buf, dma],
    )(comp, state, tracer, atm_mass, codes, rates)
    below = shifted(up, "gy", -1)
    above = shifted(down, "gy", 1)
    raw_left, raw_right, turned = call(
        pack_columns, [shape(PR, W), shape(PR, W), shape(2560, W)], 1, 2, 2, [buf, dma]
    )(comp, state, tracer, atm_mass, rate8)
    left, right = call(
        finish_columns,
        [shape(PR, W, dtype=BF16), shape(PR, W, dtype=BF16)],
        1, 0, 4,
        [],
    )(comp, raw_left, raw_right, above, below)
    halo_r = shifted(left, "gx", -1)
    halo_l = shifted(right, "gx", 1)

    top_profile = jnp.dot(profile[:, 0], coupler, precision=lax.Precision.HIGHEST)
    lhs = jnp.pad(jnp.concatenate([coupler, top_profile], axis=0), ((0, 14), (0, 8)))
    lhs_hi, lhs_lo = split(lhs)
    lhs = jnp.concatenate([lhs_hi, lhs_lo], axis=0)
    me = lax.axis_index("gx").astype(jnp.int32).reshape(1)
    small = pltpu.VMEM((EXT * 8, W), F32)

    fields, own, flux, top, coef_a, coef_b = call(
        assemble,
        [
            shape(72 * 32, W),
            shape(32, 32, W, dtype=BF16),
            shape(32, 16, W, dtype=BF16),
            shape(2, 16, W, dtype=BF16),
            shape(EXT * 16, W),
            shape(EXT * 16, W),
        ],
        2, 1, 6,
        [
            pltpu.VMEM((34 * 80, W), F32), dma, buf,
            pltpu.VMEM((32, 80, W), BF16), pltpu.VMEM((32, 80, W), BF16),
            pltpu.VMEM((80, W), F32), pltpu.VMEM((80, W), F32),
            small, small, small, small,
        ],
    )(comp, lev_speed, turned, rate8, above, below, halo_l, halo_r, lhs)
    arrived = shifted(flux, "comp", 1)
    send, = call(
        tile_products,
        [shape(band * TILES_PER_PEER, 16, W, dtype=BF16)],
        5, 0, 4,
        [
            pltpu.SMEM((band,), jnp.int32),
            pltpu.VMEM((band, 8, W), F32),
            pltpu.VMEM((512, W), F32),
        ],
    )(
        comp, me, flux_src_blk, flux_dest.reshape(1, 64), flux_dst_blk,
        own, arrived, conservative_flux_weights[0], top,
    )
    send, coef_a, coef_b = lax.optimization_barrier((send, coef_a, coef_b))
    received = lax.all_to_all(
        send.reshape(band, TILES_PER_PEER, 16, W), "gx", 0, 0, tiled=True
    ).reshape(band * TILES_PER_PEER, 16, W)
    grid = pltpu.VMEM((EXT * 160, W), F32)
    advected, dss = call(
        advect_all,
        [shape(16 * 160, W), shape(72 * 32, W)],
        2, 2, 6,
        [buf, dma, grid, grid, grid, grid, pltpu.VMEM((160, W), F32)],
    )(comp, lev_speed, turned, fields, above, below, halo_l, halo_r, coef_a, coef_b)
    levels = profile.reshape(160, 16)
    received, advected, levels = lax.optimization_barrier((received, advected, levels))
    mine, = call(surface_select, [shape(128, W)], 2, 0, 1, [])(
        back_owner, back_src_blk, received
    )
    other = shifted(mine, "comp", -1)
    ocean, = call(force, [shape(2560, W)], 1, 2, 1, [
        buf, pltpu.VMEM((band * TILES_PER_PEER, 16, W), BF16), dma, dma,
    ])(comp, advected, received, levels)
    tile_store = pltpu.VMEM(return_remap_weights.shape[1:], BF16)
    surface, = call(surface_product, [shape(64, W)], 2, 1, 2, [
        tile_store, dma,
        pltpu.VMEM((512, W), F32), pltpu.VMEM((512, W), F32), pltpu.VMEM((256, W), F32),
    ])(comp, back_dst_blk, return_remap_weights[0], mine, other)
    return (
        dss.reshape(1, 72, 32, W),
        surface.reshape(1, 2, 32, W),
        ocean.reshape(1, 2, 80, 16, W),
    )


def solution(mesh):
    placed = (
        P("comp", None, "gy", "gx"),
        P("gy", "gx"),
        P(),
        P("gy", "gx", None),
        P("gy", "gx"),
        P("gy", "gx"),
        P("gy", "gx", None, None),
        P("comp", None, None, "gy", "gx"),
        P(None, "gy", "gx"),
        P(None, "gy", "gx"),
        P(),
        P(),
        P("gy", "gx"),
        P("gy", "gx"),
        P("gy", "gx"),
        P("gy", "gx", None, None),
    )
    return jax.shard_map(
        shards,
        mesh=mesh,
        in_specs=placed,
        out_specs=(
            P("comp", None, "gy", "gx"),
            P("comp", None, "gy", "gx"),
            P("comp", None, None, "gy", "gx"),
        ),
        check_vma=False,
    )
```

```python
import functools

import jax
import jax.numpy as jnp
from jax import lax
from jax.experimental import pallas as pl
from jax.experimental.pallas import tpu as pltpu
from jax.sharding import PartitionSpec as P

F32 = jnp.float32
BF16 = jnp.bfloat16
ADV = 4
W = 128
PR = 176
EXT = 24
TILES_PER_PEER = 9


def lanes(rows):
    return lax.broadcasted_iota(jnp.int32, (rows, W), 1)


def fetch(src, dst, sem):
    copy = pltpu.make_async_copy(src, dst, sem)
    copy.start()
    copy.wait()


def split(value):
    hi = value.astype(BF16)
    return hi, (value - hi.astype(F32)).astype(BF16)


def params():
    return pltpu.CompilerParams(vmem_limit_bytes=16 * 1024 * 1024)


def call(body, out_shape, n_smem, n_any, n_vmem, scratch):
    specs = (
        [pl.BlockSpec(memory_space=pltpu.SMEM)] * n_smem
        + [pl.BlockSpec(memory_space=pl.ANY)] * n_any
        + [pl.BlockSpec(memory_space=pltpu.VMEM)] * n_vmem
    )
    return pl.pallas_call(
        body,
        out_shape=out_shape,
        in_specs=specs,
        out_specs=[pl.BlockSpec(memory_space=pltpu.VMEM)] * len(out_shape),
        scratch_shapes=scratch,
        compiler_params=params(),
        name=body.__name__,
    )


def pack_rows(comp, state, tracer, mass, codes, rates, up, down, rate8):
    @pl.when(comp[0] == 0)
    def _():
        for dst, y in ((up, 0), (down, 31)):
            m = jnp.broadcast_to(mass[y : y + 1, :], (8, W))
            parts = [state[pl.ds(g * 256 + y, 8, stride=32), :] * m for g in range(9)] + [m]
            for p in range(5):
                hi, lo = split(jnp.concatenate(parts[2 * p : 2 * p + 2], axis=0))
                dst[16 * p : 16 * p + 16, :] = hi
                dst[80 + 16 * p : 96 + 16 * p, :] = lo

    @pl.when(comp[0] == 1)
    def _():
        for o in range(8):
            acc = jnp.zeros((16, W), F32)
            for k in range(6):
                rows = slice(16 * k, 16 * k + 16)
                acc = acc + jnp.where(codes[rows, :] == o, rates[rows, :], 0.0)
            rate8[16 * o : 16 * o + 16, :] = acc
        for dst, first in ((up, 0), (down, 12)):
            for j in range(ADV):
                y = first + j
                for p in range(10):
                    both = jnp.concatenate(
                        [tracer[pl.ds(g * 128 + y, 8, stride=16), :] for g in (2 * p, 2 * p + 1)],
                        axis=0,
                    )
                    dst[j * PR + 16 * p : j * PR + 16 * p + 16, :] = both.astype(BF16)
                r = rate8[pl.ds(y, 8, stride=16), :]
                dst[j * PR + 160 : j * PR + 176, :] = jnp.concatenate([r, r], axis=0).astype(BF16)


def pack_columns(comp, state, tracer, mass, rate8, left, right, turned):
    lane = lanes(8)

    @pl.when(comp[0] == 0)
    def _():
        for g in range(10):
            to_left = jnp.zeros((8, W), F32)
            to_right = jnp.zeros((8, W), F32)
            for y in range(32):
                v = jnp.broadcast_to(mass[y : y + 1, :], (8, W))
                if g < 9:
                    v = v * state[pl.ds(g * 256 + y, 8, stride=32), :]
                turned[80 * y + 8 * g : 80 * y + 8 * g + 8, :] = v
                v = pltpu.roll(v, y, 1)
                to_left = jnp.where(lane == y, v, to_left)
                to_right = jnp.where(lane == (y - 1) % W, v, to_right)
            left[8 * g : 8 * g + 8, :] = to_left
            right[8 * g : 8 * g + 8, :] = to_right

    @pl.when(comp[0] == 1)
    def _():
        for g in range(21):
            to_left = jnp.zeros((8, W), F32)
            to_right = jnp.zeros((8, W), F32)
            for y in range(16):
                i = y + ADV
                if g < 20:
                    v = tracer[pl.ds(g * 128 + y, 8, stride=16), :]
                    turned[160 * y + 8 * g : 160 * y + 8 * g + 8, :] = v
                else:
                    v = rate8[pl.ds(y, 8, stride=16), :]
                v = pltpu.roll(v, 4 * i, 1)
                to_left = jnp.where(lane // 4 == i, v, to_left)
                to_right = jnp.where(lane // 4 == i - 1, v, to_right)
            left[8 * g : 8 * g + 8, :] = to_left
            right[8 * g : 8 * g + 8, :] = to_right
        left[168:176, :] = jnp.zeros((8, W), F32)
        right[168:176, :] = jnp.zeros((8, W), F32)


def finish_columns(comp, raw_left, raw_right, above, below, left, right):
    lane = lanes(16)

    @pl.when(comp[0] == 0)
    def _():
        for p in range(5):
            rows = slice(16 * p, 16 * p + 16)
            low = slice(80 + 16 * p, 96 + 16 * p)
            up = above[rows, :].astype(F32) + above[low, :].astype(F32)
            down = below[rows, :].astype(F32) + below[low, :].astype(F32)
            down = pltpu.roll(down, 31, 1)
            for src, dst, at in ((raw_left, left, 0), (raw_right, right, 1)):
                v = src[rows, :]
                pos = (lane + at) % 4
                before = jnp.where(lane == (W - at) % W, up, pltpu.roll(v, 1, 1))
                after = jnp.where(lane == 31 - at, down, pltpu.roll(v, W - 1, 1))
                v = v + jnp.where(pos == 0, before, 0.0) + jnp.where(pos == 3, after, 0.0)
                hi, lo = split(v)
                dst[rows, :] = hi
                dst[low, :] = lo

    @pl.when(comp[0] == 1)
    def _():
        for p in range(11):
            rows = slice(16 * p, 16 * p + 16)
            to_left = raw_left[rows, :]
            to_right = raw_right[rows, :]
            for src, first in ((above, 0), (below, 20)):
                for j in range(ADV):
                    i = first + j
                    v = src[j * PR + 16 * p : j * PR + 16 * p + 16, :].astype(F32)
                    v = pltpu.roll(v, 4 * i, 1)
                    to_left = jnp.where(lane // 4 == i, v, to_left)
                    to_right = jnp.where(lane // 4 == (i - 1) % 32, v, to_right)
            left[rows, :] = to_left.astype(BF16)
            right[rows, :] = to_right.astype(BF16)


def swap_left(a, b):
    lane = lanes(a.shape[0])
    ra, rb = pltpu.roll(a, W - 1, 1), pltpu.roll(b, W - 1, 1)
    return jnp.where(lane == W - 1, rb, ra), jnp.where(lane == W - 1, ra, rb)


def swap_right(a, b):
    lane = lanes(a.shape[0])
    ra, rb = pltpu.roll(a, 1, 1), pltpu.roll(b, 1, 1)
    return jnp.where(lane == 0, rb, ra), jnp.where(lane == 0, ra, rb)


def halo_tile(from_right, from_left, i):
    lane = lanes(8)
    v = jnp.where(lane // 4 == i, from_right, from_left)
    v = pltpu.roll(v, (W - 4 * i) % W, 1)
    return jnp.where((lane < 4) | (lane >= W - 4), v, 0.0)


def extended(g, i, main, above, below, halo_l, halo_r):
    rows = slice(8 * g, 8 * g + 8)
    half = slice(8 * (g % 2), 8 * (g % 2) + 8)
    pair = 16 * (g // 2)

    def wide(ref, at):
        return ref[at : at + 16, :].astype(F32)[half]

    if i < ADV:
        a = wide(above, i * PR + pair)
    elif i >= EXT - ADV:
        a = wide(below, (i - EXT + ADV) * PR + pair)
    else:
        a = main(g, i - ADV)
    b = halo_tile(wide(halo_r, pair), wide(halo_l, pair), i)
    return a, b


RIGHTWARD = (2, 4, 7)
LEFTWARD = (0, 3, 5)


def prepare_rates(coef_a, coef_b, rate8, above, below, halo_l, halo_r):
    sub = lax.broadcasted_iota(jnp.int32, (8, W), 0)
    right = (sub == 2) | (sub == 4) | (sub == 7)
    left = (sub == 0) | (sub == 3) | (sub == 5)

    def main(g, y):
        return rate8[pl.ds(y, 8, stride=16), :]

    for i in range(EXT):
        a, b = extended(20, i, main, above, below, halo_l, halo_r)
        la, lb = swap_left(a, b)
        ra, rb = swap_right(a, b)
        coef_a[i * 16 : i * 16 + 8, :] = jnp.where(right, ra, jnp.where(left, la, a))
        coef_b[i * 16 : i * 16 + 8, :] = jnp.where(right, rb, jnp.where(left, lb, b))
        coef_a[i * 16 + 8 : i * 16 + 16, :] = jnp.broadcast_to(
            jnp.sum(a, axis=0, keepdims=True), (8, W)
        )
        coef_b[i * 16 + 8 : i * 16 + 16, :] = jnp.broadcast_to(
            jnp.sum(b, axis=0, keepdims=True), (8, W)
        )


def level_speeds(lev_speed, groups):
    sub = lax.broadcasted_iota(jnp.int32, (8, W), 0)
    speeds = []
    for g in groups:
        v = jnp.zeros((8, W), F32)
        for k in range(8):
            v = jnp.where(sub == k, lev_speed[(8 * g + k) % 80], v)
        speeds.append(v)
    return speeds


def fill(groups, ta, tb, main, above, below, halo_l, halo_r):
    wide = 8 * len(groups)
    for n, g in enumerate(groups):
        for part in range(3):
            span = range(8 * part, 8 * part + 8)
            pairs = [extended(g, i, main, above, below, halo_l, halo_r) for i in span]
            for i, (a, b) in zip(span, pairs):
                ta[i * wide + 8 * n : i * wide + 8 * n + 8, :] = a
                tb[i * wide + 8 * n : i * wide + 8 * n + 8, :] = b


def advect_cell(cells, coefs, speed):
    outs = []
    for (t0, t1, t2), c in zip(cells, coefs):
        to_r = c[2] * t0 + c[4] * t1 + c[7] * t2
        to_l = c[0] * t0 + c[3] * t1 + c[5] * t2
        mid = c[1] * t0 + c[6] * t2 - c[8] * t1
        outs.append((t1, to_r, to_l, mid))
    (a1, ar, al, am), (b1, br, bl, bm) = outs
    ua, ub = swap_left(ar, br)
    va, vb = swap_right(al, bl)
    return a1 + speed * (am + ua + va), b1 + speed * (bm + ub + vb)


def advect(pairs, coef_a, coef_b, speed, count, chunk, result):
    wide = count * 8

    def at(i, n):
        return pl.ds(pl.multiple_of(i * wide + 8 * n, 8), 8)

    for step in range(ADV):
        now, later = pairs[step % 2], pairs[(step + 1) % 2]
        last = step == ADV - 1

        def row(i, carry, now=now, later=later, last=last):
            def coef(ref, o):
                return jnp.broadcast_to(ref[pl.ds(i * 16 + o, 1), :], (8, W))

            coefs = [[coef(ref, o) for o in range(9)] for ref in (coef_a, coef_b)]
            for base in range(0, count, chunk):
                span = range(base, base + chunk)
                news = []
                for n in span:
                    cells = [[t[at(k, n), :] for k in (i - 1, i, i + 1)] for t in now]
                    news.append(advect_cell(cells, coefs, speed[8 * n : 8 * n + 8, :]))
                for n, (new_a, new_b) in zip(span, news):
                    if last:
                        place = pl.multiple_of((i - ADV) * wide + 8 * n, 8)
                        result[pl.ds(place, 8), :] = new_a
                    else:
                        later[0][at(i, n), :] = new_a
                        later[1][at(i, n), :] = new_b
            return carry

        lax.fori_loop(step + 1, EXT - 1 - step, row, 0)


def assemble(
    comp, lev_speed, turned, rate8, above, below, halo_l, halo_r, lhs,
    dss, own, flux, top, coef_a, coef_b,
    buf, sem, edge, high, low, far_l, far_r, ta, tb, tc, td,
):
    lane = lanes(8)

    @pl.when(comp[0] == 0)
    def _():
        copy = pltpu.make_async_copy(turned, buf.at[pl.ds(80, 2560)], sem)
        copy.start()
        for p in range(5):
            rows = slice(16 * p, 16 * p + 16)
            rest = slice(80 + 16 * p, 96 + 16 * p)
            v = halo_l[rows, :].astype(F32) + halo_l[rest, :].astype(F32)
            far_l[rows, :] = pltpu.roll(v, 2, 1)
            far_r[rows, :] = halo_r[rows, :].astype(F32) + halo_r[rest, :].astype(F32)
            v = above[rows, :].astype(F32) + above[rest, :].astype(F32)
            buf[16 * p : 16 * p + 16, :] = v
            v = below[rows, :].astype(F32) + below[rest, :].astype(F32)
            buf[2640 + 16 * p : 2656 + 16 * p, :] = v
        for g in range(10):
            rows = slice(8 * g, 8 * g + 8)
            from_l, from_r = far_l[rows, :], far_r[rows, :]
            for y in range(32):
                v = jnp.where(lane == y, from_r, from_l)
                at = 80 * y + 8 * g
                edge[at : at + 8, :] = pltpu.roll(v, (W - 1 - y) % W, 1)
        copy.wait()

        def quad(q, carry):
            first = lane % 4 == 0
            final = lane % 4 == 3
            outer = (lane == 0) | (lane == W - 1)

            def at(row, g, wide=80):
                return pl.ds(pl.multiple_of(row * wide + 8 * g, 8), 8)

            for r in range(4):
                y = 4 * q + r
                values = []
                for g in (9, 0, 1, 2, 3, 4, 5, 6, 7, 8):
                    v = buf[at(y + 1, g), :]
                    if r == 0:
                        v = v + buf[at(y, g), :]
                    if r == 3:
                        v = v + buf[at(y + 2, g), :]
                    near = jnp.where(first, pltpu.roll(v, 1, 1), pltpu.roll(v, W - 1, 1))
                    near = jnp.where(outer, edge[at(y, g), :], near)
                    v = v + jnp.where(first | final, near, 0.0)
                    if g == 9:
                        inverse = 1.0 / v
                    else:
                        values.append(v * inverse)
                for g, v in enumerate(values):
                    dss[at(y, g, 72), :] = v
                hi, lo = split(jnp.concatenate(values + [jnp.zeros((8, W), F32)], axis=0))
                high[y] = hi
                low[y] = lo
            return carry

        lax.fori_loop(0, 8, quad, 0)
        for y in range(32):
            first = jnp.dot(lhs[...], high[y], preferred_element_type=F32)
            second = jnp.dot(lhs[0:32, :], low[y], preferred_element_type=F32)
            total = first[0:32] + first[32:64] + second
            flux[y] = total[0:16].astype(BF16)
            hi, lo = split(total[16:32])
            own[y, 0:16] = hi
            own[y, 16:32] = lo

    @pl.when(comp[0] == 1)
    def _():
        copy = pltpu.make_async_copy(turned, buf.at[pl.ds(80, 2560)], sem)
        copy.start()
        prepare_rates(coef_a, coef_b, rate8, above, below, halo_l, halo_r)
        copy.wait()

        def main(g, y):
            return buf[80 + 160 * y + 8 * g : 88 + 160 * y + 8 * g, :]

        sub = lax.broadcasted_iota(jnp.int32, (8, W), 0)
        for i in range(EXT):
            first = extended(0, i, main, above, below, halo_l, halo_r)
            second = extended(10, i, main, above, below, halo_l, halo_r)
            for ref, u, v in zip((ta, tb), first, second):
                ref[8 * i : 8 * i + 8, :] = jnp.where(sub == 0, u, pltpu.roll(v, 1, 0))
        pairs = ((ta, tb), (tc, td))
        speed = lev_speed[0]
        for step in range(ADV):
            now, later = pairs[step % 2], pairs[(step + 1) % 2]
            for i in range(step + 1, EXT - 1 - step):
                new_a, new_b = advect_cell(
                    [[t[8 * k : 8 * k + 8, :] for k in (i - 1, i, i + 1)] for t in now],
                    [
                        [
                            jnp.broadcast_to(ref[16 * i + o : 16 * i + o + 1, :], (8, W))
                            for o in range(9)
                        ]
                        for ref in (coef_a, coef_b)
                    ],
                    speed,
                )
                later[0][8 * i : 8 * i + 8, :] = new_a
                later[1][8 * i : 8 * i + 8, :] = new_b
        for v in range(2):
            rows = [ta[pl.ds((ADV + y) * 8 + v, 8, stride=8), :] for y in (0, 8)]
            top[v] = jnp.concatenate(rows, axis=0).astype(BF16)


def tile_products(
    comp, src, dest, dst, own, arrived, weights, top, send, count, meta, parts
):
    band = send.shape[0] // TILES_PER_PEER
    tiles = weights.shape[0]

    lane8 = lanes(8)
    sub8 = lax.broadcasted_iota(jnp.int32, (8, W), 0)

    def product(lhs, t):
        return lax.dot_general(
            lhs[src[0, t]], weights[t], (((1,), (1,)), ((), ())), preferred_element_type=F32
        )

    @pl.when(comp[0] == 0)
    def _():
        for t in range(tiles):
            both = product(own, t)
            parts[8 * t : 8 * t + 8, :] = both[0:8] + both[16:24]
        pieces = []
        for v in range(2):
            for p in range(4):
                rows = [parts[pl.ds(128 * p + 64 * q + v, 8, stride=8), :] for q in range(2)]
                pieces.append(jnp.concatenate(rows, axis=0).astype(BF16))
        ids = jnp.zeros((8, W), F32)
        for t in range(tiles):
            named = jnp.where(sub8 == 0, dest[0, t], dst[0, t]).astype(F32)
            ids = jnp.where(lane8 % tiles == t, named, ids)
        pieces.append(jnp.concatenate([ids, ids], axis=0).astype(BF16))

        def spread(h, carry):
            for j, piece in enumerate(pieces):
                send[h * TILES_PER_PEER + j] = piece
            return carry

        lax.fori_loop(0, band, spread, 0)

    @pl.when(comp[0] == 1)
    def _():
        def clear(h, carry):
            for j in range(TILES_PER_PEER):
                if j < 2:
                    send[h * TILES_PER_PEER + j] = top[j]
                else:
                    send[h * TILES_PER_PEER + j] = jnp.zeros((16, W), BF16)
            count[h] = 0
            meta[h] = jnp.full((8, W), -1.0, F32)
            return carry

        lax.fori_loop(0, band, clear, 0)
        for t in range(tiles):
            owner = dest[0, t]
            slot = count[owner]
            count[owner] = slot + 1
            place = slot + 2
            send[owner * TILES_PER_PEER + place] = product(arrived, t).astype(BF16)
            named = jnp.where(
                (lane8 // 16 == place) & (sub8 == 2), dst[0, t].astype(F32), meta[owner]
            )
            meta[owner] = named

        def finish(h, carry):
            m = meta[h]
            send[h * TILES_PER_PEER + 8] = jnp.concatenate([m, m], axis=0).astype(BF16)
            return carry

        lax.fori_loop(0, band, finish, 0)


def advect_all(
    comp, lev_speed, turned, fields, above, below, halo_l, halo_r, coef_a, coef_b,
    result, dss, buf, sem, ta, tb, tc, td, speed,
):
    @pl.when(comp[0] == 0)
    def _():
        fetch(fields, buf.at[pl.ds(0, 2304)], sem)
        for f in range(72):
            for p in range(4):
                dss[32 * f + 8 * p : 32 * f + 8 * p + 8, :] = buf[
                    pl.ds(72 * 8 * p + f, 8, stride=72), :
                ]

    @pl.when(comp[0] == 1)
    def _():
        fetch(turned, buf, sem)
        dss[...] = jnp.zeros(dss.shape, F32)

        def main(g, y):
            return buf[160 * y + 8 * g : 160 * y + 8 * g + 8, :]

        groups = tuple(range(20))
        fill(groups, ta, tb, main, above, below, halo_l, halo_r)
        for n, v in enumerate(level_speeds(lev_speed, groups[:10])):
            speed[8 * n : 8 * n + 8, :] = v
            speed[80 + 8 * n : 88 + 8 * n, :] = v
        advect(((ta, tb), (tc, td)), coef_a, coef_b, speed, 20, 4, result)


def wanted(back_owner, back_src):
    sub8 = lax.broadcasted_iota(jnp.int32, (8, W), 0)
    wants = []
    for p in range(8):
        v = jnp.zeros((8, W), jnp.int32)
        for k in range(8):
            v = jnp.where(sub8 == k, back_owner[0, 8 * p + k] * 16 + back_src[0, 8 * p + k], v)
        wants.append(v)
    return jnp.concatenate(wants, axis=0).astype(F32)


def surface_select(comp, back_owner, back_src, weights, received, out):
    band = received.shape[0] // TILES_PER_PEER

    @pl.when(comp[0] == 0)
    def _():
        lane = lanes(1)
        want = wanted(back_owner, back_src)

        def pair(q, carry):
            h = 2 * q
            ids = [received[(h + d) * TILES_PER_PEER + 8].astype(F32) for d in range(2)]
            named = [v[0:1, :] * 16.0 + v[1:2, :] for v in ids]
            row = jnp.where(lane < 64, named[0], named[1])
            hot = jnp.where(jnp.broadcast_to(row, (64, W)) == want, 1.0, 0.0).astype(BF16)
            totals = []
            for v in range(2):
                rhs = jnp.concatenate(
                    [
                        received[(h + d) * TILES_PER_PEER + 4 * v + j]
                        for d in range(2)
                        for j in range(4)
                    ],
                    axis=0,
                )
                totals.append(carry[v] + jnp.dot(hot, rhs, preferred_element_type=F32))
            return tuple(totals)

        zero = jnp.zeros((64, W), F32)
        sums = lax.fori_loop(0, band // 2, pair, (zero, zero), unroll=4)
        for v in range(2):
            out[64 * v : 64 * v + 64, :] = sums[v]


def finish(
    comp, back_owner, back_src, back_dst,
    advected, received, profile, weights, mine, other,
    ocean, surface, table, parts, acc,
):
    band = received.shape[0] // TILES_PER_PEER
    tiles = weights.shape[0]

    @pl.when(comp[0] == 0)
    def _():
        want = wanted(back_owner, back_src)
        sums = [mine[64 * v : 64 * v + 64, :] for v in range(2)]
        for c in range(band // 8):
            row = (lanes(64) + c * W).astype(F32)
            hot = jnp.where(row == want, 1.0, 0.0).astype(BF16)
            for v in range(2):
                rhs = jnp.concatenate([other[(8 * c + h) * 2 + v] for h in range(8)], axis=0)
                sums[v] = sums[v] + jnp.dot(hot, rhs, preferred_element_type=F32)
        for v in range(2):
            hi, lo = split(sums[v])
            for at, part in ((v, hi.astype(F32)), (2 + v, lo.astype(F32))):
                for p in range(8):
                    table[pl.ds(64 * p + at, 8, stride=8), :] = part[8 * p : 8 * p + 8]
        acc[...] = jnp.zeros(acc.shape, F32)
        for t in range(tiles):
            parts[8 * t : 8 * t + 8, :] = lax.dot_general(
                table[8 * t : 8 * t + 8, :].astype(BF16),
                weights[t],
                (((1,), (1,)), ((), ())),
                preferred_element_type=F32,
            )
        for t in range(tiles):
            at = pl.ds(pl.multiple_of(back_dst[0, t] * 8, 8), 8)
            acc[at, :] = acc[at, :] + parts[8 * t : 8 * t + 8, :]
        for v in range(2):
            for p in range(4):
                surface[32 * v + 8 * p : 32 * v + 8 * p + 8, :] = (
                    acc[pl.ds(64 * p + v, 8, stride=8), :]
                    + acc[pl.ds(64 * p + 2 + v, 8, stride=8), :]
                )
        ocean[...] = jnp.zeros(ocean.shape, F32)

    @pl.when(comp[0] == 1)
    def _():
        surface[...] = jnp.zeros(surface.shape, F32)
        row = lax.broadcasted_iota(jnp.int32, (256, W), 0)
        point = jnp.where(row % 16 == lanes(256) % 16, row // 16, -2).astype(F32)

        def add(h, total):
            named = received[h * TILES_PER_PEER + 8].astype(F32)[2:3, :]
            hot = jnp.where(jnp.broadcast_to(named, (256, W)) == point, 1.0, 0.0)
            rhs = jnp.concatenate(
                [received[h * TILES_PER_PEER + j] for j in range(8)], axis=0
            )
            return total + jnp.dot(hot.astype(BF16), rhs, preferred_element_type=F32)

        total = lax.fori_loop(0, band, add, jnp.zeros((256, W), F32), unroll=4)
        level_hi, level_lo = split(profile[...])
        for y in range(16):
            hi, lo = split(total[16 * y : 16 * y + 16, :])
            more = (
                jnp.dot(level_hi, hi, preferred_element_type=F32)
                + jnp.dot(level_hi, lo, preferred_element_type=F32)
                + jnp.dot(level_lo, hi, preferred_element_type=F32)
            )
            new = advected[160 * y : 160 * y + 160, :] + more
            for g in range(20):
                ocean[pl.ds(g * 128 + y, 8, stride=16), :] = new[8 * g : 8 * g + 8]


def shifted(array, axis, by):
    peers = lax.axis_size(axis)
    pairs = [(i, i + by) for i in range(peers) if 0 <= i + by < peers]
    return lax.ppermute(array, axis, pairs)


def shape(*dims, dtype=F32):
    return jax.ShapeDtypeStruct(dims, dtype)


def shards(
    atm_state,
    atm_mass,
    coupler,
    flux_dest,
    flux_dst_blk,
    flux_src_blk,
    conservative_flux_weights,
    ocn_tracers,
    ocean_neighbour_codes,
    ocn_rates,
    lev_speed,
    profile,
    back_owner,
    back_src_blk,
    back_dst_blk,
    return_remap_weights,
):
    comp = lax.axis_index("comp").astype(jnp.int32).reshape(1)
    band = lax.axis_size("gx")
    state = atm_state.reshape(72 * 32, W)
    tracer = ocn_tracers.reshape(2 * 80 * 16, W)
    codes = ocean_neighbour_codes.reshape(96, W)
    rates = ocn_rates.reshape(96, W)
    dma = pltpu.SemaphoreType.DMA
    buf = pltpu.VMEM((2560, W), F32)

    up, down, rate8 = call(
        pack_rows,
        [shape(4 * PR, W, dtype=BF16), shape(4 * PR, W, dtype=BF16), shape(128, W)],
        1, 0, 5,
        [],
    )(comp, state, tracer, atm_mass, codes, rates)
    below = shifted(up, "gy", -1)
    above = shifted(down, "gy", 1)
    raw_left, raw_right, turned = call(
        pack_columns, [shape(PR, W), shape(PR, W), shape(2560, W)], 1, 0, 4, []
    )(comp, state, tracer, atm_mass, rate8)
    left, right = call(
        finish_columns,
        [shape(PR, W, dtype=BF16), shape(PR, W, dtype=BF16)],
        1, 0, 4,
        [],
    )(comp, raw_left, raw_right, above, below)
    halo_r = shifted(left, "gx", -1)
    halo_l = shifted(right, "gx", 1)

    top_profile = jnp.dot(profile[:, 0], coupler, precision=lax.Precision.HIGHEST)
    lhs = jnp.pad(jnp.concatenate([coupler, top_profile], axis=0), ((0, 14), (0, 8)))
    lhs_hi, lhs_lo = split(lhs)
    lhs = jnp.concatenate([lhs_hi, lhs_lo], axis=0)
    small = pltpu.VMEM((EXT * 8, W), F32)

    fields, own, flux, top, coef_a, coef_b = call(
        assemble,
        [
            shape(72 * 32, W),
            shape(32, 32, W, dtype=BF16),
            shape(32, 16, W, dtype=BF16),
            shape(2, 16, W, dtype=BF16),
            shape(EXT * 16, W),
            shape(EXT * 16, W),
        ],
        2, 1, 6,
        [
            pltpu.VMEM((34 * 80, W), F32), dma, buf,
            pltpu.VMEM((32, 80, W), BF16), pltpu.VMEM((32, 80, W), BF16),
            pltpu.VMEM((80, W), F32), pltpu.VMEM((80, W), F32),
            small, small, small, small,
        ],
    )(
        comp, lev_speed, turned, rate8, above, below, halo_l, halo_r, lhs,
    )
    arrived = shifted(flux, "comp", 1)
    send, = call(
        tile_products,
        [shape(band * TILES_PER_PEER, 16, W, dtype=BF16)],
        4, 0, 4,
        [
            pltpu.SMEM((band,), jnp.int32),
            pltpu.VMEM((band, 8, W), F32),
            pltpu.VMEM((512, W), F32),
        ],
    )(
        comp, flux_src_blk, flux_dest.reshape(1, 64), flux_dst_blk,
        own, arrived, conservative_flux_weights[0], top,
    )
    send, coef_a, coef_b = lax.optimization_barrier((send, coef_a, coef_b))
    received = lax.all_to_all(
        send.reshape(band, TILES_PER_PEER, 16, W), "gx", 0, 0, tiled=True
    ).reshape(band * TILES_PER_PEER, 16, W)
    grid = pltpu.VMEM((EXT * 160, W), F32)
    advected, dss = call(
        advect_all,
        [shape(16 * 160, W), shape(72 * 32, W)],
        2, 2, 6,
        [buf, dma, grid, grid, grid, grid, pltpu.VMEM((160, W), F32)],
    )(
        comp, lev_speed, turned, fields, above, below, halo_l, halo_r, coef_a, coef_b,
    )
    levels = profile.reshape(160, 16)
    received, advected, levels = lax.optimization_barrier((received, advected, levels))
    tops = received.reshape(band, TILES_PER_PEER, 16, W)[:, :2].reshape(2 * band, 16, W)
    other = shifted(tops, "comp", -1)
    mine, = call(surface_select, [shape(128, W)], 3, 1, 1, [])(
        comp, back_owner, back_src_blk, return_remap_weights[0], received
    )
    ocean, surface = call(finish, [shape(2560, W), shape(64, W)], 4, 0, 6, [
        pltpu.VMEM((512, W), F32), pltpu.VMEM((512, W), F32), pltpu.VMEM((256, W), F32),
    ])(
        comp, back_owner, back_src_blk, back_dst_blk,
        advected, received, levels, return_remap_weights[0], mine, other,
    )
    return (
        dss.reshape(1, 72, 32, W),
        surface.reshape(1, 2, 32, W),
        ocean.reshape(1, 2, 80, 16, W),
    )


def solution(mesh):
    placed = (
        P("comp", None, "gy", "gx"),
        P("gy", "gx"),
        P(),
        P("gy", "gx", None),
        P("gy", "gx"),
        P("gy", "gx"),
        P("gy", "gx", None, None),
        P("comp", None, None, "gy", "gx"),
        P(None, "gy", "gx"),
        P(None, "gy", "gx"),
        P(),
        P(),
        P("gy", "gx"),
        P("gy", "gx"),
        P("gy", "gx"),
        P("gy", "gx", None, None),
    )
    return jax.shard_map(
        shards,
        mesh=mesh,
        in_specs=placed,
        out_specs=(
            P("comp", None, "gy", "gx"),
            P("comp", None, "gy", "gx"),
            P("comp", None, None, "gy", "gx"),
        ),
        check_vma=False,
    )
```

```python
import functools

import jax
import jax.numpy as jnp
from jax import lax
from jax.experimental import pallas as pl
from jax.experimental.pallas import tpu as pltpu
from jax.sharding import PartitionSpec as P

F32 = jnp.float32
BF16 = jnp.bfloat16
ADV = 4
W = 128
PR = 176
EXT = 24
TILES_PER_PEER = 9


def lanes(rows):
    return lax.broadcasted_iota(jnp.int32, (rows, W), 1)


def split(value):
    hi = value.astype(BF16)
    return hi, (value - hi.astype(F32)).astype(BF16)


def call(body, out_shape, n_smem, n_any, n_vmem, scratch, mebibytes=16):
    specs = (
        [pl.BlockSpec(memory_space=pltpu.SMEM)] * n_smem
        + [pl.BlockSpec(memory_space=pl.ANY)] * n_any
        + [pl.BlockSpec(memory_space=pltpu.VMEM)] * n_vmem
    )
    return pl.pallas_call(
        body,
        out_shape=out_shape,
        in_specs=specs,
        out_specs=[pl.BlockSpec(memory_space=pltpu.VMEM)] * len(out_shape),
        scratch_shapes=scratch,
        compiler_params=pltpu.CompilerParams(vmem_limit_bytes=mebibytes * 1024 * 1024),
        name=body.__name__,
    )


def pack_rows(
    comp, state_ref, tracer_ref, mass_ref, codes_ref, rates_ref, up, down, rate8,
    buf, mass, codes, rates, sem,
):
    state = tracer = buf

    def fetch_all(*pairs):
        copies = [
            pltpu.make_async_copy(src, dst, sem.at[n]) for n, (src, dst) in enumerate(pairs)
        ]
        for copy in copies:
            copy.start()
        for copy in copies:
            copy.wait()

    @pl.when(comp[0] == 0)
    def _():
        fetch_all((state_ref, buf.at[pl.ds(0, 2304)]), (mass_ref, mass))
        for dst, y in ((up, 0), (down, 31)):
            m = jnp.broadcast_to(mass[y : y + 1, :], (8, W))
            parts = [state[pl.ds(g * 256 + y, 8, stride=32), :] * m for g in range(9)] + [m]
            for p in range(5):
                hi, lo = split(jnp.concatenate(parts[2 * p : 2 * p + 2], axis=0))
                dst[16 * p : 16 * p + 16, :] = hi
                dst[80 + 16 * p : 96 + 16 * p, :] = lo

    @pl.when(comp[0] == 1)
    def _():
        fetch_all((tracer_ref, buf), (codes_ref, codes), (rates_ref, rates))
        for o in range(8):
            acc = jnp.zeros((16, W), F32)
            for k in range(6):
                rows = slice(16 * k, 16 * k + 16)
                acc = acc + jnp.where(codes[rows, :] == o, rates[rows, :], 0.0)
            rate8[16 * o : 16 * o + 16, :] = acc
        for dst, first in ((up, 0), (down, 12)):
            for j in range(ADV):
                y = first + j
                for p in range(10):
                    both = jnp.concatenate(
                        [tracer[pl.ds(g * 128 + y, 8, stride=16), :] for g in (2 * p, 2 * p + 1)],
                        axis=0,
                    )
                    dst[j * PR + 16 * p : j * PR + 16 * p + 16, :] = both.astype(BF16)
                r = rate8[pl.ds(y, 8, stride=16), :]
                dst[j * PR + 160 : j * PR + 176, :] = jnp.concatenate([r, r], axis=0).astype(BF16)


def pack_columns(comp, state, tracer, mass, rate8, left, right, turned):
    lane = lanes(8)

    @pl.when(comp[0] == 0)
    def _():
        for g in range(10):
            to_left = jnp.zeros((8, W), F32)
            to_right = jnp.zeros((8, W), F32)
            for y in range(32):
                v = jnp.broadcast_to(mass[y : y + 1, :], (8, W))
                if g < 9:
                    v = v * state[pl.ds(g * 256 + y, 8, stride=32), :]
                turned[80 * y + 8 * g : 80 * y + 8 * g + 8, :] = v
                v = pltpu.roll(v, y, 1)
                to_left = jnp.where(lane == y, v, to_left)
                to_right = jnp.where(lane == (y - 1) % W, v, to_right)
            left[8 * g : 8 * g + 8, :] = to_left
            right[8 * g : 8 * g + 8, :] = to_right

    @pl.when(comp[0] == 1)
    def _():
        for g in range(21):
            to_left = jnp.zeros((8, W), F32)
            to_right = jnp.zeros((8, W), F32)
            for y in range(16):
                i = y + ADV
                if g < 20:
                    v = tracer[pl.ds(g * 128 + y, 8, stride=16), :]
                    turned[160 * y + 8 * g : 160 * y + 8 * g + 8, :] = v
                else:
                    v = rate8[pl.ds(y, 8, stride=16), :]
                v = pltpu.roll(v, 4 * i, 1)
                to_left = jnp.where(lane // 4 == i, v, to_left)
                to_right = jnp.where(lane // 4 == i - 1, v, to_right)
            left[8 * g : 8 * g + 8, :] = to_left
            right[8 * g : 8 * g + 8, :] = to_right
        left[168:176, :] = jnp.zeros((8, W), F32)
        right[168:176, :] = jnp.zeros((8, W), F32)


def finish_columns(comp, raw_left, raw_right, above, below, left, right):
    lane = lanes(16)

    @pl.when(comp[0] == 0)
    def _():
        for p in range(5):
            rows = slice(16 * p, 16 * p + 16)
            low = slice(80 + 16 * p, 96 + 16 * p)
            up = above[rows, :].astype(F32) + above[low, :].astype(F32)
            down = below[rows, :].astype(F32) + below[low, :].astype(F32)
            down = pltpu.roll(down, 31, 1)
            for src, dst, at in ((raw_left, left, 0), (raw_right, right, 1)):
                v = src[rows, :]
                pos = (lane + at) % 4
                before = jnp.where(lane == (W - at) % W, up, pltpu.roll(v, 1, 1))
                after = jnp.where(lane == 31 - at, down, pltpu.roll(v, W - 1, 1))
                v = v + jnp.where(pos == 0, before, 0.0) + jnp.where(pos == 3, after, 0.0)
                hi, lo = split(v)
                dst[rows, :] = hi
                dst[low, :] = lo

    @pl.when(comp[0] == 1)
    def _():
        for p in range(11):
            rows = slice(16 * p, 16 * p + 16)
            to_left = raw_left[rows, :]
            to_right = raw_right[rows, :]
            for src, first in ((above, 0), (below, 20)):
                for j in range(ADV):
                    i = first + j
                    v = src[j * PR + 16 * p : j * PR + 16 * p + 16, :].astype(F32)
                    v = pltpu.roll(v, 4 * i, 1)
                    to_left = jnp.where(lane // 4 == i, v, to_left)
                    to_right = jnp.where(lane // 4 == (i - 1) % 32, v, to_right)
            left[rows, :] = to_left.astype(BF16)
            right[rows, :] = to_right.astype(BF16)


def swap_left(a, b):
    lane = lanes(a.shape[0])
    ra, rb = pltpu.roll(a, W - 1, 1), pltpu.roll(b, W - 1, 1)
    return jnp.where(lane == W - 1, rb, ra), jnp.where(lane == W - 1, ra, rb)


def swap_right(a, b):
    lane = lanes(a.shape[0])
    ra, rb = pltpu.roll(a, 1, 1), pltpu.roll(b, 1, 1)
    return jnp.where(lane == 0, rb, ra), jnp.where(lane == 0, ra, rb)


def halo_tile(from_right, from_left, i):
    lane = lanes(8)
    v = jnp.where(lane // 4 == i, from_right, from_left)
    v = pltpu.roll(v, (W - 4 * i) % W, 1)
    return jnp.where((lane < 4) | (lane >= W - 4), v, 0.0)


def extended(g, i, main, above, below, halo_l, halo_r):
    rows = slice(8 * g, 8 * g + 8)
    half = slice(8 * (g % 2), 8 * (g % 2) + 8)
    pair = 16 * (g // 2)

    def wide(ref, at):
        return ref[at : at + 16, :].astype(F32)[half]

    if i < ADV:
        a = wide(above, i * PR + pair)
    elif i >= EXT - ADV:
        a = wide(below, (i - EXT + ADV) * PR + pair)
    else:
        a = main(g, i - ADV)
    b = halo_tile(wide(halo_r, pair), wide(halo_l, pair), i)
    return a, b


RIGHTWARD = (2, 4, 7)
LEFTWARD = (0, 3, 5)


def prepare_rates(coef_a, coef_b, rate8, above, below, halo_l, halo_r):
    sub = lax.broadcasted_iota(jnp.int32, (8, W), 0)
    right = (sub == 2) | (sub == 4) | (sub == 7)
    left = (sub == 0) | (sub == 3) | (sub == 5)

    def main(g, y):
        return rate8[pl.ds(y, 8, stride=16), :]

    for i in range(EXT):
        a, b = extended(20, i, main, above, below, halo_l, halo_r)
        la, lb = swap_left(a, b)
        ra, rb = swap_right(a, b)
        coef_a[i * 16 : i * 16 + 8, :] = jnp.where(right, ra, jnp.where(left, la, a))
        coef_b[i * 16 : i * 16 + 8, :] = jnp.where(right, rb, jnp.where(left, lb, b))
        coef_a[i * 16 + 8 : i * 16 + 16, :] = jnp.broadcast_to(
            jnp.sum(a, axis=0, keepdims=True), (8, W)
        )
        coef_b[i * 16 + 8 : i * 16 + 16, :] = jnp.broadcast_to(
            jnp.sum(b, axis=0, keepdims=True), (8, W)
        )


def level_speeds(lev_speed, groups):
    sub = lax.broadcasted_iota(jnp.int32, (8, W), 0)
    speeds = []
    for g in groups:
        v = jnp.zeros((8, W), F32)
        for k in range(8):
            v = jnp.where(sub == k, lev_speed[(8 * g + k) % 80], v)
        speeds.append(v)
    return speeds


def fill(groups, ta, tb, main, above, below, halo_l, halo_r):
    wide = 8 * len(groups)
    for n, g in enumerate(groups):
        for part in range(3):
            span = range(8 * part, 8 * part + 8)
            pairs = [extended(g, i, main, above, below, halo_l, halo_r) for i in span]
            for i, (a, b) in zip(span, pairs):
                ta[i * wide + 8 * n : i * wide + 8 * n + 8, :] = a
                tb[i * wide + 8 * n : i * wide + 8 * n + 8, :] = b


def advect_cell(cells, coefs, speed):
    outs = []
    for (t0, t1, t2), c in zip(cells, coefs):
        to_r = c[2] * t0 + c[4] * t1 + c[7] * t2
        to_l = c[0] * t0 + c[3] * t1 + c[5] * t2
        mid = c[1] * t0 + c[6] * t2 - c[8] * t1
        outs.append((t1, to_r, to_l, mid))
    (a1, ar, al, am), (b1, br, bl, bm) = outs
    ua, ub = swap_left(ar, br)
    va, vb = swap_right(al, bl)
    return a1 + speed * (am + ua + va), b1 + speed * (bm + ub + vb)


def advect(pairs, coef_a, coef_b, speed, count, chunk, result):
    wide = count * 8

    def at(i, n):
        return pl.ds(pl.multiple_of(i * wide + 8 * n, 8), 8)

    for step in range(ADV):
        now, later = pairs[step % 2], pairs[(step + 1) % 2]
        last = step == ADV - 1

        def row(i, carry, now=now, later=later, last=last):
            def coef(ref, o):
                return jnp.broadcast_to(ref[pl.ds(i * 16 + o, 1), :], (8, W))

            coefs = [[coef(ref, o) for o in range(9)] for ref in (coef_a, coef_b)]
            for base in range(0, count, chunk):
                span = range(base, base + chunk)
                news = []
                for n in span:
                    cells = [[t[at(k, n), :] for k in (i - 1, i, i + 1)] for t in now]
                    news.append(advect_cell(cells, coefs, speed[8 * n : 8 * n + 8, :]))
                for n, (new_a, new_b) in zip(span, news):
                    if last:
                        place = pl.multiple_of((i - ADV) * wide + 8 * n, 8)
                        result[pl.ds(place, 8), :] = new_a
                    else:
                        later[0][at(i, n), :] = new_a
                        later[1][at(i, n), :] = new_b
            return carry

        lax.fori_loop(step + 1, EXT - 1 - step, row, 0)


def edge_sums(above, below, halo_l, halo_r, buf, edge, far_l, far_r, ready, emit):
    lane = lanes(8)
    for p in range(5):
        rows = slice(16 * p, 16 * p + 16)
        rest = slice(80 + 16 * p, 96 + 16 * p)
        v = halo_l[rows, :].astype(F32) + halo_l[rest, :].astype(F32)
        far_l[rows, :] = pltpu.roll(v, 2, 1)
        far_r[rows, :] = halo_r[rows, :].astype(F32) + halo_r[rest, :].astype(F32)
        v = above[rows, :].astype(F32) + above[rest, :].astype(F32)
        buf[16 * p : 16 * p + 16, :] = v
        v = below[rows, :].astype(F32) + below[rest, :].astype(F32)
        buf[2640 + 16 * p : 2656 + 16 * p, :] = v
    for g in range(10):
        rows = slice(8 * g, 8 * g + 8)
        from_l, from_r = far_l[rows, :], far_r[rows, :]
        for y in range(32):
            v = jnp.where(lane == y, from_r, from_l)
            at = 80 * y + 8 * g
            edge[at : at + 8, :] = pltpu.roll(v, (W - 1 - y) % W, 1)
    ready()

    def quad(q, carry):
        first = lane % 4 == 0
        final = lane % 4 == 3
        outer = (lane == 0) | (lane == W - 1)

        def at(row, g, wide=80):
            return pl.ds(pl.multiple_of(row * wide + 8 * g, 8), 8)

        for r in range(4):
            y = 4 * q + r
            values = []
            for g in (9, 0, 1, 2, 3, 4, 5, 6, 7, 8):
                v = buf[at(y + 1, g), :]
                if r == 0:
                    v = v + buf[at(y, g), :]
                if r == 3:
                    v = v + buf[at(y + 2, g), :]
                near = jnp.where(first, pltpu.roll(v, 1, 1), pltpu.roll(v, W - 1, 1))
                near = jnp.where(outer, edge[at(y, g), :], near)
                v = v + jnp.where(first | final, near, 0.0)
                if g == 9:
                    inverse = 1.0 / v
                else:
                    values.append(v * inverse)
            emit(y, values, at)
        return carry

    lax.fori_loop(0, 8, quad, 0)


def assemble(
    comp, lev_speed, turned, rate8, above, below, halo_l, halo_r, lhs,
    own, flux, top,
    buf, sem, edge, high, low, far_l, far_r, ta, tb, tc, td, coef_a, coef_b,
):
    @pl.when(comp[0] == 0)
    def _():
        def emit(y, values, at):
            hi, lo = split(jnp.concatenate(values + [jnp.zeros((8, W), F32)], axis=0))
            high[y] = hi
            low[y] = lo

        copy = pltpu.make_async_copy(turned, buf.at[pl.ds(80, 2560)], sem)
        copy.start()
        edge_sums(above, below, halo_l, halo_r, buf, edge, far_l, far_r, copy.wait, emit)
        for y in range(32):
            first = jnp.dot(lhs[...], high[y], preferred_element_type=F32)
            second = jnp.dot(lhs[0:32, :], low[y], preferred_element_type=F32)
            total = first[0:32] + first[32:64] + second
            flux[y] = total[0:16].astype(BF16)
            hi, lo = split(total[16:32])
            own[y, 0:16] = hi
            own[y, 16:32] = lo

    @pl.when(comp[0] == 1)
    def _():
        copy = pltpu.make_async_copy(turned, buf.at[pl.ds(80, 2560)], sem)
        copy.start()
        prepare_rates(coef_a, coef_b, rate8, above, below, halo_l, halo_r)
        copy.wait()

        def main(g, y):
            return buf[80 + 160 * y + 8 * g : 88 + 160 * y + 8 * g, :]

        sub = lax.broadcasted_iota(jnp.int32, (8, W), 0)
        for i in range(EXT):
            first = extended(0, i, main, above, below, halo_l, halo_r)
            second = extended(10, i, main, above, below, halo_l, halo_r)
            for ref, u, v in zip((ta, tb), first, second):
                ref[8 * i : 8 * i + 8, :] = jnp.where(sub == 0, u, pltpu.roll(v, 1, 0))
        pairs = ((ta, tb), (tc, td))
        speed = lev_speed[0]
        for step in range(ADV):
            now, later = pairs[step % 2], pairs[(step + 1) % 2]
            for i in range(step + 1, EXT - 1 - step):
                new_a, new_b = advect_cell(
                    [[t[8 * k : 8 * k + 8, :] for k in (i - 1, i, i + 1)] for t in now],
                    [
                        [
                            jnp.broadcast_to(ref[16 * i + o : 16 * i + o + 1, :], (8, W))
                            for o in range(9)
                        ]
                        for ref in (coef_a, coef_b)
                    ],
                    speed,
                )
                later[0][8 * i : 8 * i + 8, :] = new_a
                later[1][8 * i : 8 * i + 8, :] = new_b
        for v in range(2):
            rows = [ta[pl.ds((ADV + y) * 8 + v, 8, stride=8), :] for y in (0, 8)]
            top[v] = jnp.concatenate(rows, axis=0).astype(BF16)


def tile_products(
    comp, src, dest, dst, own, arrived, weights, top, send, count, meta, parts
):
    band = send.shape[0] // TILES_PER_PEER
    tiles = weights.shape[0]

    lane8 = lanes(8)
    sub8 = lax.broadcasted_iota(jnp.int32, (8, W), 0)

    def product(lhs, t):
        return lax.dot_general(
            lhs[src[0, t]], weights[t], (((1,), (1,)), ((), ())), preferred_element_type=F32
        )

    @pl.when(comp[0] == 0)
    def _():
        for t in range(tiles):
            both = product(own, t)
            parts[8 * t : 8 * t + 8, :] = both[0:8] + both[16:24]
        pieces = []
        for v in range(2):
            for p in range(4):
                rows = [parts[pl.ds(128 * p + 64 * q + v, 8, stride=8), :] for q in range(2)]
                pieces.append(jnp.concatenate(rows, axis=0).astype(BF16))
        ids = jnp.zeros((8, W), F32)
        for t in range(tiles):
            named = jnp.where(sub8 == 0, dest[0, t], dst[0, t]).astype(F32)
            ids = jnp.where(lane8 % tiles == t, named, ids)
        pieces.append(jnp.concatenate([ids, ids], axis=0).astype(BF16))

        def spread(h, carry):
            for j, piece in enumerate(pieces):
                send[h * TILES_PER_PEER + j] = piece
            return carry

        lax.fori_loop(0, band, spread, 0)

    @pl.when(comp[0] == 1)
    def _():
        def clear(h, carry):
            for j in range(TILES_PER_PEER):
                if j < 2:
                    send[h * TILES_PER_PEER + j] = top[j]
                else:
                    send[h * TILES_PER_PEER + j] = jnp.zeros((16, W), BF16)
            count[h] = 0
            meta[h] = jnp.full((8, W), -1.0, F32)
            return carry

        lax.fori_loop(0, band, clear, 0)
        for t in range(tiles):
            owner = dest[0, t]
            slot = count[owner]
            count[owner] = slot + 1
            place = slot + 2
            send[owner * TILES_PER_PEER + place] = product(arrived, t).astype(BF16)
            named = jnp.where(
                (lane8 // 16 == place) & (sub8 == 2), dst[0, t].astype(F32), meta[owner]
            )
            meta[owner] = named

        def finish(h, carry):
            m = meta[h]
            send[h * TILES_PER_PEER + 8] = jnp.concatenate([m, m], axis=0).astype(BF16)
            return carry

        lax.fori_loop(0, band, finish, 0)


def advect_all(
    comp, lev_speed, state, tracer, mass, rate8, above, below, halo_l, halo_r, after,
    result, dss, buf, edge, far_l, far_r, ta, tb, tc, td, coef_a, coef_b, speed,
):
    del after

    @pl.when(comp[0] == 0)
    def _():
        def emit(y, values, at):
            for g, v in enumerate(values):
                ta[at(y, g, 72), :] = v

        for y in range(32):
            m = jnp.broadcast_to(mass[y : y + 1, :], (8, W))
            for g in range(9):
                at = 80 + 80 * y + 8 * g
                buf[at : at + 8, :] = m * state[pl.ds(g * 256 + y, 8, stride=32), :]
            buf[152 + 80 * y : 160 + 80 * y, :] = m
        edge_sums(above, below, halo_l, halo_r, buf, edge, far_l, far_r, lambda: None, emit)
        for f in range(72):
            for p in range(4):
                dss[32 * f + 8 * p : 32 * f + 8 * p + 8, :] = ta[
                    pl.ds(72 * 8 * p + f, 8, stride=72), :
                ]

    @pl.when(comp[0] == 1)
    def _():
        dss[...] = jnp.zeros(dss.shape, F32)
        prepare_rates(coef_a, coef_b, rate8, above, below, halo_l, halo_r)

        def main(g, y):
            return tracer[pl.ds(g * 128 + y, 8, stride=16), :]

        groups = tuple(range(20))
        fill(groups, ta, tb, main, above, below, halo_l, halo_r)
        for n, v in enumerate(level_speeds(lev_speed, groups[:10])):
            speed[8 * n : 8 * n + 8, :] = v
            speed[80 + 8 * n : 88 + 8 * n, :] = v
        advect(((ta, tb), (tc, td)), coef_a, coef_b, speed, 20, 4, result)


def wanted(back_owner, back_src):
    sub8 = lax.broadcasted_iota(jnp.int32, (8, W), 0)
    wants = []
    for p in range(8):
        v = jnp.zeros((8, W), jnp.int32)
        for k in range(8):
            v = jnp.where(sub8 == k, back_owner[0, 8 * p + k] * 16 + back_src[0, 8 * p + k], v)
        wants.append(v)
    return jnp.concatenate(wants, axis=0).astype(F32)


def surface_select(comp, back_owner, back_src, received, out):
    band = received.shape[0] // TILES_PER_PEER

    @pl.when(comp[0] == 0)
    def _():
        lane = lanes(1)
        want = wanted(back_owner, back_src)

        def pair(q, carry):
            h = 2 * q
            ids = [received[(h + d) * TILES_PER_PEER + 8].astype(F32) for d in range(2)]
            named = [v[0:1, :] * 16.0 + v[1:2, :] for v in ids]
            row = jnp.where(lane < 64, named[0], named[1])
            hot = jnp.where(jnp.broadcast_to(row, (64, W)) == want, 1.0, 0.0).astype(BF16)
            totals = []
            for v in range(2):
                rhs = jnp.concatenate(
                    [
                        received[(h + d) * TILES_PER_PEER + 4 * v + j]
                        for d in range(2)
                        for j in range(4)
                    ],
                    axis=0,
                )
                totals.append(carry[v] + jnp.dot(hot, rhs, preferred_element_type=F32))
            return tuple(totals)

        zero = jnp.zeros((64, W), F32)
        sums = lax.fori_loop(0, band // 2, pair, (zero, zero), unroll=4)
        for v in range(2):
            out[64 * v : 64 * v + 64, :] = sums[v]


def finish(
    comp, back_owner, back_src, back_dst,
    advected, received, profile, weights, mine, other,
    ocean, surface, table, parts, acc,
):
    band = received.shape[0] // TILES_PER_PEER
    tiles = weights.shape[0]

    @pl.when(comp[0] == 0)
    def _():
        want = wanted(back_owner, back_src)
        sums = [mine[64 * v : 64 * v + 64, :] for v in range(2)]
        for c in range(band // 8):
            row = (lanes(64) + c * W).astype(F32)
            hot = jnp.where(row == want, 1.0, 0.0).astype(BF16)
            for v in range(2):
                rhs = jnp.concatenate([other[(8 * c + h) * 2 + v] for h in range(8)], axis=0)
                sums[v] = sums[v] + jnp.dot(hot, rhs, preferred_element_type=F32)
        for v in range(2):
            hi, lo = split(sums[v])
            for at, part in ((v, hi.astype(F32)), (2 + v, lo.astype(F32))):
                for p in range(8):
                    table[pl.ds(64 * p + at, 8, stride=8), :] = part[8 * p : 8 * p + 8]
        acc[...] = jnp.zeros(acc.shape, F32)
        for t in range(tiles):
            parts[8 * t : 8 * t + 8, :] = lax.dot_general(
                table[8 * t : 8 * t + 8, :].astype(BF16),
                weights[t],
                (((1,), (1,)), ((), ())),
                preferred_element_type=F32,
            )
        for t in range(tiles):
            at = pl.ds(pl.multiple_of(back_dst[0, t] * 8, 8), 8)
            acc[at, :] = acc[at, :] + parts[8 * t : 8 * t + 8, :]
        for v in range(2):
            for p in range(4):
                surface[32 * v + 8 * p : 32 * v + 8 * p + 8, :] = (
                    acc[pl.ds(64 * p + v, 8, stride=8), :]
                    + acc[pl.ds(64 * p + 2 + v, 8, stride=8), :]
                )
        ocean[...] = jnp.zeros(ocean.shape, F32)

    @pl.when(comp[0] == 1)
    def _():
        surface[...] = jnp.zeros(surface.shape, F32)
        row = lax.broadcasted_iota(jnp.int32, (256, W), 0)
        point = jnp.where(row % 16 == lanes(256) % 16, row // 16, -2).astype(F32)

        def add(h, total):
            named = received[h * TILES_PER_PEER + 8].astype(F32)[2:3, :]
            hot = jnp.where(jnp.broadcast_to(named, (256, W)) == point, 1.0, 0.0)
            rhs = jnp.concatenate(
                [received[h * TILES_PER_PEER + j] for j in range(8)], axis=0
            )
            return total + jnp.dot(hot.astype(BF16), rhs, preferred_element_type=F32)

        total = lax.fori_loop(0, band, add, jnp.zeros((256, W), F32), unroll=4)
        level_hi, level_lo = split(profile[...])
        for y in range(16):
            hi, lo = split(total[16 * y : 16 * y + 16, :])
            more = (
                jnp.dot(level_hi, hi, preferred_element_type=F32)
                + jnp.dot(level_hi, lo, preferred_element_type=F32)
                + jnp.dot(level_lo, hi, preferred_element_type=F32)
            )
            new = advected[160 * y : 160 * y + 160, :] + more
            for g in range(20):
                ocean[pl.ds(g * 128 + y, 8, stride=16), :] = new[8 * g : 8 * g + 8]


def shifted(array, axis, by):
    peers = lax.axis_size(axis)
    pairs = [(i, i + by) for i in range(peers) if 0 <= i + by < peers]
    return lax.ppermute(array, axis, pairs)


def shape(*dims, dtype=F32):
    return jax.ShapeDtypeStruct(dims, dtype)


def shards(
    atm_state,
    atm_mass,
    coupler,
    flux_dest,
    flux_dst_blk,
    flux_src_blk,
    conservative_flux_weights,
    ocn_tracers,
    ocean_neighbour_codes,
    ocn_rates,
    lev_speed,
    profile,
    back_owner,
    back_src_blk,
    back_dst_blk,
    return_remap_weights,
):
    comp = lax.axis_index("comp").astype(jnp.int32).reshape(1)
    band = lax.axis_size("gx")
    state = atm_state.reshape(72 * 32, W)
    tracer = ocn_tracers.reshape(2 * 80 * 16, W)
    codes = ocean_neighbour_codes.reshape(96, W)
    rates = ocn_rates.reshape(96, W)
    dma = pltpu.SemaphoreType.DMA
    buf = pltpu.VMEM((2560, W), F32)

    up, down, rate8 = call(
        pack_rows,
        [shape(4 * PR, W, dtype=BF16), shape(4 * PR, W, dtype=BF16), shape(128, W)],
        1, 5, 0,
        [
            buf, pltpu.VMEM((32, W), F32), pltpu.VMEM((96, W), jnp.int32),
            pltpu.VMEM((96, W), F32), dma((3,)),
        ],
        62,
    )(comp, state, tracer, atm_mass, codes, rates)
    below = shifted(up, "gy", -1)
    above = shifted(down, "gy", 1)
    raw_left, raw_right, turned = call(
        pack_columns, [shape(PR, W), shape(PR, W), shape(2560, W)], 1, 0, 4, []
    )(comp, state, tracer, atm_mass, rate8)
    left, right = call(
        finish_columns,
        [shape(PR, W, dtype=BF16), shape(PR, W, dtype=BF16)],
        1, 0, 4,
        [],
    )(comp, raw_left, raw_right, above, below)
    halo_r = shifted(left, "gx", -1)
    halo_l = shifted(right, "gx", 1)

    top_profile = jnp.dot(profile[:, 0], coupler, precision=lax.Precision.HIGHEST)
    lhs = jnp.pad(jnp.concatenate([coupler, top_profile], axis=0), ((0, 14), (0, 8)))
    lhs_hi, lhs_lo = split(lhs)
    lhs = jnp.concatenate([lhs_hi, lhs_lo], axis=0)
    small = pltpu.VMEM((EXT * 8, W), F32)

    coef = pltpu.VMEM((EXT * 16, W), F32)
    points = pltpu.VMEM((34 * 80, W), F32)
    rows = pltpu.VMEM((80, W), F32)
    own, flux, top = call(
        assemble,
        [
            shape(32, 32, W, dtype=BF16),
            shape(32, 16, W, dtype=BF16),
            shape(2, 16, W, dtype=BF16),
        ],
        2, 1, 6,
        [
            points, dma, buf,
            pltpu.VMEM((32, 80, W), BF16), pltpu.VMEM((32, 80, W), BF16), rows, rows,
            small, small, small, small, coef, coef,
        ],
    )(
        comp, lev_speed, turned, rate8, above, below, halo_l, halo_r, lhs,
    )
    arrived = shifted(flux, "comp", 1)
    send, = call(
        tile_products,
        [shape(band * TILES_PER_PEER, 16, W, dtype=BF16)],
        4, 0, 4,
        [
            pltpu.SMEM((band,), jnp.int32),
            pltpu.VMEM((band, 8, W), F32),
            pltpu.VMEM((512, W), F32),
        ],
    )(
        comp, flux_src_blk, flux_dest.reshape(1, 64), flux_dst_blk,
        own, arrived, conservative_flux_weights[0], top,
    )
    send, top = lax.optimization_barrier((send, top))
    received = lax.all_to_all(
        send.reshape(band, TILES_PER_PEER, 16, W), "gx", 0, 0, tiled=True
    ).reshape(band * TILES_PER_PEER, 16, W)
    grid = pltpu.VMEM((EXT * 160, W), F32)
    advected, dss = call(
        advect_all,
        [shape(16 * 160, W), shape(72 * 32, W)],
        2, 0, 9,
        [
            points, buf, rows, rows, grid, grid, grid, grid, coef, coef,
            pltpu.VMEM((160, W), F32),
        ],
    )(
        comp, lev_speed, state, tracer, atm_mass, rate8, above, below, halo_l, halo_r, top,
    )
    levels = profile.reshape(160, 16)
    received, advected, levels = lax.optimization_barrier((received, advected, levels))
    tops = received.reshape(band, TILES_PER_PEER, 16, W)[:, :2].reshape(2 * band, 16, W)
    other = shifted(tops, "comp", -1)
    mine, = call(surface_select, [shape(128, W)], 3, 0, 1, [])(
        comp, back_owner, back_src_blk, received
    )
    ocean, surface = call(finish, [shape(2560, W), shape(64, W)], 4, 0, 6, [
        pltpu.VMEM((512, W), F32), pltpu.VMEM((512, W), F32), pltpu.VMEM((256, W), F32),
    ])(
        comp, back_owner, back_src_blk, back_dst_blk,
        advected, received, levels, return_remap_weights[0], mine, other,
    )
    return (
        dss.reshape(1, 72, 32, W),
        surface.reshape(1, 2, 32, W),
        ocean.reshape(1, 2, 80, 16, W),
    )


def solution(mesh):
    placed = (
        P("comp", None, "gy", "gx"),
        P("gy", "gx"),
        P(),
        P("gy", "gx", None),
        P("gy", "gx"),
        P("gy", "gx"),
        P("gy", "gx", None, None),
        P("comp", None, None, "gy", "gx"),
        P(None, "gy", "gx"),
        P(None, "gy", "gx"),
        P(),
        P(),
        P("gy", "gx"),
        P("gy", "gx"),
        P("gy", "gx"),
        P("gy", "gx", None, None),
    )
    return jax.shard_map(
        shards,
        mesh=mesh,
        in_specs=placed,
        out_specs=(
            P("comp", None, "gy", "gx"),
            P("comp", None, "gy", "gx"),
            P("comp", None, None, "gy", "gx"),
        ),
        check_vma=False,
    )
```

```python
import functools

import jax
import jax.numpy as jnp
from jax import lax
from jax.experimental import pallas as pl
from jax.experimental.pallas import tpu as pltpu
from jax.sharding import PartitionSpec as P

F32 = jnp.float32
BF16 = jnp.bfloat16
ADV = 4
W = 128
PR = 176
EXT = 24
TILES_PER_PEER = 9
CHUNKS = 8


def lanes(rows):
    return lax.broadcasted_iota(jnp.int32, (rows, W), 1)


def in_hbm(array):
    return pltpu.with_memory_space_constraint(array, pltpu.HBM)


def in_pieces(src, dst, sem):
    size = src.shape[0] // CHUNKS
    spans = [pl.ds(size * n, size) for n in range(CHUNKS)]
    return [
        pltpu.make_async_copy(src.at[span], dst.at[span], sem.at[n])
        for n, span in enumerate(spans)
    ]


def split(value):
    hi = value.astype(BF16)
    return hi, (value - hi.astype(F32)).astype(BF16)


def call(body, out_shape, n_smem, n_any, n_vmem, scratch, mebibytes=16):
    specs = (
        [pl.BlockSpec(memory_space=pltpu.SMEM)] * n_smem
        + [pl.BlockSpec(memory_space=pl.ANY)] * n_any
        + [pl.BlockSpec(memory_space=pltpu.VMEM)] * n_vmem
    )
    return pl.pallas_call(
        body,
        out_shape=out_shape,
        in_specs=specs,
        out_specs=[pl.BlockSpec(memory_space=pltpu.VMEM)] * len(out_shape),
        scratch_shapes=scratch,
        compiler_params=pltpu.CompilerParams(vmem_limit_bytes=mebibytes * 1024 * 1024),
        name=body.__name__,
    )


def pack_rows(
    comp, state_ref, tracer_ref, mass_ref, codes_ref, rates_ref, up, down, rate8,
    buf, mass, codes, rates, sem,
):
    state = tracer = buf

    def pieces(ref, rows):
        spans = [pl.ds(rows // CHUNKS * n, rows // CHUNKS) for n in range(CHUNKS)]
        return [(ref.at[span], buf.at[span]) for span in spans]

    def fetch_all(*pairs):
        copies = [
            pltpu.make_async_copy(src, dst, sem.at[n]) for n, (src, dst) in enumerate(pairs)
        ]
        for copy in copies:
            copy.start()
        for copy in copies:
            copy.wait()

    @pl.when(comp[0] == 0)
    def _():
        fetch_all(*pieces(state_ref, 2304), (mass_ref, mass))
        for dst, y in ((up, 0), (down, 31)):
            m = jnp.broadcast_to(mass[y : y + 1, :], (8, W))
            parts = [state[pl.ds(g * 256 + y, 8, stride=32), :] * m for g in range(9)] + [m]
            for p in range(5):
                hi, lo = split(jnp.concatenate(parts[2 * p : 2 * p + 2], axis=0))
                dst[16 * p : 16 * p + 16, :] = hi
                dst[80 + 16 * p : 96 + 16 * p, :] = lo

    @pl.when(comp[0] == 1)
    def _():
        fetch_all(*pieces(tracer_ref, 2560), (codes_ref, codes), (rates_ref, rates))
        for o in range(8):
            acc = jnp.zeros((16, W), F32)
            for k in range(6):
                rows = slice(16 * k, 16 * k + 16)
                acc = acc + jnp.where(codes[rows, :] == o, rates[rows, :], 0.0)
            rate8[16 * o : 16 * o + 16, :] = acc
        for dst, first in ((up, 0), (down, 12)):
            for j in range(ADV):
                y = first + j
                for p in range(10):
                    both = jnp.concatenate(
                        [tracer[pl.ds(g * 128 + y, 8, stride=16), :] for g in (2 * p, 2 * p + 1)],
                        axis=0,
                    )
                    dst[j * PR + 16 * p : j * PR + 16 * p + 16, :] = both.astype(BF16)
                r = rate8[pl.ds(y, 8, stride=16), :]
                dst[j * PR + 160 : j * PR + 176, :] = jnp.concatenate([r, r], axis=0).astype(BF16)


def pack_columns(comp, state, tracer, mass, rate8, left, right, turned):
    lane = lanes(8)

    @pl.when(comp[0] == 0)
    def _():
        for g in range(10):
            to_left = jnp.zeros((8, W), F32)
            to_right = jnp.zeros((8, W), F32)
            for y in range(32):
                v = jnp.broadcast_to(mass[y : y + 1, :], (8, W))
                if g < 9:
                    v = v * state[pl.ds(g * 256 + y, 8, stride=32), :]
                turned[80 * y + 8 * g : 80 * y + 8 * g + 8, :] = v
                v = pltpu.roll(v, y, 1)
                to_left = jnp.where(lane == y, v, to_left)
                to_right = jnp.where(lane == (y - 1) % W, v, to_right)
            left[8 * g : 8 * g + 8, :] = to_left
            right[8 * g : 8 * g + 8, :] = to_right

    @pl.when(comp[0] == 1)
    def _():
        for g in range(21):
            to_left = jnp.zeros((8, W), F32)
            to_right = jnp.zeros((8, W), F32)
            for y in range(16):
                i = y + ADV
                if g < 20:
                    v = tracer[pl.ds(g * 128 + y, 8, stride=16), :]
                    turned[160 * y + 8 * g : 160 * y + 8 * g + 8, :] = v
                else:
                    v = rate8[pl.ds(y, 8, stride=16), :]
                v = pltpu.roll(v, 4 * i, 1)
                to_left = jnp.where(lane // 4 == i, v, to_left)
                to_right = jnp.where(lane // 4 == i - 1, v, to_right)
            left[8 * g : 8 * g + 8, :] = to_left
            right[8 * g : 8 * g + 8, :] = to_right
        left[168:176, :] = jnp.zeros((8, W), F32)
        right[168:176, :] = jnp.zeros((8, W), F32)


def finish_columns(comp, raw_left, raw_right, above, below, left, right):
    lane = lanes(16)

    @pl.when(comp[0] == 0)
    def _():
        for p in range(5):
            rows = slice(16 * p, 16 * p + 16)
            low = slice(80 + 16 * p, 96 + 16 * p)
            up = above[rows, :].astype(F32) + above[low, :].astype(F32)
            down = below[rows, :].astype(F32) + below[low, :].astype(F32)
            down = pltpu.roll(down, 31, 1)
            for src, dst, at in ((raw_left, left, 0), (raw_right, right, 1)):
                v = src[rows, :]
                pos = (lane + at) % 4
                before = jnp.where(lane == (W - at) % W, up, pltpu.roll(v, 1, 1))
                after = jnp.where(lane == 31 - at, down, pltpu.roll(v, W - 1, 1))
                v = v + jnp.where(pos == 0, before, 0.0) + jnp.where(pos == 3, after, 0.0)
                hi, lo = split(v)
                dst[rows, :] = hi
                dst[low, :] = lo

    @pl.when(comp[0] == 1)
    def _():
        for p in range(11):
            rows = slice(16 * p, 16 * p + 16)
            to_left = raw_left[rows, :]
            to_right = raw_right[rows, :]
            for src, first in ((above, 0), (below, 20)):
                for j in range(ADV):
                    i = first + j
                    v = src[j * PR + 16 * p : j * PR + 16 * p + 16, :].astype(F32)
                    v = pltpu.roll(v, 4 * i, 1)
                    to_left = jnp.where(lane // 4 == i, v, to_left)
                    to_right = jnp.where(lane // 4 == (i - 1) % 32, v, to_right)
            left[rows, :] = to_left.astype(BF16)
            right[rows, :] = to_right.astype(BF16)


def swap_left(a, b):
    lane = lanes(a.shape[0])
    ra, rb = pltpu.roll(a, W - 1, 1), pltpu.roll(b, W - 1, 1)
    return jnp.where(lane == W - 1, rb, ra), jnp.where(lane == W - 1, ra, rb)


def swap_right(a, b):
    lane = lanes(a.shape[0])
    ra, rb = pltpu.roll(a, 1, 1), pltpu.roll(b, 1, 1)
    return jnp.where(lane == 0, rb, ra), jnp.where(lane == 0, ra, rb)


def halo_tile(from_right, from_left, i):
    lane = lanes(8)
    v = jnp.where(lane // 4 == i, from_right, from_left)
    v = pltpu.roll(v, (W - 4 * i) % W, 1)
    return jnp.where((lane < 4) | (lane >= W - 4), v, 0.0)


def extended(g, i, main, above, below, halo_l, halo_r):
    rows = slice(8 * g, 8 * g + 8)
    half = slice(8 * (g % 2), 8 * (g % 2) + 8)
    pair = 16 * (g // 2)

    def wide(ref, at):
        return ref[at : at + 16, :].astype(F32)[half]

    if i < ADV:
        a = wide(above, i * PR + pair)
    elif i >= EXT - ADV:
        a = wide(below, (i - EXT + ADV) * PR + pair)
    else:
        a = main(g, i - ADV)
    b = halo_tile(wide(halo_r, pair), wide(halo_l, pair), i)
    return a, b


RIGHTWARD = (2, 4, 7)
LEFTWARD = (0, 3, 5)


def prepare_rates(coef_a, coef_b, rate8, above, below, halo_l, halo_r):
    sub = lax.broadcasted_iota(jnp.int32, (8, W), 0)
    right = (sub == 2) | (sub == 4) | (sub == 7)
    left = (sub == 0) | (sub == 3) | (sub == 5)

    def main(g, y):
        return rate8[pl.ds(y, 8, stride=16), :]

    for i in range(EXT):
        a, b = extended(20, i, main, above, below, halo_l, halo_r)
        la, lb = swap_left(a, b)
        ra, rb = swap_right(a, b)
        coef_a[i * 16 : i * 16 + 8, :] = jnp.where(right, ra, jnp.where(left, la, a))
        coef_b[i * 16 : i * 16 + 8, :] = jnp.where(right, rb, jnp.where(left, lb, b))
        coef_a[i * 16 + 8 : i * 16 + 16, :] = jnp.broadcast_to(
            jnp.sum(a, axis=0, keepdims=True), (8, W)
        )
        coef_b[i * 16 + 8 : i * 16 + 16, :] = jnp.broadcast_to(
            jnp.sum(b, axis=0, keepdims=True), (8, W)
        )


def level_speeds(lev_speed, groups):
    sub = lax.broadcasted_iota(jnp.int32, (8, W), 0)
    speeds = []
    for g in groups:
        v = jnp.zeros((8, W), F32)
        for k in range(8):
            v = jnp.where(sub == k, lev_speed[(8 * g + k) % 80], v)
        speeds.append(v)
    return speeds


def fill(groups, ta, tb, main, above, below, halo_l, halo_r):
    wide = 8 * len(groups)
    for n, g in enumerate(groups):
        for part in range(3):
            span = range(8 * part, 8 * part + 8)
            pairs = [extended(g, i, main, above, below, halo_l, halo_r) for i in span]
            for i, (a, b) in zip(span, pairs):
                ta[i * wide + 8 * n : i * wide + 8 * n + 8, :] = a
                tb[i * wide + 8 * n : i * wide + 8 * n + 8, :] = b


def advect_cell(cells, coefs, speed):
    outs = []
    for (t0, t1, t2), c in zip(cells, coefs):
        to_r = c[2] * t0 + c[4] * t1 + c[7] * t2
        to_l = c[0] * t0 + c[3] * t1 + c[5] * t2
        mid = c[1] * t0 + c[6] * t2 - c[8] * t1
        outs.append((t1, to_r, to_l, mid))
    (a1, ar, al, am), (b1, br, bl, bm) = outs
    ua, ub = swap_left(ar, br)
    va, vb = swap_right(al, bl)
    return a1 + speed * (am + ua + va), b1 + speed * (bm + ub + vb)


def advect(pairs, coef_a, coef_b, speed, count, chunk, result):
    wide = count * 8

    def at(i, n):
        return pl.ds(pl.multiple_of(i * wide + 8 * n, 8), 8)

    for step in range(ADV):
        now, later = pairs[step % 2], pairs[(step + 1) % 2]
        last = step == ADV - 1

        def row(i, carry, now=now, later=later, last=last):
            def coef(ref, o):
                return jnp.broadcast_to(ref[pl.ds(i * 16 + o, 1), :], (8, W))

            coefs = [[coef(ref, o) for o in range(9)] for ref in (coef_a, coef_b)]
            for base in range(0, count, chunk):
                span = range(base, base + chunk)
                news = []
                for n in span:
                    cells = [[t[at(k, n), :] for k in (i - 1, i, i + 1)] for t in now]
                    news.append(advect_cell(cells, coefs, speed[8 * n : 8 * n + 8, :]))
                for n, (new_a, new_b) in zip(span, news):
                    if last:
                        place = pl.multiple_of((i - ADV) * wide + 8 * n, 8)
                        result[pl.ds(place, 8), :] = new_a
                    else:
                        later[0][at(i, n), :] = new_a
                        later[1][at(i, n), :] = new_b
            return carry

        lax.fori_loop(step + 1, EXT - 1 - step, row, 0)


def edge_sums(above, below, halo_l, halo_r, buf, edge, far_l, far_r, ready, emit):
    lane = lanes(8)
    for p in range(5):
        rows = slice(16 * p, 16 * p + 16)
        rest = slice(80 + 16 * p, 96 + 16 * p)
        v = halo_l[rows, :].astype(F32) + halo_l[rest, :].astype(F32)
        far_l[rows, :] = pltpu.roll(v, 2, 1)
        far_r[rows, :] = halo_r[rows, :].astype(F32) + halo_r[rest, :].astype(F32)
        v = above[rows, :].astype(F32) + above[rest, :].astype(F32)
        buf[16 * p : 16 * p + 16, :] = v
        v = below[rows, :].astype(F32) + below[rest, :].astype(F32)
        buf[2640 + 16 * p : 2656 + 16 * p, :] = v
    for g in range(10):
        rows = slice(8 * g, 8 * g + 8)
        from_l, from_r = far_l[rows, :], far_r[rows, :]
        for y in range(32):
            v = jnp.where(lane == y, from_r, from_l)
            at = 80 * y + 8 * g
            edge[at : at + 8, :] = pltpu.roll(v, (W - 1 - y) % W, 1)
    ready()

    def quad(q, carry):
        first = lane % 4 == 0
        final = lane % 4 == 3
        outer = (lane == 0) | (lane == W - 1)

        def at(row, g, wide=80):
            return pl.ds(pl.multiple_of(row * wide + 8 * g, 8), 8)

        for r in range(4):
            y = 4 * q + r
            values = []
            for g in (9, 0, 1, 2, 3, 4, 5, 6, 7, 8):
                v = buf[at(y + 1, g), :]
                if r == 0:
                    v = v + buf[at(y, g), :]
                if r == 3:
                    v = v + buf[at(y + 2, g), :]
                near = jnp.where(first, pltpu.roll(v, 1, 1), pltpu.roll(v, W - 1, 1))
                near = jnp.where(outer, edge[at(y, g), :], near)
                v = v + jnp.where(first | final, near, 0.0)
                if g == 9:
                    inverse = 1.0 / v
                else:
                    values.append(v * inverse)
            emit(y, values, at)
        return carry

    lax.fori_loop(0, 8, quad, 0)


def assemble(
    comp, lev_speed, turned, rate8, above, below, halo_l, halo_r, lhs,
    own, flux, top,
    buf, sem, edge, high, low, far_l, far_r, ta, tb, tc, td, coef_a, coef_b,
):
    @pl.when(comp[0] == 0)
    def _():
        def emit(y, values, at):
            hi, lo = split(jnp.concatenate(values + [jnp.zeros((8, W), F32)], axis=0))
            high[y] = hi
            low[y] = lo

        copy = pltpu.make_async_copy(turned, buf.at[pl.ds(80, 2560)], sem)
        copy.start()
        edge_sums(above, below, halo_l, halo_r, buf, edge, far_l, far_r, copy.wait, emit)
        for y in range(32):
            first = jnp.dot(lhs[...], high[y], preferred_element_type=F32)
            second = jnp.dot(lhs[0:32, :], low[y], preferred_element_type=F32)
            total = first[0:32] + first[32:64] + second
            flux[y] = total[0:16].astype(BF16)
            hi, lo = split(total[16:32])
            own[y, 0:16] = hi
            own[y, 16:32] = lo

    @pl.when(comp[0] == 1)
    def _():
        copy = pltpu.make_async_copy(turned, buf.at[pl.ds(80, 2560)], sem)
        copy.start()
        prepare_rates(coef_a, coef_b, rate8, above, below, halo_l, halo_r)
        copy.wait()

        def main(g, y):
            return buf[80 + 160 * y + 8 * g : 88 + 160 * y + 8 * g, :]

        sub = lax.broadcasted_iota(jnp.int32, (8, W), 0)
        for i in range(EXT):
            first = extended(0, i, main, above, below, halo_l, halo_r)
            second = extended(10, i, main, above, below, halo_l, halo_r)
            for ref, u, v in zip((ta, tb), first, second):
                ref[8 * i : 8 * i + 8, :] = jnp.where(sub == 0, u, pltpu.roll(v, 1, 0))
        pairs = ((ta, tb), (tc, td))
        speed = lev_speed[0]
        for step in range(ADV):
            now, later = pairs[step % 2], pairs[(step + 1) % 2]
            for i in range(step + 1, EXT - 1 - step):
                new_a, new_b = advect_cell(
                    [[t[8 * k : 8 * k + 8, :] for k in (i - 1, i, i + 1)] for t in now],
                    [
                        [
                            jnp.broadcast_to(ref[16 * i + o : 16 * i + o + 1, :], (8, W))
                            for o in range(9)
                        ]
                        for ref in (coef_a, coef_b)
                    ],
                    speed,
                )
                later[0][8 * i : 8 * i + 8, :] = new_a
                later[1][8 * i : 8 * i + 8, :] = new_b
        for v in range(2):
            rows = [ta[pl.ds((ADV + y) * 8 + v, 8, stride=8), :] for y in (0, 8)]
            top[v] = jnp.concatenate(rows, axis=0).astype(BF16)


def tile_products(
    comp, src, dest, dst, own, arrived, weights, top, send, count, meta, parts
):
    band = send.shape[0] // TILES_PER_PEER
    tiles = weights.shape[0]

    lane8 = lanes(8)
    sub8 = lax.broadcasted_iota(jnp.int32, (8, W), 0)

    def product(lhs, t):
        return lax.dot_general(
            lhs[src[0, t]], weights[t], (((1,), (1,)), ((), ())), preferred_element_type=F32
        )

    @pl.when(comp[0] == 0)
    def _():
        for t in range(tiles):
            both = product(own, t)
            parts[8 * t : 8 * t + 8, :] = both[0:8] + both[16:24]
        pieces = []
        for v in range(2):
            for p in range(4):
                rows = [parts[pl.ds(128 * p + 64 * q + v, 8, stride=8), :] for q in range(2)]
                pieces.append(jnp.concatenate(rows, axis=0).astype(BF16))
        ids = jnp.zeros((8, W), F32)
        for t in range(tiles):
            named = jnp.where(sub8 == 0, dest[0, t], dst[0, t]).astype(F32)
            ids = jnp.where(lane8 % tiles == t, named, ids)
        pieces.append(jnp.concatenate([ids, ids], axis=0).astype(BF16))

        def spread(h, carry):
            for j, piece in enumerate(pieces):
                send[h * TILES_PER_PEER + j] = piece
            return carry

        lax.fori_loop(0, band, spread, 0)

    @pl.when(comp[0] == 1)
    def _():
        def clear(h, carry):
            for j in range(TILES_PER_PEER):
                if j < 2:
                    send[h * TILES_PER_PEER + j] = top[j]
                else:
                    send[h * TILES_PER_PEER + j] = jnp.zeros((16, W), BF16)
            count[h] = 0
            meta[h] = jnp.full((8, W), -1.0, F32)
            return carry

        lax.fori_loop(0, band, clear, 0)
        for t in range(tiles):
            owner = dest[0, t]
            slot = count[owner]
            count[owner] = slot + 1
            place = slot + 2
            send[owner * TILES_PER_PEER + place] = product(arrived, t).astype(BF16)
            named = jnp.where(
                (lane8 // 16 == place) & (sub8 == 2), dst[0, t].astype(F32), meta[owner]
            )
            meta[owner] = named

        def finish(h, carry):
            m = meta[h]
            send[h * TILES_PER_PEER + 8] = jnp.concatenate([m, m], axis=0).astype(BF16)
            return carry

        lax.fori_loop(0, band, finish, 0)


def advect_all(
    comp, lev_speed, state, tracer, mass, rate8, above, below, halo_l, halo_r, after,
    result, dss, buf, edge, far_l, far_r, ta, tb, tc, td, coef_a, coef_b, speed,
):
    del after

    @pl.when(comp[0] == 0)
    def _():
        def emit(y, values, at):
            for g, v in enumerate(values):
                ta[at(y, g, 72), :] = v

        for y in range(32):
            m = jnp.broadcast_to(mass[y : y + 1, :], (8, W))
            for g in range(9):
                at = 80 + 80 * y + 8 * g
                buf[at : at + 8, :] = m * state[pl.ds(g * 256 + y, 8, stride=32), :]
            buf[152 + 80 * y : 160 + 80 * y, :] = m
        edge_sums(above, below, halo_l, halo_r, buf, edge, far_l, far_r, lambda: None, emit)
        for f in range(72):
            for p in range(4):
                dss[32 * f + 8 * p : 32 * f + 8 * p + 8, :] = ta[
                    pl.ds(72 * 8 * p + f, 8, stride=72), :
                ]

    @pl.when(comp[0] == 1)
    def _():
        dss[...] = jnp.zeros(dss.shape, F32)
        prepare_rates(coef_a, coef_b, rate8, above, below, halo_l, halo_r)

        def main(g, y):
            return tracer[pl.ds(g * 128 + y, 8, stride=16), :]

        groups = tuple(range(20))
        fill(groups, ta, tb, main, above, below, halo_l, halo_r)
        for n, v in enumerate(level_speeds(lev_speed, groups[:10])):
            speed[8 * n : 8 * n + 8, :] = v
            speed[80 + 8 * n : 88 + 8 * n, :] = v
        advect(((ta, tb), (tc, td)), coef_a, coef_b, speed, 20, 4, result)


def wanted(back_owner, back_src):
    sub8 = lax.broadcasted_iota(jnp.int32, (8, W), 0)
    wants = []
    for p in range(8):
        v = jnp.zeros((8, W), jnp.int32)
        for k in range(8):
            v = jnp.where(sub8 == k, back_owner[0, 8 * p + k] * 16 + back_src[0, 8 * p + k], v)
        wants.append(v)
    return jnp.concatenate(wants, axis=0).astype(F32)


def select_or_force(
    comp, back_owner, back_src, received_ref, advected_ref, profile, out, ocean,
    received, advected, sem, sem2,
):
    band = received.shape[0] // TILES_PER_PEER
    arrivals = in_pieces(received_ref, received, sem)
    for copy in arrivals:
        copy.start()

    @pl.when(comp[0] == 0)
    def _():
        lane = lanes(1)
        want = wanted(back_owner, back_src)

        def pair(q, carry):
            h = 2 * q
            ids = [received[(h + d) * TILES_PER_PEER + 8].astype(F32) for d in range(2)]
            named = [v[0:1, :] * 16.0 + v[1:2, :] for v in ids]
            row = jnp.where(lane < 64, named[0], named[1])
            hot = jnp.where(jnp.broadcast_to(row, (64, W)) == want, 1.0, 0.0).astype(BF16)
            totals = []
            for v in range(2):
                rhs = jnp.concatenate(
                    [
                        received[(h + d) * TILES_PER_PEER + 4 * v + j]
                        for d in range(2)
                        for j in range(4)
                    ],
                    axis=0,
                )
                totals.append(carry[v] + jnp.dot(hot, rhs, preferred_element_type=F32))
            return tuple(totals)

        zero = jnp.zeros((64, W), F32)
        sums = (zero, zero)
        for n, copy in enumerate(arrivals):
            copy.wait()
            for q in range(n * band // (2 * CHUNKS), (n + 1) * band // (2 * CHUNKS)):
                sums = pair(q, sums)
        for v in range(2):
            out[64 * v : 64 * v + 64, :] = sums[v]
        ocean[...] = jnp.zeros(ocean.shape, F32)

    @pl.when(comp[0] == 1)
    def _():
        others = in_pieces(advected_ref, advected, sem2)
        for copy in others:
            copy.start()
        row = lax.broadcasted_iota(jnp.int32, (256, W), 0)
        point = jnp.where(row % 16 == lanes(256) % 16, row // 16, -2).astype(F32)

        def add(h, total):
            named = received[h * TILES_PER_PEER + 8].astype(F32)[2:3, :]
            hot = jnp.where(jnp.broadcast_to(named, (256, W)) == point, 1.0, 0.0)
            rhs = jnp.concatenate(
                [received[h * TILES_PER_PEER + j] for j in range(8)], axis=0
            )
            return total + jnp.dot(hot.astype(BF16), rhs, preferred_element_type=F32)

        total = jnp.zeros((256, W), F32)
        for n, copy in enumerate(arrivals):
            copy.wait()
            for h in range(n * band // CHUNKS, (n + 1) * band // CHUNKS):
                total = add(h, total)
        level_hi, level_lo = split(profile[...])
        for y in range(16):
            if y % 2 == 0:
                others[y // 2].wait()
            hi, lo = split(total[16 * y : 16 * y + 16, :])
            more = (
                jnp.dot(level_hi, hi, preferred_element_type=F32)
                + jnp.dot(level_hi, lo, preferred_element_type=F32)
                + jnp.dot(level_lo, hi, preferred_element_type=F32)
            )
            new = advected[160 * y : 160 * y + 160, :] + more
            for g in range(20):
                ocean[pl.ds(g * 128 + y, 8, stride=16), :] = new[8 * g : 8 * g + 8]


def finish(
    comp, back_owner, back_src, back_dst, weights_ref, mine, other,
    surface, weights, sem, table, parts, acc,
):
    band = other.shape[0] // 2
    tiles = weights.shape[0]

    @pl.when(comp[0] == 0)
    def _():
        chunk = tiles // CHUNKS
        copies = in_pieces(weights_ref, weights, sem)
        for copy in copies:
            copy.start()
        want = wanted(back_owner, back_src)
        sums = [mine[64 * v : 64 * v + 64, :] for v in range(2)]
        for c in range(band // 8):
            row = (lanes(64) + c * W).astype(F32)
            hot = jnp.where(row == want, 1.0, 0.0).astype(BF16)
            for v in range(2):
                rhs = jnp.concatenate([other[(8 * c + h) * 2 + v] for h in range(8)], axis=0)
                sums[v] = sums[v] + jnp.dot(hot, rhs, preferred_element_type=F32)
        for v in range(2):
            hi, lo = split(sums[v])
            for at, part in ((v, hi.astype(F32)), (2 + v, lo.astype(F32))):
                for p in range(8):
                    table[pl.ds(64 * p + at, 8, stride=8), :] = part[8 * p : 8 * p + 8]
        acc[...] = jnp.zeros(acc.shape, F32)
        for t in range(tiles):
            if t % chunk == 0:
                copies[t // chunk].wait()
            parts[8 * t : 8 * t + 8, :] = lax.dot_general(
                table[8 * t : 8 * t + 8, :].astype(BF16),
                weights[t],
                (((1,), (1,)), ((), ())),
                preferred_element_type=F32,
            )
        for t in range(tiles):
            at = pl.ds(pl.multiple_of(back_dst[0, t] * 8, 8), 8)
            acc[at, :] = acc[at, :] + parts[8 * t : 8 * t + 8, :]
        for v in range(2):
            for p in range(4):
                surface[32 * v + 8 * p : 32 * v + 8 * p + 8, :] = (
                    acc[pl.ds(64 * p + v, 8, stride=8), :]
                    + acc[pl.ds(64 * p + 2 + v, 8, stride=8), :]
                )

    @pl.when(comp[0] == 1)
    def _():
        surface[...] = jnp.zeros(surface.shape, F32)


def shifted(array, axis, by):
    peers = lax.axis_size(axis)
    pairs = [(i, i + by) for i in range(peers) if 0 <= i + by < peers]
    return lax.ppermute(array, axis, pairs)


def shape(*dims, dtype=F32):
    return jax.ShapeDtypeStruct(dims, dtype)


def shards(
    atm_state,
    atm_mass,
    coupler,
    flux_dest,
    flux_dst_blk,
    flux_src_blk,
    conservative_flux_weights,
    ocn_tracers,
    ocean_neighbour_codes,
    ocn_rates,
    lev_speed,
    profile,
    back_owner,
    back_src_blk,
    back_dst_blk,
    return_remap_weights,
):
    comp = lax.axis_index("comp").astype(jnp.int32).reshape(1)
    band = lax.axis_size("gx")
    state = atm_state.reshape(72 * 32, W)
    tracer = ocn_tracers.reshape(2 * 80 * 16, W)
    codes = ocean_neighbour_codes.reshape(96, W)
    rates = ocn_rates.reshape(96, W)
    dma = pltpu.SemaphoreType.DMA
    buf = pltpu.VMEM((2560, W), F32)

    up, down, rate8 = call(
        pack_rows,
        [shape(4 * PR, W, dtype=BF16), shape(4 * PR, W, dtype=BF16), shape(128, W)],
        1, 5, 0,
        [
            buf, pltpu.VMEM((32, W), F32), pltpu.VMEM((96, W), jnp.int32),
            pltpu.VMEM((96, W), F32), dma((CHUNKS + 2,)),
        ],
        62,
    )(comp, state, tracer, atm_mass, codes, rates)
    below = shifted(up, "gy", -1)
    above = shifted(down, "gy", 1)
    raw_left, raw_right, turned = call(
        pack_columns, [shape(PR, W), shape(PR, W), shape(2560, W)], 1, 0, 4, []
    )(comp, state, tracer, atm_mass, rate8)
    left, right = call(
        finish_columns,
        [shape(PR, W, dtype=BF16), shape(PR, W, dtype=BF16)],
        1, 0, 4,
        [],
    )(comp, raw_left, raw_right, above, below)
    halo_r = shifted(left, "gx", -1)
    halo_l = shifted(right, "gx", 1)

    top_profile = jnp.dot(profile[:, 0], coupler, precision=lax.Precision.HIGHEST)
    lhs = jnp.pad(jnp.concatenate([coupler, top_profile], axis=0), ((0, 14), (0, 8)))
    lhs_hi, lhs_lo = split(lhs)
    lhs = jnp.concatenate([lhs_hi, lhs_lo], axis=0)
    small = pltpu.VMEM((EXT * 8, W), F32)

    coef = pltpu.VMEM((EXT * 16, W), F32)
    points = pltpu.VMEM((34 * 80, W), F32)
    rows = pltpu.VMEM((80, W), F32)
    own, flux, top = call(
        assemble,
        [
            shape(32, 32, W, dtype=BF16),
            shape(32, 16, W, dtype=BF16),
            shape(2, 16, W, dtype=BF16),
        ],
        2, 1, 6,
        [
            points, dma, buf,
            pltpu.VMEM((32, 80, W), BF16), pltpu.VMEM((32, 80, W), BF16), rows, rows,
            small, small, small, small, coef, coef,
        ],
    )(
        comp, lev_speed, turned, rate8, above, below, halo_l, halo_r, lhs,
    )
    arrived = shifted(flux, "comp", 1)
    send, = call(
        tile_products,
        [shape(band * TILES_PER_PEER, 16, W, dtype=BF16)],
        4, 0, 4,
        [
            pltpu.SMEM((band,), jnp.int32),
            pltpu.VMEM((band, 8, W), F32),
            pltpu.VMEM((512, W), F32),
        ],
    )(
        comp, flux_src_blk, flux_dest.reshape(1, 64), flux_dst_blk,
        own, arrived, conservative_flux_weights[0], top,
    )
    send, top = lax.optimization_barrier((send, top))
    received = lax.all_to_all(
        send.reshape(band, TILES_PER_PEER, 16, W), "gx", 0, 0, tiled=True
    ).reshape(band * TILES_PER_PEER, 16, W)
    grid = pltpu.VMEM((EXT * 160, W), F32)
    advected, dss = call(
        advect_all,
        [shape(16 * 160, W), shape(72 * 32, W)],
        2, 0, 9,
        [
            points, buf, rows, rows, grid, grid, grid, grid, coef, coef,
            pltpu.VMEM((160, W), F32),
        ],
    )(
        comp, lev_speed, state, tracer, atm_mass, rate8, above, below, halo_l, halo_r, top,
    )
    levels = profile.reshape(160, 16)
    received, advected, levels = lax.optimization_barrier((received, advected, levels))
    tops = received.reshape(band, TILES_PER_PEER, 16, W)[:, :2].reshape(2 * band, 16, W)
    other = shifted(tops, "comp", -1)
    mine, ocean = call(select_or_force, [shape(128, W), shape(2560, W)], 3, 2, 1, [
        pltpu.VMEM((band * TILES_PER_PEER, 16, W), BF16), buf,
        dma((CHUNKS,)), dma((CHUNKS,)),
    ])(
        comp, back_owner, back_src_blk, in_hbm(received), in_hbm(advected), levels
    )
    surface, = call(finish, [shape(64, W)], 4, 1, 2, [
        pltpu.VMEM(return_remap_weights.shape[1:], BF16), dma((CHUNKS,)),
        pltpu.VMEM((512, W), F32), pltpu.VMEM((512, W), F32), pltpu.VMEM((256, W), F32),
    ])(
        comp, back_owner, back_src_blk, back_dst_blk, in_hbm(return_remap_weights[0]), mine, other,
    )
    return (
        dss.reshape(1, 72, 32, W),
        surface.reshape(1, 2, 32, W),
        ocean.reshape(1, 2, 80, 16, W),
    )


def solution(mesh):
    placed = (
        P("comp", None, "gy", "gx"),
        P("gy", "gx"),
        P(),
        P("gy", "gx", None),
        P("gy", "gx"),
        P("gy", "gx"),
        P("gy", "gx", None, None),
        P("comp", None, None, "gy", "gx"),
        P(None, "gy", "gx"),
        P(None, "gy", "gx"),
        P(),
        P(),
        P("gy", "gx"),
        P("gy", "gx"),
        P("gy", "gx"),
        P("gy", "gx", None, None),
    )
    return jax.shard_map(
        shards,
        mesh=mesh,
        in_specs=placed,
        out_specs=(
            P("comp", None, "gy", "gx"),
            P("comp", None, "gy", "gx"),
            P("comp", None, None, "gy", "gx"),
        ),
        check_vma=False,
    )
```

```python
import functools

import jax
import jax.numpy as jnp
from jax import lax
from jax.experimental import pallas as pl
from jax.experimental.pallas import tpu as pltpu
from jax.sharding import PartitionSpec as P

F32 = jnp.float32
BF16 = jnp.bfloat16
ADV = 4
W = 128
PR = 176
EXT = 24
TILES_PER_PEER = 9


def lanes(rows):
    return lax.broadcasted_iota(jnp.int32, (rows, W), 1)


def split(value):
    hi = value.astype(BF16)
    return hi, (value - hi.astype(F32)).astype(BF16)


def call(body, out_shape, n_smem, n_any, n_vmem, scratch, mebibytes=16):
    specs = (
        [pl.BlockSpec(memory_space=pltpu.SMEM)] * n_smem
        + [pl.BlockSpec(memory_space=pl.ANY)] * n_any
        + [pl.BlockSpec(memory_space=pltpu.VMEM)] * n_vmem
    )
    return pl.pallas_call(
        body,
        out_shape=out_shape,
        in_specs=specs,
        out_specs=[pl.BlockSpec(memory_space=pltpu.VMEM)] * len(out_shape),
        scratch_shapes=scratch,
        compiler_params=pltpu.CompilerParams(vmem_limit_bytes=mebibytes * 1024 * 1024),
        name=body.__name__,
    )


def pack_rows(
    comp, state_ref, tracer_ref, mass_ref, codes_ref, rates_ref, up, down, rate8,
    buf, mass, codes, rates, sem,
):
    state = tracer = buf

    def fetch_all(*pairs):
        copies = [
            pltpu.make_async_copy(src, dst, sem.at[n]) for n, (src, dst) in enumerate(pairs)
        ]
        for copy in copies:
            copy.start()
        for copy in copies:
            copy.wait()

    @pl.when(comp[0] == 0)
    def _():
        fetch_all((state_ref, buf.at[pl.ds(0, 2304)]), (mass_ref, mass))
        for dst, y in ((up, 0), (down, 31)):
            m = jnp.broadcast_to(mass[y : y + 1, :], (8, W))
            parts = [state[pl.ds(g * 256 + y, 8, stride=32), :] * m for g in range(9)] + [m]
            for p in range(5):
                hi, lo = split(jnp.concatenate(parts[2 * p : 2 * p + 2], axis=0))
                dst[16 * p : 16 * p + 16, :] = hi
                dst[80 + 16 * p : 96 + 16 * p, :] = lo

    @pl.when(comp[0] == 1)
    def _():
        fetch_all((tracer_ref, buf), (codes_ref, codes), (rates_ref, rates))
        for o in range(8):
            acc = jnp.zeros((16, W), F32)
            for k in range(6):
                rows = slice(16 * k, 16 * k + 16)
                acc = acc + jnp.where(codes[rows, :] == o, rates[rows, :], 0.0)
            rate8[16 * o : 16 * o + 16, :] = acc
        for dst, first in ((up, 0), (down, 12)):
            for j in range(ADV):
                y = first + j
                for p in range(10):
                    both = jnp.concatenate(
                        [tracer[pl.ds(g * 128 + y, 8, stride=16), :] for g in (2 * p, 2 * p + 1)],
                        axis=0,
                    )
                    dst[j * PR + 16 * p : j * PR + 16 * p + 16, :] = both.astype(BF16)
                r = rate8[pl.ds(y, 8, stride=16), :]
                dst[j * PR + 160 : j * PR + 176, :] = jnp.concatenate([r, r], axis=0).astype(BF16)


def pack_columns(comp, state, tracer, mass, rate8, left, right, turned):
    lane = lanes(8)

    @pl.when(comp[0] == 0)
    def _():
        for g in range(10):
            to_left = jnp.zeros((8, W), F32)
            to_right = jnp.zeros((8, W), F32)
            for y in range(32):
                v = jnp.broadcast_to(mass[y : y + 1, :], (8, W))
                if g < 9:
                    v = v * state[pl.ds(g * 256 + y, 8, stride=32), :]
                turned[80 * y + 8 * g : 80 * y + 8 * g + 8, :] = v
                v = pltpu.roll(v, y, 1)
                to_left = jnp.where(lane == y, v, to_left)
                to_right = jnp.where(lane == (y - 1) % W, v, to_right)
            left[8 * g : 8 * g + 8, :] = to_left
            right[8 * g : 8 * g + 8, :] = to_right

    @pl.when(comp[0] == 1)
    def _():
        for g in range(21):
            to_left = jnp.zeros((8, W), F32)
            to_right = jnp.zeros((8, W), F32)
            for y in range(16):
                i = y + ADV
                if g < 20:
                    v = tracer[pl.ds(g * 128 + y, 8, stride=16), :]
                    turned[160 * y + 8 * g : 160 * y + 8 * g + 8, :] = v
                else:
                    v = rate8[pl.ds(y, 8, stride=16), :]
                v = pltpu.roll(v, 4 * i, 1)
                to_left = jnp.where(lane // 4 == i, v, to_left)
                to_right = jnp.where(lane // 4 == i - 1, v, to_right)
            left[8 * g : 8 * g + 8, :] = to_left
            right[8 * g : 8 * g + 8, :] = to_right
        left[168:176, :] = jnp.zeros((8, W), F32)
        right[168:176, :] = jnp.zeros((8, W), F32)


def finish_columns(comp, raw_left, raw_right, above, below, left, right):
    lane = lanes(16)

    @pl.when(comp[0] == 0)
    def _():
        for p in range(5):
            rows = slice(16 * p, 16 * p + 16)
            low = slice(80 + 16 * p, 96 + 16 * p)
            up = above[rows, :].astype(F32) + above[low, :].astype(F32)
            down = below[rows, :].astype(F32) + below[low, :].astype(F32)
            down = pltpu.roll(down, 31, 1)
            for src, dst, at in ((raw_left, left, 0), (raw_right, right, 1)):
                v = src[rows, :]
                pos = (lane + at) % 4
                before = jnp.where(lane == (W - at) % W, up, pltpu.roll(v, 1, 1))
                after = jnp.where(lane == 31 - at, down, pltpu.roll(v, W - 1, 1))
                v = v + jnp.where(pos == 0, before, 0.0) + jnp.where(pos == 3, after, 0.0)
                hi, lo = split(v)
                dst[rows, :] = hi
                dst[low, :] = lo

    @pl.when(comp[0] == 1)
    def _():
        for p in range(11):
            rows = slice(16 * p, 16 * p + 16)
            to_left = raw_left[rows, :]
            to_right = raw_right[rows, :]
            for src, first in ((above, 0), (below, 20)):
                for j in range(ADV):
                    i = first + j
                    v = src[j * PR + 16 * p : j * PR + 16 * p + 16, :].astype(F32)
                    v = pltpu.roll(v, 4 * i, 1)
                    to_left = jnp.where(lane // 4 == i, v, to_left)
                    to_right = jnp.where(lane // 4 == (i - 1) % 32, v, to_right)
            left[rows, :] = to_left.astype(BF16)
            right[rows, :] = to_right.astype(BF16)


def swap_left(a, b):
    lane = lanes(a.shape[0])
    ra, rb = pltpu.roll(a, W - 1, 1), pltpu.roll(b, W - 1, 1)
    return jnp.where(lane == W - 1, rb, ra), jnp.where(lane == W - 1, ra, rb)


def swap_right(a, b):
    lane = lanes(a.shape[0])
    ra, rb = pltpu.roll(a, 1, 1), pltpu.roll(b, 1, 1)
    return jnp.where(lane == 0, rb, ra), jnp.where(lane == 0, ra, rb)


def halo_tile(from_right, from_left, i):
    lane = lanes(8)
    v = jnp.where(lane // 4 == i, from_right, from_left)
    v = pltpu.roll(v, (W - 4 * i) % W, 1)
    return jnp.where((lane < 4) | (lane >= W - 4), v, 0.0)


def extended(g, i, main, above, below, halo_l, halo_r):
    rows = slice(8 * g, 8 * g + 8)
    half = slice(8 * (g % 2), 8 * (g % 2) + 8)
    pair = 16 * (g // 2)

    def wide(ref, at):
        return ref[at : at + 16, :].astype(F32)[half]

    if i < ADV:
        a = wide(above, i * PR + pair)
    elif i >= EXT - ADV:
        a = wide(below, (i - EXT + ADV) * PR + pair)
    else:
        a = main(g, i - ADV)
    b = halo_tile(wide(halo_r, pair), wide(halo_l, pair), i)
    return a, b


RIGHTWARD = (2, 4, 7)
LEFTWARD = (0, 3, 5)


def prepare_rates(coef_a, coef_b, rate8, above, below, halo_l, halo_r):
    sub = lax.broadcasted_iota(jnp.int32, (8, W), 0)
    right = (sub == 2) | (sub == 4) | (sub == 7)
    left = (sub == 0) | (sub == 3) | (sub == 5)

    def main(g, y):
        return rate8[pl.ds(y, 8, stride=16), :]

    for i in range(EXT):
        a, b = extended(20, i, main, above, below, halo_l, halo_r)
        la, lb = swap_left(a, b)
        ra, rb = swap_right(a, b)
        coef_a[i * 16 : i * 16 + 8, :] = jnp.where(right, ra, jnp.where(left, la, a))
        coef_b[i * 16 : i * 16 + 8, :] = jnp.where(right, rb, jnp.where(left, lb, b))
        coef_a[i * 16 + 8 : i * 16 + 16, :] = jnp.broadcast_to(
            jnp.sum(a, axis=0, keepdims=True), (8, W)
        )
        coef_b[i * 16 + 8 : i * 16 + 16, :] = jnp.broadcast_to(
            jnp.sum(b, axis=0, keepdims=True), (8, W)
        )


def level_speeds(lev_speed, groups):
    sub = lax.broadcasted_iota(jnp.int32, (8, W), 0)
    speeds = []
    for g in groups:
        v = jnp.zeros((8, W), F32)
        for k in range(8):
            v = jnp.where(sub == k, lev_speed[(8 * g + k) % 80], v)
        speeds.append(v)
    return speeds


def fill(groups, ta, tb, main, above, below, halo_l, halo_r):
    wide = 8 * len(groups)
    for n, g in enumerate(groups):
        for part in range(3):
            span = range(8 * part, 8 * part + 8)
            pairs = [extended(g, i, main, above, below, halo_l, halo_r) for i in span]
            for i, (a, b) in zip(span, pairs):
                ta[i * wide + 8 * n : i * wide + 8 * n + 8, :] = a
                tb[i * wide + 8 * n : i * wide + 8 * n + 8, :] = b


def advect_cell(cells, coefs, speed):
    outs = []
    for (t0, t1, t2), c in zip(cells, coefs):
        to_r = c[2] * t0 + c[4] * t1 + c[7] * t2
        to_l = c[0] * t0 + c[3] * t1 + c[5] * t2
        mid = c[1] * t0 + c[6] * t2 - c[8] * t1
        outs.append((t1, to_r, to_l, mid))
    (a1, ar, al, am), (b1, br, bl, bm) = outs
    ua, ub = swap_left(ar, br)
    va, vb = swap_right(al, bl)
    return a1 + speed * (am + ua + va), b1 + speed * (bm + ub + vb)


def advect(pairs, coef_a, coef_b, speed, count, chunk, result):
    wide = count * 8

    def at(i, n):
        return pl.ds(pl.multiple_of(i * wide + 8 * n, 8), 8)

    for step in range(ADV):
        now, later = pairs[step % 2], pairs[(step + 1) % 2]
        last = step == ADV - 1

        def row(i, carry, now=now, later=later, last=last):
            def coef(ref, o):
                return jnp.broadcast_to(ref[pl.ds(i * 16 + o, 1), :], (8, W))

            coefs = [[coef(ref, o) for o in range(9)] for ref in (coef_a, coef_b)]
            for base in range(0, count, chunk):
                span = range(base, base + chunk)
                news = []
                for n in span:
                    cells = [[t[at(k, n), :] for k in (i - 1, i, i + 1)] for t in now]
                    news.append(advect_cell(cells, coefs, speed[8 * n : 8 * n + 8, :]))
                for n, (new_a, new_b) in zip(span, news):
                    if last:
                        place = pl.multiple_of((i - ADV) * wide + 8 * n, 8)
                        result[pl.ds(place, 8), :] = new_a
                    else:
                        later[0][at(i, n), :] = new_a
                        later[1][at(i, n), :] = new_b
            return carry

        lax.fori_loop(step + 1, EXT - 1 - step, row, 0)


def edge_sums(above, below, halo_l, halo_r, buf, edge, far_l, far_r, ready, emit):
    lane = lanes(8)
    for p in range(5):
        rows = slice(16 * p, 16 * p + 16)
        rest = slice(80 + 16 * p, 96 + 16 * p)
        v = halo_l[rows, :].astype(F32) + halo_l[rest, :].astype(F32)
        far_l[rows, :] = pltpu.roll(v, 2, 1)
        far_r[rows, :] = halo_r[rows, :].astype(F32) + halo_r[rest, :].astype(F32)
        v = above[rows, :].astype(F32) + above[rest, :].astype(F32)
        buf[16 * p : 16 * p + 16, :] = v
        v = below[rows, :].astype(F32) + below[rest, :].astype(F32)
        buf[2640 + 16 * p : 2656 + 16 * p, :] = v
    for g in range(10):
        rows = slice(8 * g, 8 * g + 8)
        from_l, from_r = far_l[rows, :], far_r[rows, :]
        for y in range(32):
            v = jnp.where(lane == y, from_r, from_l)
            at = 80 * y + 8 * g
            edge[at : at + 8, :] = pltpu.roll(v, (W - 1 - y) % W, 1)
    ready()

    def quad(q, carry):
        first = lane % 4 == 0
        final = lane % 4 == 3
        outer = (lane == 0) | (lane == W - 1)

        def at(row, g, wide=80):
            return pl.ds(pl.multiple_of(row * wide + 8 * g, 8), 8)

        for r in range(4):
            y = 4 * q + r
            values = []
            for g in (9, 0, 1, 2, 3, 4, 5, 6, 7, 8):
                v = buf[at(y + 1, g), :]
                if r == 0:
                    v = v + buf[at(y, g), :]
                if r == 3:
                    v = v + buf[at(y + 2, g), :]
                near = jnp.where(first, pltpu.roll(v, 1, 1), pltpu.roll(v, W - 1, 1))
                near = jnp.where(outer, edge[at(y, g), :], near)
                v = v + jnp.where(first | final, near, 0.0)
                if g == 9:
                    inverse = 1.0 / v
                else:
                    values.append(v * inverse)
            emit(y, values, at)
        return carry

    lax.fori_loop(0, 8, quad, 0)


def assemble(
    comp, lev_speed, turned, rate8, above, below, halo_l, halo_r, lhs,
    own, flux, top,
    buf, sem, edge, high, low, far_l, far_r, ta, tb, tc, td, coef_a, coef_b,
):
    @pl.when(comp[0] == 0)
    def _():
        def emit(y, values, at):
            hi, lo = split(jnp.concatenate(values + [jnp.zeros((8, W), F32)], axis=0))
            high[y] = hi
            low[y] = lo

        copy = pltpu.make_async_copy(turned, buf.at[pl.ds(80, 2560)], sem)
        copy.start()
        edge_sums(above, below, halo_l, halo_r, buf, edge, far_l, far_r, copy.wait, emit)
        for y in range(32):
            first = jnp.dot(lhs[...], high[y], preferred_element_type=F32)
            second = jnp.dot(lhs[0:32, :], low[y], preferred_element_type=F32)
            total = first[0:32] + first[32:64] + second
            flux[y] = total[0:16].astype(BF16)
            hi, lo = split(total[16:32])
            own[y, 0:16] = hi
            own[y, 16:32] = lo

    @pl.when(comp[0] == 1)
    def _():
        copy = pltpu.make_async_copy(turned, buf.at[pl.ds(80, 2560)], sem)
        copy.start()
        prepare_rates(coef_a, coef_b, rate8, above, below, halo_l, halo_r)
        copy.wait()

        def main(g, y):
            return buf[80 + 160 * y + 8 * g : 88 + 160 * y + 8 * g, :]

        sub = lax.broadcasted_iota(jnp.int32, (8, W), 0)
        for i in range(EXT):
            first = extended(0, i, main, above, below, halo_l, halo_r)
            second = extended(10, i, main, above, below, halo_l, halo_r)
            for ref, u, v in zip((ta, tb), first, second):
                ref[8 * i : 8 * i + 8, :] = jnp.where(sub == 0, u, pltpu.roll(v, 1, 0))
        pairs = ((ta, tb), (tc, td))
        speed = lev_speed[0]
        for step in range(ADV):
            now, later = pairs[step % 2], pairs[(step + 1) % 2]
            for i in range(step + 1, EXT - 1 - step):
                new_a, new_b = advect_cell(
                    [[t[8 * k : 8 * k + 8, :] for k in (i - 1, i, i + 1)] for t in now],
                    [
                        [
                            jnp.broadcast_to(ref[16 * i + o : 16 * i + o + 1, :], (8, W))
                            for o in range(9)
                        ]
                        for ref in (coef_a, coef_b)
                    ],
                    speed,
                )
                later[0][8 * i : 8 * i + 8, :] = new_a
                later[1][8 * i : 8 * i + 8, :] = new_b
        for v in range(2):
            rows = [ta[pl.ds((ADV + y) * 8 + v, 8, stride=8), :] for y in (0, 8)]
            top[v] = jnp.concatenate(rows, axis=0).astype(BF16)


def tile_products(
    comp, src, dest, dst, own, arrived, weights, top, send, count, meta, parts
):
    band = send.shape[0] // TILES_PER_PEER
    tiles = weights.shape[0]

    lane8 = lanes(8)
    sub8 = lax.broadcasted_iota(jnp.int32, (8, W), 0)

    def product(lhs, t):
        return lax.dot_general(
            lhs[src[0, t]], weights[t], (((1,), (1,)), ((), ())), preferred_element_type=F32
        )

    @pl.when(comp[0] == 0)
    def _():
        for t in range(tiles):
            both = product(own, t)
            parts[8 * t : 8 * t + 8, :] = both[0:8] + both[16:24]
        pieces = []
        for v in range(2):
            for p in range(4):
                rows = [parts[pl.ds(128 * p + 64 * q + v, 8, stride=8), :] for q in range(2)]
                pieces.append(jnp.concatenate(rows, axis=0).astype(BF16))
        ids = jnp.zeros((8, W), F32)
        for t in range(tiles):
            named = jnp.where(sub8 == 0, dest[0, t], dst[0, t]).astype(F32)
            ids = jnp.where(lane8 % tiles == t, named, ids)
        pieces.append(jnp.concatenate([ids, ids], axis=0).astype(BF16))

        def spread(h, carry):
            for j, piece in enumerate(pieces):
                send[h * TILES_PER_PEER + j] = piece
            return carry

        lax.fori_loop(0, band, spread, 0)

    @pl.when(comp[0] == 1)
    def _():
        def clear(h, carry):
            for j in range(TILES_PER_PEER):
                if j < 2:
                    send[h * TILES_PER_PEER + j] = top[j]
                else:
                    send[h * TILES_PER_PEER + j] = jnp.zeros((16, W), BF16)
            count[h] = 0
            meta[h] = jnp.full((8, W), -1.0, F32)
            return carry

        lax.fori_loop(0, band, clear, 0)
        for t in range(tiles):
            owner = dest[0, t]
            slot = count[owner]
            count[owner] = slot + 1
            place = slot + 2
            send[owner * TILES_PER_PEER + place] = product(arrived, t).astype(BF16)
            named = jnp.where(
                (lane8 // 16 == place) & (sub8 == 2), dst[0, t].astype(F32), meta[owner]
            )
            meta[owner] = named

        def finish(h, carry):
            m = meta[h]
            send[h * TILES_PER_PEER + 8] = jnp.concatenate([m, m], axis=0).astype(BF16)
            return carry

        lax.fori_loop(0, band, finish, 0)


def advect_all(
    comp, lev_speed, state, tracer, mass, rate8, above, below, halo_l, halo_r, after,
    result, dss, buf, edge, far_l, far_r, ta, tb, tc, td, coef_a, coef_b, speed,
):
    del after

    @pl.when(comp[0] == 0)
    def _():
        def emit(y, values, at):
            for g, v in enumerate(values):
                ta[at(y, g, 72), :] = v

        for y in range(32):
            m = jnp.broadcast_to(mass[y : y + 1, :], (8, W))
            for g in range(9):
                at = 80 + 80 * y + 8 * g
                buf[at : at + 8, :] = m * state[pl.ds(g * 256 + y, 8, stride=32), :]
            buf[152 + 80 * y : 160 + 80 * y, :] = m
        edge_sums(above, below, halo_l, halo_r, buf, edge, far_l, far_r, lambda: None, emit)
        for f in range(72):
            for p in range(4):
                dss[32 * f + 8 * p : 32 * f + 8 * p + 8, :] = ta[
                    pl.ds(72 * 8 * p + f, 8, stride=72), :
                ]

    @pl.when(comp[0] == 1)
    def _():
        dss[...] = jnp.zeros(dss.shape, F32)
        prepare_rates(coef_a, coef_b, rate8, above, below, halo_l, halo_r)

        def main(g, y):
            return tracer[pl.ds(g * 128 + y, 8, stride=16), :]

        groups = tuple(range(20))
        fill(groups, ta, tb, main, above, below, halo_l, halo_r)
        for n, v in enumerate(level_speeds(lev_speed, groups[:10])):
            speed[8 * n : 8 * n + 8, :] = v
            speed[80 + 8 * n : 88 + 8 * n, :] = v
        advect(((ta, tb), (tc, td)), coef_a, coef_b, speed, 20, 4, result)


def wanted(back_owner, back_src):
    sub8 = lax.broadcasted_iota(jnp.int32, (8, W), 0)
    wants = []
    for p in range(8):
        v = jnp.zeros((8, W), jnp.int32)
        for k in range(8):
            v = jnp.where(sub8 == k, back_owner[0, 8 * p + k] * 16 + back_src[0, 8 * p + k], v)
        wants.append(v)
    return jnp.concatenate(wants, axis=0).astype(F32)


def surface_select(comp, back_owner, back_src, received, out):
    band = received.shape[0] // TILES_PER_PEER

    @pl.when(comp[0] == 0)
    def _():
        lane = lanes(1)
        want = wanted(back_owner, back_src)

        def pair(q, carry):
            h = 2 * q
            ids = [received[(h + d) * TILES_PER_PEER + 8].astype(F32) for d in range(2)]
            named = [v[0:1, :] * 16.0 + v[1:2, :] for v in ids]
            row = jnp.where(lane < 64, named[0], named[1])
            hot = jnp.where(jnp.broadcast_to(row, (64, W)) == want, 1.0, 0.0).astype(BF16)
            totals = []
            for v in range(2):
                rhs = jnp.concatenate(
                    [
                        received[(h + d) * TILES_PER_PEER + 4 * v + j]
                        for d in range(2)
                        for j in range(4)
                    ],
                    axis=0,
                )
                totals.append(carry[v] + jnp.dot(hot, rhs, preferred_element_type=F32))
            return tuple(totals)

        zero = jnp.zeros((64, W), F32)
        sums = lax.fori_loop(0, band // 2, pair, (zero, zero), unroll=4)
        for v in range(2):
            out[64 * v : 64 * v + 64, :] = sums[v]


def finish(
    comp, back_owner, back_src, back_dst,
    weights_ref, advected, received, profile, mine, other,
    ocean, surface, weights, sem, table, parts, acc,
):
    band = received.shape[0] // TILES_PER_PEER
    tiles = weights.shape[0]

    @pl.when(comp[0] == 0)
    def _():
        half = tiles // 2
        copies = [
            pltpu.make_async_copy(
                weights_ref.at[pl.ds(half * n, half)], weights.at[pl.ds(half * n, half)],
                sem.at[n],
            )
            for n in range(2)
        ]
        for copy in copies:
            copy.start()
        want = wanted(back_owner, back_src)
        ocean[...] = jnp.zeros(ocean.shape, F32)
        sums = [mine[64 * v : 64 * v + 64, :] for v in range(2)]
        for c in range(band // 8):
            row = (lanes(64) + c * W).astype(F32)
            hot = jnp.where(row == want, 1.0, 0.0).astype(BF16)
            for v in range(2):
                rhs = jnp.concatenate([other[(8 * c + h) * 2 + v] for h in range(8)], axis=0)
                sums[v] = sums[v] + jnp.dot(hot, rhs, preferred_element_type=F32)
        for v in range(2):
            hi, lo = split(sums[v])
            for at, part in ((v, hi.astype(F32)), (2 + v, lo.astype(F32))):
                for p in range(8):
                    table[pl.ds(64 * p + at, 8, stride=8), :] = part[8 * p : 8 * p + 8]
        acc[...] = jnp.zeros(acc.shape, F32)
        for t in range(tiles):
            if t % half == 0:
                copies[t // half].wait()
            parts[8 * t : 8 * t + 8, :] = lax.dot_general(
                table[8 * t : 8 * t + 8, :].astype(BF16),
                weights[t],
                (((1,), (1,)), ((), ())),
                preferred_element_type=F32,
            )
        for t in range(tiles):
            at = pl.ds(pl.multiple_of(back_dst[0, t] * 8, 8), 8)
            acc[at, :] = acc[at, :] + parts[8 * t : 8 * t + 8, :]
        for v in range(2):
            for p in range(4):
                surface[32 * v + 8 * p : 32 * v + 8 * p + 8, :] = (
                    acc[pl.ds(64 * p + v, 8, stride=8), :]
                    + acc[pl.ds(64 * p + 2 + v, 8, stride=8), :]
                )

    @pl.when(comp[0] == 1)
    def _():
        surface[...] = jnp.zeros(surface.shape, F32)
        row = lax.broadcasted_iota(jnp.int32, (256, W), 0)
        point = jnp.where(row % 16 == lanes(256) % 16, row // 16, -2).astype(F32)

        def add(h, total):
            named = received[h * TILES_PER_PEER + 8].astype(F32)[2:3, :]
            hot = jnp.where(jnp.broadcast_to(named, (256, W)) == point, 1.0, 0.0)
            rhs = jnp.concatenate(
                [received[h * TILES_PER_PEER + j] for j in range(8)], axis=0
            )
            return total + jnp.dot(hot.astype(BF16), rhs, preferred_element_type=F32)

        total = lax.fori_loop(0, band, add, jnp.zeros((256, W), F32), unroll=4)
        level_hi, level_lo = split(profile[...])
        for y in range(16):
            hi, lo = split(total[16 * y : 16 * y + 16, :])
            more = (
                jnp.dot(level_hi, hi, preferred_element_type=F32)
                + jnp.dot(level_hi, lo, preferred_element_type=F32)
                + jnp.dot(level_lo, hi, preferred_element_type=F32)
            )
            new = advected[160 * y : 160 * y + 160, :] + more
            for g in range(20):
                ocean[pl.ds(g * 128 + y, 8, stride=16), :] = new[8 * g : 8 * g + 8]


def shifted(array, axis, by):
    peers = lax.axis_size(axis)
    pairs = [(i, i + by) for i in range(peers) if 0 <= i + by < peers]
    return lax.ppermute(array, axis, pairs)


def shape(*dims, dtype=F32):
    return jax.ShapeDtypeStruct(dims, dtype)


def shards(
    atm_state,
    atm_mass,
    coupler,
    flux_dest,
    flux_dst_blk,
    flux_src_blk,
    conservative_flux_weights,
    ocn_tracers,
    ocean_neighbour_codes,
    ocn_rates,
    lev_speed,
    profile,
    back_owner,
    back_src_blk,
    back_dst_blk,
    return_remap_weights,
):
    comp = lax.axis_index("comp").astype(jnp.int32).reshape(1)
    band = lax.axis_size("gx")
    state = atm_state.reshape(72 * 32, W)
    tracer = ocn_tracers.reshape(2 * 80 * 16, W)
    codes = ocean_neighbour_codes.reshape(96, W)
    rates = ocn_rates.reshape(96, W)
    dma = pltpu.SemaphoreType.DMA
    buf = pltpu.VMEM((2560, W), F32)

    up, down, rate8 = call(
        pack_rows,
        [shape(4 * PR, W, dtype=BF16), shape(4 * PR, W, dtype=BF16), shape(128, W)],
        1, 5, 0,
        [
            buf, pltpu.VMEM((32, W), F32), pltpu.VMEM((96, W), jnp.int32),
            pltpu.VMEM((96, W), F32), dma((3,)),
        ],
        62,
    )(comp, state, tracer, atm_mass, codes, rates)
    below = shifted(up, "gy", -1)
    above = shifted(down, "gy", 1)
    raw_left, raw_right, turned = call(
        pack_columns, [shape(PR, W), shape(PR, W), shape(2560, W)], 1, 0, 4, []
    )(comp, state, tracer, atm_mass, rate8)
    left, right = call(
        finish_columns,
        [shape(PR, W, dtype=BF16), shape(PR, W, dtype=BF16)],
        1, 0, 4,
        [],
    )(comp, raw_left, raw_right, above, below)
    halo_r = shifted(left, "gx", -1)
    halo_l = shifted(right, "gx", 1)

    top_profile = jnp.dot(profile[:, 0], coupler, precision=lax.Precision.HIGHEST)
    lhs = jnp.pad(jnp.concatenate([coupler, top_profile], axis=0), ((0, 14), (0, 8)))
    lhs_hi, lhs_lo = split(lhs)
    lhs = jnp.concatenate([lhs_hi, lhs_lo], axis=0)
    small = pltpu.VMEM((EXT * 8, W), F32)

    coef = pltpu.VMEM((EXT * 16, W), F32)
    points = pltpu.VMEM((34 * 80, W), F32)
    rows = pltpu.VMEM((80, W), F32)
    own, flux, top = call(
        assemble,
        [
            shape(32, 32, W, dtype=BF16),
            shape(32, 16, W, dtype=BF16),
            shape(2, 16, W, dtype=BF16),
        ],
        2, 1, 6,
        [
            points, dma, buf,
            pltpu.VMEM((32, 80, W), BF16), pltpu.VMEM((32, 80, W), BF16), rows, rows,
            small, small, small, small, coef, coef,
        ],
    )(
        comp, lev_speed, turned, rate8, above, below, halo_l, halo_r, lhs,
    )
    arrived = shifted(flux, "comp", 1)
    send, = call(
        tile_products,
        [shape(band * TILES_PER_PEER, 16, W, dtype=BF16)],
        4, 0, 4,
        [
            pltpu.SMEM((band,), jnp.int32),
            pltpu.VMEM((band, 8, W), F32),
            pltpu.VMEM((512, W), F32),
        ],
    )(
        comp, flux_src_blk, flux_dest.reshape(1, 64), flux_dst_blk,
        own, arrived, conservative_flux_weights[0], top,
    )
    send, top = lax.optimization_barrier((send, top))
    received = lax.all_to_all(
        send.reshape(band, TILES_PER_PEER, 16, W), "gx", 0, 0, tiled=True
    ).reshape(band * TILES_PER_PEER, 16, W)
    grid = pltpu.VMEM((EXT * 160, W), F32)
    advected, dss = call(
        advect_all,
        [shape(16 * 160, W), shape(72 * 32, W)],
        2, 0, 9,
        [
            points, buf, rows, rows, grid, grid, grid, grid, coef, coef,
            pltpu.VMEM((160, W), F32),
        ],
    )(
        comp, lev_speed, state, tracer, atm_mass, rate8, above, below, halo_l, halo_r, top,
    )
    levels = profile.reshape(160, 16)
    received, advected, levels = lax.optimization_barrier((received, advected, levels))
    tops = received.reshape(band, TILES_PER_PEER, 16, W)[:, :2].reshape(2 * band, 16, W)
    other = shifted(tops, "comp", -1)
    mine, = call(surface_select, [shape(128, W)], 3, 0, 1, [])(
        comp, back_owner, back_src_blk, received
    )
    return_weights = pltpu.with_memory_space_constraint(return_remap_weights[0], pltpu.HBM)
    ocean, surface = call(finish, [shape(2560, W), shape(64, W)], 4, 1, 5, [
        pltpu.VMEM(return_remap_weights.shape[1:], BF16), dma((2,)),
        pltpu.VMEM((512, W), F32), pltpu.VMEM((512, W), F32), pltpu.VMEM((256, W), F32),
    ])(
        comp, back_owner, back_src_blk, back_dst_blk,
        return_weights, advected, received, levels, mine, other,
    )
    return (
        dss.reshape(1, 72, 32, W),
        surface.reshape(1, 2, 32, W),
        ocean.reshape(1, 2, 80, 16, W),
    )


def solution(mesh):
    placed = (
        P("comp", None, "gy", "gx"),
        P("gy", "gx"),
        P(),
        P("gy", "gx", None),
        P("gy", "gx"),
        P("gy", "gx"),
        P("gy", "gx", None, None),
        P("comp", None, None, "gy", "gx"),
        P(None, "gy", "gx"),
        P(None, "gy", "gx"),
        P(),
        P(),
        P("gy", "gx"),
        P("gy", "gx"),
        P("gy", "gx"),
        P("gy", "gx", None, None),
    )
    return jax.shard_map(
        shards,
        mesh=mesh,
        in_specs=placed,
        out_specs=(
            P("comp", None, "gy", "gx"),
            P("comp", None, "gy", "gx"),
            P("comp", None, None, "gy", "gx"),
        ),
        check_vma=False,
    )
```

```python
import functools

import jax
import jax.numpy as jnp
from jax import lax
from jax.experimental import pallas as pl
from jax.experimental.pallas import tpu as pltpu
from jax.sharding import PartitionSpec as P

F32 = jnp.float32
BF16 = jnp.bfloat16
ADV = 4
W = 128
PR = 176
EXT = 24
TILES_PER_PEER = 9


def lanes(rows):
    return lax.broadcasted_iota(jnp.int32, (rows, W), 1)


def in_hbm(array):
    return pltpu.with_memory_space_constraint(array, pltpu.HBM)


def split(value):
    hi = value.astype(BF16)
    return hi, (value - hi.astype(F32)).astype(BF16)


def call(body, out_shape, n_smem, n_any, n_vmem, scratch):
    specs = (
        [pl.BlockSpec(memory_space=pltpu.SMEM)] * n_smem
        + [pl.BlockSpec(memory_space=pl.ANY)] * n_any
        + [pl.BlockSpec(memory_space=pltpu.VMEM)] * n_vmem
    )
    return pl.pallas_call(
        body,
        out_shape=out_shape,
        in_specs=specs,
        out_specs=[pl.BlockSpec(memory_space=pltpu.VMEM)] * len(out_shape),
        scratch_shapes=scratch,
        compiler_params=pltpu.CompilerParams(vmem_limit_bytes=16 * 1024 * 1024),
        name=body.__name__,
    )


def pack_rows(
    comp, state_ref, tracer_ref, mass_ref, codes_ref, rates_ref, up, down, rate8,
    buf, mass, codes, rates, sem,
):
    state = tracer = buf

    def fetch_all(*pairs):
        copies = [
            pltpu.make_async_copy(src, dst, sem.at[n]) for n, (src, dst) in enumerate(pairs)
        ]
        for copy in copies:
            copy.start()
        for copy in copies:
            copy.wait()

    @pl.when(comp[0] == 0)
    def _():
        fetch_all((state_ref, buf.at[pl.ds(0, 2304)]), (mass_ref, mass))
        for dst, y in ((up, 0), (down, 31)):
            m = jnp.broadcast_to(mass[y : y + 1, :], (8, W))
            parts = [state[pl.ds(g * 256 + y, 8, stride=32), :] * m for g in range(9)] + [m]
            for p in range(5):
                hi, lo = split(jnp.concatenate(parts[2 * p : 2 * p + 2], axis=0))
                dst[16 * p : 16 * p + 16, :] = hi
                dst[80 + 16 * p : 96 + 16 * p, :] = lo

    @pl.when(comp[0] == 1)
    def _():
        fetch_all((tracer_ref, buf), (codes_ref, codes), (rates_ref, rates))
        for o in range(8):
            acc = jnp.zeros((16, W), F32)
            for k in range(6):
                rows = slice(16 * k, 16 * k + 16)
                acc = acc + jnp.where(codes[rows, :] == o, rates[rows, :], 0.0)
            rate8[16 * o : 16 * o + 16, :] = acc
        for dst, first in ((up, 0), (down, 12)):
            for j in range(ADV):
                y = first + j
                for p in range(10):
                    both = jnp.concatenate(
                        [tracer[pl.ds(g * 128 + y, 8, stride=16), :] for g in (2 * p, 2 * p + 1)],
                        axis=0,
                    )
                    dst[j * PR + 16 * p : j * PR + 16 * p + 16, :] = both.astype(BF16)
                r = rate8[pl.ds(y, 8, stride=16), :]
                dst[j * PR + 160 : j * PR + 176, :] = jnp.concatenate([r, r], axis=0).astype(BF16)


def pack_columns(comp, state, tracer, mass, rate8, left, right, turned):
    lane = lanes(8)

    @pl.when(comp[0] == 0)
    def _():
        for g in range(10):
            to_left = jnp.zeros((8, W), F32)
            to_right = jnp.zeros((8, W), F32)
            for y in range(32):
                v = jnp.broadcast_to(mass[y : y + 1, :], (8, W))
                if g < 9:
                    v = v * state[pl.ds(g * 256 + y, 8, stride=32), :]
                turned[80 * y + 8 * g : 80 * y + 8 * g + 8, :] = v
                v = pltpu.roll(v, y, 1)
                to_left = jnp.where(lane == y, v, to_left)
                to_right = jnp.where(lane == (y - 1) % W, v, to_right)
            left[8 * g : 8 * g + 8, :] = to_left
            right[8 * g : 8 * g + 8, :] = to_right

    @pl.when(comp[0] == 1)
    def _():
        for g in range(21):
            to_left = jnp.zeros((8, W), F32)
            to_right = jnp.zeros((8, W), F32)
            for y in range(16):
                i = y + ADV
                if g < 20:
                    v = tracer[pl.ds(g * 128 + y, 8, stride=16), :]
                    turned[160 * y + 8 * g : 160 * y + 8 * g + 8, :] = v
                else:
                    v = rate8[pl.ds(y, 8, stride=16), :]
                v = pltpu.roll(v, 4 * i, 1)
                to_left = jnp.where(lane // 4 == i, v, to_left)
                to_right = jnp.where(lane // 4 == i - 1, v, to_right)
            left[8 * g : 8 * g + 8, :] = to_left
            right[8 * g : 8 * g + 8, :] = to_right
        left[168:176, :] = jnp.zeros((8, W), F32)
        right[168:176, :] = jnp.zeros((8, W), F32)


def finish_columns(comp, raw_left, raw_right, above, below, left, right):
    lane = lanes(16)

    @pl.when(comp[0] == 0)
    def _():
        for p in range(5):
            rows = slice(16 * p, 16 * p + 16)
            low = slice(80 + 16 * p, 96 + 16 * p)
            up = above[rows, :].astype(F32) + above[low, :].astype(F32)
            down = below[rows, :].astype(F32) + below[low, :].astype(F32)
            down = pltpu.roll(down, 31, 1)
            for src, dst, at in ((raw_left, left, 0), (raw_right, right, 1)):
                v = src[rows, :]
                pos = (lane + at) % 4
                before = jnp.where(lane == (W - at) % W, up, pltpu.roll(v, 1, 1))
                after = jnp.where(lane == 31 - at, down, pltpu.roll(v, W - 1, 1))
                v = v + jnp.where(pos == 0, before, 0.0) + jnp.where(pos == 3, after, 0.0)
                hi, lo = split(v)
                dst[rows, :] = hi
                dst[low, :] = lo

    @pl.when(comp[0] == 1)
    def _():
        for p in range(11):
            rows = slice(16 * p, 16 * p + 16)
            to_left = raw_left[rows, :]
            to_right = raw_right[rows, :]
            for src, first in ((above, 0), (below, 20)):
                for j in range(ADV):
                    i = first + j
                    v = src[j * PR + 16 * p : j * PR + 16 * p + 16, :].astype(F32)
                    v = pltpu.roll(v, 4 * i, 1)
                    to_left = jnp.where(lane // 4 == i, v, to_left)
                    to_right = jnp.where(lane // 4 == (i - 1) % 32, v, to_right)
            left[rows, :] = to_left.astype(BF16)
            right[rows, :] = to_right.astype(BF16)


def swap_left(a, b):
    lane = lanes(a.shape[0])
    ra, rb = pltpu.roll(a, W - 1, 1), pltpu.roll(b, W - 1, 1)
    return jnp.where(lane == W - 1, rb, ra), jnp.where(lane == W - 1, ra, rb)


def swap_right(a, b):
    lane = lanes(a.shape[0])
    ra, rb = pltpu.roll(a, 1, 1), pltpu.roll(b, 1, 1)
    return jnp.where(lane == 0, rb, ra), jnp.where(lane == 0, ra, rb)


def halo_tile(from_right, from_left, i):
    lane = lanes(8)
    v = jnp.where(lane // 4 == i, from_right, from_left)
    v = pltpu.roll(v, (W - 4 * i) % W, 1)
    return jnp.where((lane < 4) | (lane >= W - 4), v, 0.0)


def extended(g, i, main, above, below, halo_l, halo_r):
    rows = slice(8 * g, 8 * g + 8)
    half = slice(8 * (g % 2), 8 * (g % 2) + 8)
    pair = 16 * (g // 2)

    def wide(ref, at):
        return ref[at : at + 16, :].astype(F32)[half]

    if i < ADV:
        a = wide(above, i * PR + pair)
    elif i >= EXT - ADV:
        a = wide(below, (i - EXT + ADV) * PR + pair)
    else:
        a = main(g, i - ADV)
    b = halo_tile(wide(halo_r, pair), wide(halo_l, pair), i)
    return a, b


RIGHTWARD = (2, 4, 7)
LEFTWARD = (0, 3, 5)


def prepare_rates(coef_a, coef_b, rate8, above, below, halo_l, halo_r):
    sub = lax.broadcasted_iota(jnp.int32, (8, W), 0)
    right = (sub == 2) | (sub == 4) | (sub == 7)
    left = (sub == 0) | (sub == 3) | (sub == 5)

    def main(g, y):
        return rate8[pl.ds(y, 8, stride=16), :]

    for i in range(EXT):
        a, b = extended(20, i, main, above, below, halo_l, halo_r)
        la, lb = swap_left(a, b)
        ra, rb = swap_right(a, b)
        coef_a[i * 16 : i * 16 + 8, :] = jnp.where(right, ra, jnp.where(left, la, a))
        coef_b[i * 16 : i * 16 + 8, :] = jnp.where(right, rb, jnp.where(left, lb, b))
        coef_a[i * 16 + 8 : i * 16 + 16, :] = jnp.broadcast_to(
            jnp.sum(a, axis=0, keepdims=True), (8, W)
        )
        coef_b[i * 16 + 8 : i * 16 + 16, :] = jnp.broadcast_to(
            jnp.sum(b, axis=0, keepdims=True), (8, W)
        )


def level_speeds(lev_speed, groups):
    sub = lax.broadcasted_iota(jnp.int32, (8, W), 0)
    speeds = []
    for g in groups:
        v = jnp.zeros((8, W), F32)
        for k in range(8):
            v = jnp.where(sub == k, lev_speed[(8 * g + k) % 80], v)
        speeds.append(v)
    return speeds


def fill(groups, ta, tb, main, above, below, halo_l, halo_r):
    wide = 8 * len(groups)
    for n, g in enumerate(groups):
        for part in range(3):
            span = range(8 * part, 8 * part + 8)
            pairs = [extended(g, i, main, above, below, halo_l, halo_r) for i in span]
            for i, (a, b) in zip(span, pairs):
                ta[i * wide + 8 * n : i * wide + 8 * n + 8, :] = a
                tb[i * wide + 8 * n : i * wide + 8 * n + 8, :] = b


def advect_cell(cells, coefs, speed):
    outs = []
    for (t0, t1, t2), c in zip(cells, coefs):
        to_r = c[2] * t0 + c[4] * t1 + c[7] * t2
        to_l = c[0] * t0 + c[3] * t1 + c[5] * t2
        mid = c[1] * t0 + c[6] * t2 - c[8] * t1
        outs.append((t1, to_r, to_l, mid))
    (a1, ar, al, am), (b1, br, bl, bm) = outs
    ua, ub = swap_left(ar, br)
    va, vb = swap_right(al, bl)
    return a1 + speed * (am + ua + va), b1 + speed * (bm + ub + vb)


def advect(pairs, coef_a, coef_b, speed, count, chunk, result):
    wide = count * 8

    def at(i, n):
        return pl.ds(pl.multiple_of(i * wide + 8 * n, 8), 8)

    for step in range(ADV):
        now, later = pairs[step % 2], pairs[(step + 1) % 2]
        last = step == ADV - 1

        def row(i, carry, now=now, later=later, last=last):
            def coef(ref, o):
                return jnp.broadcast_to(ref[pl.ds(i * 16 + o, 1), :], (8, W))

            coefs = [[coef(ref, o) for o in range(9)] for ref in (coef_a, coef_b)]
            for base in range(0, count, chunk):
                span = range(base, base + chunk)
                news = []
                for n in span:
                    cells = [[t[at(k, n), :] for k in (i - 1, i, i + 1)] for t in now]
                    news.append(advect_cell(cells, coefs, speed[8 * n : 8 * n + 8, :]))
                for n, (new_a, new_b) in zip(span, news):
                    if last:
                        place = pl.multiple_of((i - ADV) * wide + 8 * n, 8)
                        result[pl.ds(place, 8), :] = new_a
                    else:
                        later[0][at(i, n), :] = new_a
                        later[1][at(i, n), :] = new_b
            return carry

        lax.fori_loop(step + 1, EXT - 1 - step, row, 0)


def edge_sums(above, below, halo_l, halo_r, buf, edge, far_l, far_r, ready, emit):
    lane = lanes(8)
    for p in range(5):
        rows = slice(16 * p, 16 * p + 16)
        rest = slice(80 + 16 * p, 96 + 16 * p)
        v = halo_l[rows, :].astype(F32) + halo_l[rest, :].astype(F32)
        far_l[rows, :] = pltpu.roll(v, 2, 1)
        far_r[rows, :] = halo_r[rows, :].astype(F32) + halo_r[rest, :].astype(F32)
        v = above[rows, :].astype(F32) + above[rest, :].astype(F32)
        buf[16 * p : 16 * p + 16, :] = v
        v = below[rows, :].astype(F32) + below[rest, :].astype(F32)
        buf[2640 + 16 * p : 2656 + 16 * p, :] = v
    for g in range(10):
        rows = slice(8 * g, 8 * g + 8)
        from_l, from_r = far_l[rows, :], far_r[rows, :]
        for y in range(32):
            v = jnp.where(lane == y, from_r, from_l)
            at = 80 * y + 8 * g
            edge[at : at + 8, :] = pltpu.roll(v, (W - 1 - y) % W, 1)
    ready()

    def quad(q, carry):
        first = lane % 4 == 0
        final = lane % 4 == 3
        outer = (lane == 0) | (lane == W - 1)

        def at(row, g, wide=80):
            return pl.ds(pl.multiple_of(row * wide + 8 * g, 8), 8)

        for r in range(4):
            y = 4 * q + r
            values = []
            for g in (9, 0, 1, 2, 3, 4, 5, 6, 7, 8):
                v = buf[at(y + 1, g), :]
                if r == 0:
                    v = v + buf[at(y, g), :]
                if r == 3:
                    v = v + buf[at(y + 2, g), :]
                near = jnp.where(first, pltpu.roll(v, 1, 1), pltpu.roll(v, W - 1, 1))
                near = jnp.where(outer, edge[at(y, g), :], near)
                v = v + jnp.where(first | final, near, 0.0)
                if g == 9:
                    inverse = 1.0 / v
                else:
                    values.append(v * inverse)
            emit(y, values, at)
        return carry

    lax.fori_loop(0, 8, quad, 0)


def assemble(
    comp, lev_speed, turned, rate8, above, below, halo_l, halo_r, lhs,
    own, flux, top,
    buf, sem, edge, high, low, far_l, far_r, ta, tb, tc, td, coef_a, coef_b,
):
    @pl.when(comp[0] == 0)
    def _():
        def emit(y, values, at):
            hi, lo = split(jnp.concatenate(values + [jnp.zeros((8, W), F32)], axis=0))
            high[y] = hi
            low[y] = lo

        copy = pltpu.make_async_copy(turned, buf.at[pl.ds(80, 2560)], sem)
        copy.start()
        edge_sums(above, below, halo_l, halo_r, buf, edge, far_l, far_r, copy.wait, emit)
        for y in range(32):
            first = jnp.dot(lhs[...], high[y], preferred_element_type=F32)
            second = jnp.dot(lhs[0:32, :], low[y], preferred_element_type=F32)
            total = first[0:32] + first[32:64] + second
            flux[y] = total[0:16].astype(BF16)
            hi, lo = split(total[16:32])
            own[y, 0:16] = hi
            own[y, 16:32] = lo

    @pl.when(comp[0] == 1)
    def _():
        copy = pltpu.make_async_copy(turned, buf.at[pl.ds(80, 2560)], sem)
        copy.start()
        prepare_rates(coef_a, coef_b, rate8, above, below, halo_l, halo_r)
        copy.wait()

        def main(g, y):
            return buf[80 + 160 * y + 8 * g : 88 + 160 * y + 8 * g, :]

        sub = lax.broadcasted_iota(jnp.int32, (8, W), 0)
        for i in range(EXT):
            first = extended(0, i, main, above, below, halo_l, halo_r)
            second = extended(10, i, main, above, below, halo_l, halo_r)
            for ref, u, v in zip((ta, tb), first, second):
                ref[8 * i : 8 * i + 8, :] = jnp.where(sub == 0, u, pltpu.roll(v, 1, 0))
        pairs = ((ta, tb), (tc, td))
        speed = lev_speed[0]
        for step in range(ADV):
            now, later = pairs[step % 2], pairs[(step + 1) % 2]
            for i in range(step + 1, EXT - 1 - step):
                new_a, new_b = advect_cell(
                    [[t[8 * k : 8 * k + 8, :] for k in (i - 1, i, i + 1)] for t in now],
                    [
                        [
                            jnp.broadcast_to(ref[16 * i + o : 16 * i + o + 1, :], (8, W))
                            for o in range(9)
                        ]
                        for ref in (coef_a, coef_b)
                    ],
                    speed,
                )
                later[0][8 * i : 8 * i + 8, :] = new_a
                later[1][8 * i : 8 * i + 8, :] = new_b
        for v in range(2):
            rows = [ta[pl.ds((ADV + y) * 8 + v, 8, stride=8), :] for y in (0, 8)]
            top[v] = jnp.concatenate(rows, axis=0).astype(BF16)


def tile_products(
    comp, src, dest, dst, own, arrived, weights, top, send, count, meta, parts
):
    band = send.shape[0] // TILES_PER_PEER
    tiles = weights.shape[0]

    lane8 = lanes(8)
    sub8 = lax.broadcasted_iota(jnp.int32, (8, W), 0)

    def product(lhs, t):
        return lax.dot_general(
            lhs[src[0, t]], weights[t], (((1,), (1,)), ((), ())), preferred_element_type=F32
        )

    @pl.when(comp[0] == 0)
    def _():
        for t in range(tiles):
            both = product(own, t)
            parts[8 * t : 8 * t + 8, :] = both[0:8] + both[16:24]
        pieces = []
        for v in range(2):
            for p in range(4):
                rows = [parts[pl.ds(128 * p + 64 * q + v, 8, stride=8), :] for q in range(2)]
                pieces.append(jnp.concatenate(rows, axis=0).astype(BF16))
        ids = jnp.zeros((8, W), F32)
        for t in range(tiles):
            named = jnp.where(sub8 == 0, dest[0, t], dst[0, t]).astype(F32)
            ids = jnp.where(lane8 % tiles == t, named, ids)
        pieces.append(jnp.concatenate([ids, ids], axis=0).astype(BF16))

        def spread(h, carry):
            for j, piece in enumerate(pieces):
                send[h * TILES_PER_PEER + j] = piece
            return carry

        lax.fori_loop(0, band, spread, 0)

    @pl.when(comp[0] == 1)
    def _():
        def clear(h, carry):
            for j in range(TILES_PER_PEER):
                if j < 2:
                    send[h * TILES_PER_PEER + j] = top[j]
                else:
                    send[h * TILES_PER_PEER + j] = jnp.zeros((16, W), BF16)
            count[h] = 0
            meta[h] = jnp.full((8, W), -1.0, F32)
            return carry

        lax.fori_loop(0, band, clear, 0)
        for t in range(tiles):
            owner = dest[0, t]
            slot = count[owner]
            count[owner] = slot + 1
            place = slot + 2
            send[owner * TILES_PER_PEER + place] = product(arrived, t).astype(BF16)
            named = jnp.where(
                (lane8 // 16 == place) & (sub8 == 2), dst[0, t].astype(F32), meta[owner]
            )
            meta[owner] = named

        def finish(h, carry):
            m = meta[h]
            send[h * TILES_PER_PEER + 8] = jnp.concatenate([m, m], axis=0).astype(BF16)
            return carry

        lax.fori_loop(0, band, finish, 0)


def advect_all(
    comp, lev_speed, state, tracer, mass, rate8, above, below, halo_l, halo_r, after,
    result, dss, buf, edge, far_l, far_r, ta, tb, tc, td, coef_a, coef_b, speed,
):
    del after

    @pl.when(comp[0] == 0)
    def _():
        def emit(y, values, at):
            for g, v in enumerate(values):
                ta[at(y, g, 72), :] = v

        for y in range(32):
            m = jnp.broadcast_to(mass[y : y + 1, :], (8, W))
            for g in range(9):
                at = 80 + 80 * y + 8 * g
                buf[at : at + 8, :] = m * state[pl.ds(g * 256 + y, 8, stride=32), :]
            buf[152 + 80 * y : 160 + 80 * y, :] = m
        edge_sums(above, below, halo_l, halo_r, buf, edge, far_l, far_r, lambda: None, emit)
        for f in range(72):
            for p in range(4):
                dss[32 * f + 8 * p : 32 * f + 8 * p + 8, :] = ta[
                    pl.ds(72 * 8 * p + f, 8, stride=72), :
                ]

    @pl.when(comp[0] == 1)
    def _():
        dss[...] = jnp.zeros(dss.shape, F32)
        prepare_rates(coef_a, coef_b, rate8, above, below, halo_l, halo_r)

        def main(g, y):
            return tracer[pl.ds(g * 128 + y, 8, stride=16), :]

        groups = tuple(range(20))
        fill(groups, ta, tb, main, above, below, halo_l, halo_r)
        for n, v in enumerate(level_speeds(lev_speed, groups[:10])):
            speed[8 * n : 8 * n + 8, :] = v
            speed[80 + 8 * n : 88 + 8 * n, :] = v
        advect(((ta, tb), (tc, td)), coef_a, coef_b, speed, 20, 4, result)


def wanted(back_owner, back_src):
    sub8 = lax.broadcasted_iota(jnp.int32, (8, W), 0)
    wants = []
    for p in range(8):
        v = jnp.zeros((8, W), jnp.int32)
        for k in range(8):
            v = jnp.where(sub8 == k, back_owner[0, 8 * p + k] * 16 + back_src[0, 8 * p + k], v)
        wants.append(v)
    return jnp.concatenate(wants, axis=0).astype(F32)


def surface_select(comp, back_owner, back_src, received, out):
    band = received.shape[0] // TILES_PER_PEER

    @pl.when(comp[0] == 0)
    def _():
        lane = lanes(1)
        want = wanted(back_owner, back_src)

        def pair(q, carry):
            h = 2 * q
            ids = [received[(h + d) * TILES_PER_PEER + 8].astype(F32) for d in range(2)]
            named = [v[0:1, :] * 16.0 + v[1:2, :] for v in ids]
            row = jnp.where(lane < 64, named[0], named[1])
            hot = jnp.where(jnp.broadcast_to(row, (64, W)) == want, 1.0, 0.0).astype(BF16)
            totals = []
            for v in range(2):
                rhs = jnp.concatenate(
                    [
                        received[(h + d) * TILES_PER_PEER + 4 * v + j]
                        for d in range(2)
                        for j in range(4)
                    ],
                    axis=0,
                )
                totals.append(carry[v] + jnp.dot(hot, rhs, preferred_element_type=F32))
            return tuple(totals)

        zero = jnp.zeros((64, W), F32)
        sums = lax.fori_loop(0, band // 2, pair, (zero, zero), unroll=4)
        for v in range(2):
            out[64 * v : 64 * v + 64, :] = sums[v]


def finish(
    comp, back_owner, back_src, back_dst,
    weights_ref, advected, received, profile, mine, other,
    ocean, surface, weights, sem, table, parts, acc,
):
    band = received.shape[0] // TILES_PER_PEER
    tiles = weights.shape[0]

    @pl.when(comp[0] == 0)
    def _():
        half = tiles // 2
        copies = [
            pltpu.make_async_copy(
                weights_ref.at[pl.ds(half * n, half)], weights.at[pl.ds(half * n, half)],
                sem.at[n],
            )
            for n in range(2)
        ]
        for copy in copies:
            copy.start()
        want = wanted(back_owner, back_src)
        ocean[...] = jnp.zeros(ocean.shape, F32)
        sums = [mine[64 * v : 64 * v + 64, :] for v in range(2)]
        for c in range(band // 8):
            row = (lanes(64) + c * W).astype(F32)
            hot = jnp.where(row == want, 1.0, 0.0).astype(BF16)
            for v in range(2):
                rhs = jnp.concatenate([other[(8 * c + h) * 2 + v] for h in range(8)], axis=0)
                sums[v] = sums[v] + jnp.dot(hot, rhs, preferred_element_type=F32)
        for v in range(2):
            hi, lo = split(sums[v])
            for at, part in ((v, hi.astype(F32)), (2 + v, lo.astype(F32))):
                for p in range(8):
                    table[pl.ds(64 * p + at, 8, stride=8), :] = part[8 * p : 8 * p + 8]
        acc[...] = jnp.zeros(acc.shape, F32)
        for t in range(tiles):
            if t % half == 0:
                copies[t // half].wait()
            parts[8 * t : 8 * t + 8, :] = lax.dot_general(
                table[8 * t : 8 * t + 8, :].astype(BF16),
                weights[t],
                (((1,), (1,)), ((), ())),
                preferred_element_type=F32,
            )
        for t in range(tiles):
            at = pl.ds(pl.multiple_of(back_dst[0, t] * 8, 8), 8)
            acc[at, :] = acc[at, :] + parts[8 * t : 8 * t + 8, :]
        for v in range(2):
            for p in range(4):
                surface[32 * v + 8 * p : 32 * v + 8 * p + 8, :] = (
                    acc[pl.ds(64 * p + v, 8, stride=8), :]
                    + acc[pl.ds(64 * p + 2 + v, 8, stride=8), :]
                )

    @pl.when(comp[0] == 1)
    def _():
        surface[...] = jnp.zeros(surface.shape, F32)
        row = lax.broadcasted_iota(jnp.int32, (256, W), 0)
        point = jnp.where(row % 16 == lanes(256) % 16, row // 16, -2).astype(F32)

        def add(h, total):
            named = received[h * TILES_PER_PEER + 8].astype(F32)[2:3, :]
            hot = jnp.where(jnp.broadcast_to(named, (256, W)) == point, 1.0, 0.0)
            rhs = jnp.concatenate(
                [received[h * TILES_PER_PEER + j] for j in range(8)], axis=0
            )
            return total + jnp.dot(hot.astype(BF16), rhs, preferred_element_type=F32)

        total = lax.fori_loop(0, band, add, jnp.zeros((256, W), F32), unroll=4)
        level_hi, level_lo = split(profile[...])
        for y in range(16):
            hi, lo = split(total[16 * y : 16 * y + 16, :])
            more = (
                jnp.dot(level_hi, hi, preferred_element_type=F32)
                + jnp.dot(level_hi, lo, preferred_element_type=F32)
                + jnp.dot(level_lo, hi, preferred_element_type=F32)
            )
            new = advected[160 * y : 160 * y + 160, :] + more
            for g in range(20):
                ocean[pl.ds(g * 128 + y, 8, stride=16), :] = new[8 * g : 8 * g + 8]


def shifted(array, axis, by):
    peers = lax.axis_size(axis)
    pairs = [(i, i + by) for i in range(peers) if 0 <= i + by < peers]
    return lax.ppermute(array, axis, pairs)


def shape(*dims, dtype=F32):
    return jax.ShapeDtypeStruct(dims, dtype)


def shards(
    atm_state,
    atm_mass,
    coupler,
    flux_dest,
    flux_dst_blk,
    flux_src_blk,
    conservative_flux_weights,
    ocn_tracers,
    ocean_neighbour_codes,
    ocn_rates,
    lev_speed,
    profile,
    back_owner,
    back_src_blk,
    back_dst_blk,
    return_remap_weights,
):
    comp = lax.axis_index("comp").astype(jnp.int32).reshape(1)
    band = lax.axis_size("gx")
    state = atm_state.reshape(72 * 32, W)
    tracer = ocn_tracers.reshape(2 * 80 * 16, W)
    codes = ocean_neighbour_codes.reshape(96, W)
    rates = ocn_rates.reshape(96, W)
    dma = pltpu.SemaphoreType.DMA
    buf = pltpu.VMEM((2560, W), F32)

    up, down, rate8 = call(
        pack_rows,
        [shape(4 * PR, W, dtype=BF16), shape(4 * PR, W, dtype=BF16), shape(128, W)],
        1, 5, 0,
        [
            buf, pltpu.VMEM((32, W), F32), pltpu.VMEM((96, W), jnp.int32),
            pltpu.VMEM((96, W), F32), dma((3,)),
        ],
    )(comp, *(in_hbm(array) for array in (state, tracer, atm_mass, codes, rates)))
    below = shifted(up, "gy", -1)
    above = shifted(down, "gy", 1)
    raw_left, raw_right, turned = call(
        pack_columns, [shape(PR, W), shape(PR, W), shape(2560, W)], 1, 0, 4, []
    )(comp, state, tracer, atm_mass, rate8)
    left, right = call(
        finish_columns,
        [shape(PR, W, dtype=BF16), shape(PR, W, dtype=BF16)],
        1, 0, 4,
        [],
    )(comp, raw_left, raw_right, above, below)
    halo_r = shifted(left, "gx", -1)
    halo_l = shifted(right, "gx", 1)

    top_profile = jnp.dot(profile[:, 0], coupler, precision=lax.Precision.HIGHEST)
    lhs = jnp.pad(jnp.concatenate([coupler, top_profile], axis=0), ((0, 14), (0, 8)))
    lhs_hi, lhs_lo = split(lhs)
    lhs = jnp.concatenate([lhs_hi, lhs_lo], axis=0)
    small = pltpu.VMEM((EXT * 8, W), F32)

    coef = pltpu.VMEM((EXT * 16, W), F32)
    points = pltpu.VMEM((34 * 80, W), F32)
    rows = pltpu.VMEM((80, W), F32)
    own, flux, top = call(
        assemble,
        [
            shape(32, 32, W, dtype=BF16),
            shape(32, 16, W, dtype=BF16),
            shape(2, 16, W, dtype=BF16),
        ],
        2, 1, 6,
        [
            points, dma, buf,
            pltpu.VMEM((32, 80, W), BF16), pltpu.VMEM((32, 80, W), BF16), rows, rows,
            small, small, small, small, coef, coef,
        ],
    )(
        comp, lev_speed, turned, rate8, above, below, halo_l, halo_r, lhs,
    )
    arrived = shifted(flux, "comp", 1)
    send, = call(
        tile_products,
        [shape(band * TILES_PER_PEER, 16, W, dtype=BF16)],
        4, 0, 4,
        [
            pltpu.SMEM((band,), jnp.int32),
            pltpu.VMEM((band, 8, W), F32),
            pltpu.VMEM((512, W), F32),
        ],
    )(
        comp, flux_src_blk, flux_dest.reshape(1, 64), flux_dst_blk,
        own, arrived, conservative_flux_weights[0], top,
    )
    send, top = lax.optimization_barrier((send, top))
    received = lax.all_to_all(
        send.reshape(band, TILES_PER_PEER, 16, W), "gx", 0, 0, tiled=True
    ).reshape(band * TILES_PER_PEER, 16, W)
    grid = pltpu.VMEM((EXT * 160, W), F32)
    advected, dss = call(
        advect_all,
        [shape(16 * 160, W), shape(72 * 32, W)],
        2, 0, 9,
        [
            points, buf, rows, rows, grid, grid, grid, grid, coef, coef,
            pltpu.VMEM((160, W), F32),
        ],
    )(
        comp, lev_speed, state, tracer, atm_mass, rate8, above, below, halo_l, halo_r, top,
    )
    levels = profile.reshape(160, 16)
    received, advected, levels = lax.optimization_barrier((received, advected, levels))
    tops = received.reshape(band, TILES_PER_PEER, 16, W)[:, :2].reshape(2 * band, 16, W)
    other = shifted(tops, "comp", -1)
    mine, = call(surface_select, [shape(128, W)], 3, 0, 1, [])(
        comp, back_owner, back_src_blk, received
    )
    ocean, surface = call(finish, [shape(2560, W), shape(64, W)], 4, 1, 5, [
        pltpu.VMEM(return_remap_weights.shape[1:], BF16), dma((2,)),
        pltpu.VMEM((512, W), F32), pltpu.VMEM((512, W), F32), pltpu.VMEM((256, W), F32),
    ])(
        comp, back_owner, back_src_blk, back_dst_blk,
        in_hbm(return_remap_weights[0]), advected, received, levels, mine, other,
    )
    return (
        dss.reshape(1, 72, 32, W),
        surface.reshape(1, 2, 32, W),
        ocean.reshape(1, 2, 80, 16, W),
    )


def solution(mesh):
    placed = (
        P("comp", None, "gy", "gx"),
        P("gy", "gx"),
        P(),
        P("gy", "gx", None),
        P("gy", "gx"),
        P("gy", "gx"),
        P("gy", "gx", None, None),
        P("comp", None, None, "gy", "gx"),
        P(None, "gy", "gx"),
        P(None, "gy", "gx"),
        P(),
        P(),
        P("gy", "gx"),
        P("gy", "gx"),
        P("gy", "gx"),
        P("gy", "gx", None, None),
    )
    return jax.shard_map(
        shards,
        mesh=mesh,
        in_specs=placed,
        out_specs=(
            P("comp", None, "gy", "gx"),
            P("comp", None, "gy", "gx"),
            P("comp", None, None, "gy", "gx"),
        ),
        check_vma=False,
    )
```
